128 devices in a mesh: row: 8 (over x, core), col: 16 (over y, z).
Axes of the slice: x: 4, y: 4, z: 4, core: 2. Of those that a mesh axis runs over, the one named last changes fastest.
Arguments:
- density: bfloat16 [4096, 4096], P('row', 'col'), may hold values from -2 to 2
- core_ham: float32 [4096, 4096], P('row', 'col'), may hold values from -6 to 6
- block_mask: int32 [64, 64], P('row', 'col'), may hold values 0 or 1
- send_blocks: int32 [128, 128, 8], P(('row', 'col')), may hold values from -1 to 31, as said below
- task_atoms: int32 [2, 128, 128, 8], P(None, ('row', 'col')), may hold values from 0 to 15
- basis: bfloat16 [128, 1024, 2048], P(('row', 'col')), may hold values from -0.375 to 0.375
- v_loc: float32 [128, 2048], P(('row', 'col')), may hold values from -6 to 6
Outputs:
- ks_matrix: float32 [4096, 4096], P('row', 'col')
- sign_step: float32 [4096, 4096], P('row', 'col')
The draws below stay inside these ranges and needn't reach their ends.
Inputs may be any that keep to these rules, and one draw needn't show every extreme that they name: In each list send_blocks[o, e] the live entries come first and the rest are -1; every list has one live entry or more, and in every draw some sub-slab receives all 8 slots live from every owner.
All inputs are finite; a program needn't handle non-finite values. No bound on the sum of `block_mask` on one device may be relied on, other than what follows from the above.
Results may differ from the reference program's by a relative error of at most 0.0048.
Values may be sent and summed in bfloat16 or wider, within the bound.
No kernel may reach another device: no remote copies, remote signals or barrier semaphores. Data moves between devices by JAX's collectives and lax.ppermute only.
A program may use at most 64 MiB of HBM per device.

```python
import math
import jax
import jax.numpy as jnp
from jax import lax

BLK = 64
BC = 4
CELLS = 2048
ATOMS = 16
CAP = 8
NBLK = 64
BR = 8
NMAT = 4096
N_ROW = 8
N_COL = 16
DEVICES = 128


def draw_send_blocks(key, part):
    key_count = jax.random.fold_in(key, 11)
    key_full = jax.random.fold_in(key, 12)
    key_block = jax.random.fold_in(key, 13)
    counts = jax.random.randint(key_count, (DEVICES, DEVICES), 1, CAP + 1)
    full_dest = jax.random.randint(key_full, (), 0, DEVICES)
    counts = jnp.where(jnp.arange(DEVICES)[None, :] == full_dest, CAP, counts)
    numbers = jax.random.randint(key_block, (DEVICES, DEVICES, CAP), 0, BR * BC)
    slots = jnp.arange(CAP)[None, None, :]
    return jnp.where(slots < counts[:, :, None], numbers, -1).astype(jnp.int32)


def touch_ends(result, rng, least, top_value):
    longest = result.shape.index(max(result.shape))
    spots = []
    for shift in (0, 1):
        where = [jax.random.randint(jax.random.fold_in(rng, axis), (), 0, length) for axis, length in enumerate(result.shape)]
        where[longest] = (where[longest] + shift) % result.shape[longest]
        spots.append(tuple(where))
    return result.at[spots[0]].set(least).at[spots[1]].set(top_value)


def shard_levels(stream_key, extent, cuts, least, largest):
    factor_of = 1.0
    for dim, blocks in cuts:
        heights = jax.random.uniform(jax.random.fold_in(jax.random.fold_in(stream_key, 6), dim), (blocks,), jnp.float32, least / len(cuts), largest / len(cuts))
        factor_of = factor_of * jnp.repeat(jnp.exp(heights), extent[dim] // blocks).reshape((-1,) + (1,) * (len(extent) - 1 - dim))
    return factor_of


def scatter_about(rng, extent, deviation, bound, cuts=(), kind=jnp.bfloat16):
    gain = shard_levels(rng, extent, cuts, -0.22, 0.18) if cuts else 1.0
    values = jax.random.normal(rng, extent, jnp.float32) * deviation * gain
    return jnp.minimum(jnp.maximum(values, -bound), bound).astype(kind)


def setup_inputs(seed: int = 0) -> dict:
    key_list = jax.random.split(jax.random.key(seed), 8)
    return {
        "density": scatter_about(key_list[0], (NMAT, NMAT), 0.125, 2.0, ((0, 8), (1, 16))),
        "core_ham": scatter_about(key_list[1], (NMAT, NMAT), 1.0, 6.0, ((0, 8), (1, 16)), jnp.float32),
        "block_mask": touch_ends((jax.random.randint(key_list[2], (NBLK, NBLK), 0, 3) < 1).astype(jnp.int32), jax.random.fold_in(key_list[2], 1), 0, 1),
        "send_blocks": draw_send_blocks(jax.random.fold_in(key_list[7], 71), 0),
        "task_atoms": touch_ends(jax.random.randint(key_list[4], (2, DEVICES, DEVICES, CAP), 0, ATOMS), jax.random.fold_in(key_list[4], 1), 0, ATOMS - 1).astype(jnp.int32),
        "basis": scatter_about(key_list[5], (DEVICES, ATOMS * BLK, CELLS), 256 ** -0.5, 0.375, ((0, 128),)),
        "v_loc": scatter_about(key_list[6], (DEVICES, CELLS), 1.0, 6.0, ((0, 128),), jnp.float32),
    }


def reference(density, core_ham, block_mask, send_blocks, task_atoms, basis, v_loc):
    local_count = BR * BC
    dens_blocks = density.reshape(N_ROW, BR, BLK, N_COL, BC, BLK).transpose(0, 3, 1, 4, 2, 5).reshape(DEVICES, local_count, BLK * BLK)
    owners = jnp.arange(DEVICES, dtype=jnp.int32)[:, None]
    pair_ids = jnp.arange(ATOMS * ATOMS, dtype=jnp.int32)

    def slab_step(ham_sum, slab):
        slots = lax.dynamic_index_in_dim(send_blocks, slab, 1, keepdims=False)
        live = slots >= 0
        safe = jnp.maximum(slots, 0).astype(jnp.int32)
        sent = dens_blocks[owners, safe] * live[:, :, None].astype(jnp.bfloat16)
        atoms = lax.dynamic_index_in_dim(task_atoms, slab, 1, keepdims=False)
        pair = (atoms[0] * ATOMS + atoms[1]).reshape(-1)
        onehot = (pair[:, None] == pair_ids[None, :]).astype(jnp.bfloat16)
        pair_sum = jnp.dot(onehot.T, sent.reshape(-1, BLK * BLK), preferred_element_type=jnp.float32)
        pair_mat = pair_sum.reshape(ATOMS, ATOMS, BLK, BLK).transpose(0, 2, 1, 3).reshape(ATOMS * BLK, ATOMS * BLK).astype(jnp.bfloat16)
        basis_vals = lax.dynamic_index_in_dim(basis, slab, 0, keepdims=False)
        mixed = jnp.dot(pair_mat, basis_vals, preferred_element_type=jnp.float32)
        rho = lax.optimization_barrier(jnp.sum(basis_vals.astype(jnp.float32) * mixed, axis=0))
        pot = lax.dynamic_index_in_dim(v_loc, slab, 0, keepdims=False) + 0.5 * rho / jnp.sqrt(1.0 + rho * rho)
        weighted = (basis_vals.astype(jnp.float32) * pot[None, :]).astype(jnp.bfloat16)
        k_all = jnp.dot(weighted, basis_vals.T, preferred_element_type=jnp.float32)
        k_pairs = k_all.reshape(ATOMS, BLK, ATOMS, BLK).transpose(0, 2, 1, 3).reshape(ATOMS * ATOMS, BLK * BLK)
        k_slot = k_pairs[pair].astype(jnp.bfloat16).reshape(DEVICES, CAP, BLK * BLK)
        added = jnp.where(live[:, :, None], k_slot.astype(jnp.float32), jnp.zeros((), jnp.float32))
        ham_sum = ham_sum.at[owners, safe].add(added)
        return (ham_sum, None)
    start = jnp.zeros((DEVICES, local_count, BLK * BLK), jnp.float32)
    ham_sum, _ = lax.scan(slab_step, start, jnp.arange(DEVICES, dtype=jnp.int32))
    ham_full = ham_sum.reshape(N_ROW, N_COL, BR, BC, BLK, BLK).transpose(0, 2, 4, 1, 3, 5).reshape(NMAT, NMAT)
    ks_matrix = core_ham + ham_full
    mask = jnp.broadcast_to(block_mask.astype(jnp.float32)[:, None, :, None], (NBLK, BLK, NBLK, BLK)).reshape(NMAT, NMAT)
    scale = 1.0 / math.sqrt(16.0 * NBLK)
    x0 = (mask * ks_matrix * scale).astype(jnp.bfloat16)
    x2 = (mask * jnp.dot(x0, x0, preferred_element_type=jnp.float32)).astype(jnp.bfloat16)
    x3 = mask * jnp.dot(x0, x2, preferred_element_type=jnp.float32)
    sign_step = (1.5 * x0.astype(jnp.float32) - 0.5 * x3) / scale
    return (ks_matrix, sign_step)
```

```python
import math

import jax
import jax.numpy as jnp
from jax import lax
from jax.experimental import pallas as pl
from jax.experimental.pallas import tpu as pltpu
from jax.sharding import PartitionSpec as P

ATOMS = 16
block_edge = 64
NX, NC, NY, NZ = 4, 2, 4, 4
F32 = jnp.float32
BF16 = jnp.bfloat16


def move_x(v, d):
    pairs = [(x * NC + c, ((x + d) % NX) * NC + c) for x in range(NX) for c in range(NC)]
    return lax.ppermute(v, "row", pairs)


def swap_core(v):
    pairs = [(x * NC + c, x * NC + 1 - c) for x in range(NX) for c in range(NC)]
    return lax.ppermute(v, "row", pairs)


def move_y(v, d):
    pairs = [(y * NZ + z, ((y + d) % NY) * NZ + z) for y in range(NY) for z in range(NZ)]
    return lax.ppermute(v, "col", pairs)


def move_z(v, d):
    pairs = [(y * NZ + z, y * NZ + (z + d) % NZ) for y in range(NY) for z in range(NZ)]
    return lax.ppermute(v, "col", pairs)


def all_to_all(v):
    return lax.all_to_all(v, ("row", "col"), split_axis=0, concat_axis=0, tiled=True)


def grid_kernel(pair_ref, basis_ref, vloc_ref, out_ref, acc_ref):
    step = pl.program_id(0)
    vals = basis_ref[...]
    mixed = jnp.dot(pair_ref[...], vals, preferred_element_type=F32)
    wide = vals.astype(F32)
    rho = jnp.sum(wide * mixed, axis=0, keepdims=True)
    pot = vloc_ref[...] + 0.5 * rho / jnp.sqrt(1.0 + rho * rho)
    weighted = (wide * pot).astype(BF16)
    part = lax.dot_general(weighted, vals, (((1,), (1,)), ((), ())), preferred_element_type=F32)

    @pl.when(step == 0)
    def _():
        acc_ref[...] = part

    @pl.when(step > 0)
    def _():
        acc_ref[...] += part

    @pl.when(step == pl.num_programs(0) - 1)
    def _():
        out_ref[...] = acc_ref[...].astype(BF16)


def grid_build(pair_mat, basis_vals, v_loc):
    order, cells = basis_vals.shape
    tile = 512
    return pl.pallas_call(
        grid_kernel,
        grid=(cells // tile,),
        in_specs=[
            pl.BlockSpec((order, order), lambda g: (0, 0)),
            pl.BlockSpec((order, tile), lambda g: (0, g)),
            pl.BlockSpec((1, tile), lambda g: (0, g)),
        ],
        out_specs=pl.BlockSpec((order, order), lambda g: (0, 0)),
        out_shape=jax.ShapeDtypeStruct((order, order), BF16),
        scratch_shapes=[pltpu.VMEM((order, order), F32)],
        compiler_params=pltpu.CompilerParams(vmem_limit_bytes=48 << 20),
        cost_estimate=pl.CostEstimate(
            flops=4 * order * order * cells,
            bytes_accessed=2 * order * cells + 4 * order * order,
            transcendentals=cells,
        ),
    )(pair_mat, basis_vals, v_loc)


def panel_sum(where_ref, left_a, left_b, right_refs):
    half = left_a[0].shape[1]
    out = []
    for left, first_y in ((left_a, True), (left_b, False)):
        total = None
        for outer in range(4):
            for inner in range(4):
                dy, dz = (outer, inner) if first_y else (inner, outer)
                piece = left[outer][inner]
                spot = where_ref[dy * 4 + dz]
                depth = piece.shape[1]
                rows = right_refs[pl.ds(pl.multiple_of(spot * depth, depth), depth), :]
                term = jnp.dot(piece, rows, preferred_element_type=F32)
                total = term if total is None else total + term
        out.append(total)
    return out


def square_kernel(where_ref, *refs):
    left_a, left_b = refs[0:4], refs[4:8]
    right_ref, mask_ref, out_ref = refs[8:11]
    top, low = panel_sum(where_ref, left_a, left_b, right_ref)
    half = top.shape[0]
    out_ref[:half] = (mask_ref[:half] * top).astype(BF16)
    out_ref[half:] = (mask_ref[half:] * low).astype(BF16)


def cube_kernel(scale, where_ref, *refs):
    left_a, left_b = refs[0:4], refs[4:8]
    right_ref, mask_ref, x0_ref, out_ref = refs[8:12]
    top, low = panel_sum(where_ref, left_a, left_b, right_ref)
    half = top.shape[0]
    for part, rows in ((top, slice(0, half)), (low, slice(half, 2 * half))):
        x3 = mask_ref[rows] * part
        out_ref[rows] = (1.5 * x0_ref[rows].astype(F32) - 0.5 * x3) / scale


def panel_call(kernel, where, operands, shape, dtype):
    vmem = pl.BlockSpec(memory_space=pltpu.VMEM)
    rows, cols = shape
    return pl.pallas_call(
        kernel,
        in_specs=[pl.BlockSpec(memory_space=pltpu.SMEM)] + [vmem] * len(operands),
        out_specs=vmem,
        out_shape=jax.ShapeDtypeStruct(shape, dtype),
        compiler_params=pltpu.CompilerParams(vmem_limit_bytes=40 << 20),
        cost_estimate=pl.CostEstimate(
            flops=2 * rows * cols * 4096, bytes_accessed=7 << 20, transcendentals=0
        ),
    )(where, *operands)


def gather_left(x0):
    rows = x0.shape[0]
    half = rows // 2
    a, b = x0[:half], x0[half:]
    za = [a] + [None] * 3
    yb = [b] + [None] * 3
    for d in (1, 3, 2):
        za[d] = move_z(a, d)
        yb[d] = move_y(b, d)
    a4, b4 = jnp.stack(za), jnp.stack(yb)
    out_a, out_b = [a4] + [None] * 3, [b4] + [None] * 3
    for d in (1, 3, 2):
        out_a[d] = move_y(a4, d)
        out_b[d] = move_z(b4, d)
    return out_a, out_b


def gather_right(tile):
    got = [move_x(tile, d) for d in (1, 3, 2)]
    other = swap_core(tile)
    same = jnp.concatenate([tile, got[0], got[2], got[1]])
    rest = swap_core(same[tile.shape[0]:])
    return jnp.concatenate([same, other, rest])


def body(density, core_ham, block_mask, send_blocks, task_atoms, basis, v_loc):
    block_rows = density.shape[0] // block_edge
    block_cols = density.shape[1] // block_edge
    local_count = block_rows * block_cols
    area = block_edge * block_edge
    slot_count = send_blocks.shape[2]
    device_count = send_blocks.shape[1]
    row, col = lax.axis_index("row"), lax.axis_index("col")
    x_at, c_at, y_at, z_at = row // NC, row % NC, col // NZ, col % NZ

    dens_blocks = (
        density.reshape(block_rows, block_edge, block_cols, block_edge)
        .transpose(0, 2, 1, 3)
        .reshape(local_count, area)
    )
    slots = send_blocks[0].reshape(-1)
    local_ids = jnp.arange(local_count, dtype=jnp.int32)
    pick = (slots[:, None] == local_ids[None, :]).astype(BF16)
    outgoing = jnp.dot(pick, dens_blocks, preferred_element_type=F32).astype(BF16)
    received = all_to_all(outgoing.reshape(device_count, slot_count, area)).reshape(-1, area)
    atoms = task_atoms[:, 0]
    pair = (atoms[0] * ATOMS + atoms[1]).reshape(-1)
    pair_ids = jnp.arange(ATOMS * ATOMS, dtype=jnp.int32)
    gather_pairs = (pair_ids[:, None] == pair[None, :]).astype(BF16)
    pair_sum = jnp.dot(gather_pairs, received, preferred_element_type=F32).astype(BF16)
    pair_mat = (
        pair_sum.reshape(ATOMS, ATOMS, block_edge, block_edge)
        .transpose(0, 2, 1, 3)
        .reshape(ATOMS * block_edge, ATOMS * block_edge)
    )
    k_all = grid_build(pair_mat, basis[0], v_loc)
    k_pairs = (
        k_all.reshape(ATOMS, block_edge, ATOMS, block_edge)
        .transpose(0, 2, 1, 3)
        .reshape(ATOMS * ATOMS, area)
    )
    spread_pairs = (pair[:, None] == pair_ids[None, :]).astype(BF16)
    k_slot = jnp.dot(spread_pairs, k_pairs, preferred_element_type=F32).astype(BF16)
    returned = all_to_all(k_slot.reshape(device_count, slot_count, area)).reshape(-1, area)
    select = (local_ids[:, None] == slots[None, :]).astype(BF16)
    ham_blocks = jnp.dot(select, returned, preferred_element_type=F32)
    ham_tile = (
        ham_blocks.reshape(block_rows, block_cols, block_edge, block_edge)
        .transpose(0, 2, 1, 3)
        .reshape(density.shape)
    )
    ks_matrix = core_ham + ham_tile
    mask = jnp.broadcast_to(
        block_mask.astype(F32)[:, None, :, None],
        (block_rows, block_edge, block_cols, block_edge),
    ).reshape(density.shape)
    scale = 1.0 / math.sqrt(16.0 * block_rows * NX * NC)
    x0 = (mask * ks_matrix * scale).astype(BF16)

    left_a, left_b = gather_left(x0)
    shift = jnp.arange(NY * NZ, dtype=jnp.int32)
    src = ((y_at - shift // NZ) % NY) * NZ + (z_at - shift % NZ) % NZ
    src_x, src_c = src // (2 * NC), (src // 2) % NC
    where = (((src_c ^ c_at) * NX + (x_at - src_x) % NX) * 2 + src % 2).astype(jnp.int32)
    x2 = panel_call(
        square_kernel, where, [*left_a, *left_b, gather_right(x0), mask], x0.shape, BF16
    )
    sign_step = panel_call(
        lambda *refs: cube_kernel(scale, *refs),
        where,
        [*left_a, *left_b, gather_right(x2), mask, x0],
        x0.shape,
        F32,
    )
    return (ks_matrix, sign_step)


def solution(mesh):
    placed = (
        P("row", "col"),
        P("row", "col"),
        P("row", "col"),
        P(("row", "col"), None, None),
        P(None, ("row", "col"), None, None),
        P(("row", "col"), None, None),
        P(("row", "col"), None),
    )
    return jax.shard_map(
        body,
        mesh=mesh,
        in_specs=placed,
        out_specs=(P("row", "col"), P("row", "col")),
        check_vma=False,
    )
```

```python
import math

import jax
import jax.numpy as jnp
from jax import lax
from jax.experimental import pallas as pl
from jax.experimental.pallas import tpu as pltpu
from jax.sharding import PartitionSpec as P

ATOMS = 16
block_edge = 64
NX, NC, NY, NZ = 4, 2, 4, 4
F32 = jnp.float32
BF16 = jnp.bfloat16


def move_x(v, d):
    pairs = [(x * NC + c, ((x + d) % NX) * NC + c) for x in range(NX) for c in range(NC)]
    return lax.ppermute(v, "row", pairs)


def swap_core(v):
    pairs = [(x * NC + c, x * NC + 1 - c) for x in range(NX) for c in range(NC)]
    return lax.ppermute(v, "row", pairs)


def move_y(v, d):
    pairs = [(y * NZ + z, ((y + d) % NY) * NZ + z) for y in range(NY) for z in range(NZ)]
    return lax.ppermute(v, "col", pairs)


def move_z(v, d):
    pairs = [(y * NZ + z, y * NZ + (z + d) % NZ) for y in range(NY) for z in range(NZ)]
    return lax.ppermute(v, "col", pairs)


def all_to_all(v):
    return lax.all_to_all(v, ("row", "col"), split_axis=0, concat_axis=0, tiled=True)


def low_half(shape):
    return lax.broadcasted_iota(jnp.int32, shape, 1) < block_edge


def trade_halves(first, second):
    low = low_half(first.shape)
    turned_first = pltpu.roll(first, block_edge, 1)
    turned_second = pltpu.roll(second, block_edge, 1)
    return jnp.where(low, first, turned_second), jnp.where(low, turned_first, second)


def blocks_to_matrix(blocks, matrix_ref, first_row, heights):
    groups, _, lanes = matrix_ref.shape
    half = heights * groups
    for tile in range(blocks.shape[1] // lanes):
        cut = slice(tile * lanes, (tile + 1) * lanes)
        rows = trade_halves(blocks[:half, cut], blocks[half:, cut])
        for odd in range(2):
            for group in range(groups):
                matrix_ref[group, pl.ds(first_row + 2 * tile + odd, heights, stride=block_edge), :] = (
                    rows[odd][group * heights : (group + 1) * heights]
                )


def matrix_to_blocks(matrix_ref, first_row, tiles, heights):
    groups = matrix_ref.shape[0]
    out = []
    for tile in range(tiles):
        rows = [
            jnp.concatenate(
                [
                    matrix_ref[group, pl.ds(first_row + 2 * tile + odd, heights, stride=block_edge), :]
                    for group in range(groups)
                ],
                axis=0,
            )
            for odd in range(2)
        ]
        out.append(jnp.concatenate(trade_halves(*rows), axis=0))
    return jnp.concatenate(out, axis=1)


def fold(matrix_ref, split_ref):
    groups, _, lanes = split_ref.shape
    for group in range(groups):
        split_ref[group] = matrix_ref[:, group * lanes : (group + 1) * lanes].astype(F32)


def split_scratch(shape):
    lanes = 2 * block_edge
    return pltpu.VMEM((shape[1] // lanes, shape[0], lanes), F32)


CHUNK = 512
CHUNK_ROWS = CHUNK // block_edge
CHUNK_TILES = CHUNK // (2 * block_edge)


def send_kernel(pick_ref, density_ref, out_ref, wide_ref):
    step = pl.program_id(0)

    @pl.when(step == 0)
    def _():
        fold(density_ref, wide_ref)

    heights = density_ref.shape[0] // block_edge
    blocks = matrix_to_blocks(wide_ref, step * CHUNK_ROWS, CHUNK_TILES, heights)
    out_ref[...] = jnp.dot(
        pick_ref[...], blocks.astype(BF16), preferred_element_type=F32
    ).astype(BF16)


def send_tasks(pick, density):
    tasks = pick.shape[0]
    area = block_edge * block_edge
    return pl.pallas_call(
        send_kernel,
        grid=(area // CHUNK,),
        in_specs=[
            pl.BlockSpec(pick.shape, lambda g: (0, 0)),
            pl.BlockSpec(density.shape, lambda g: (0, 0)),
        ],
        out_specs=pl.BlockSpec((tasks, CHUNK), lambda g: (0, g)),
        out_shape=jax.ShapeDtypeStruct((tasks, area), BF16),
        scratch_shapes=[split_scratch(density.shape)],
        compiler_params=pltpu.CompilerParams(vmem_limit_bytes=32 << 20),
        cost_estimate=pl.CostEstimate(
            flops=2 * tasks * 256 * area, bytes_accessed=2 * tasks * area, transcendentals=0
        ),
    )(pick, density)


def grid_kernel(
    steps, gather_ref, got_ref, basis_ref, vloc_ref, spread_ref, out_ref, wide_ref, pair_ref, acc_ref
):
    first, middle, _ = steps
    step = pl.program_id(0)

    @pl.when(step < first)
    def _():
        sums = jnp.dot(gather_ref[...], got_ref[...], preferred_element_type=F32)
        blocks_to_matrix(sums, wide_ref, step * CHUNK_ROWS, ATOMS)

    @pl.when(step == first)
    def _():
        for group in range(wide_ref.shape[0]):
            lanes = slice(group * 2 * block_edge, (group + 1) * 2 * block_edge)
            pair_ref[:, lanes] = wide_ref[group].astype(BF16)
        acc_ref[...] = jnp.zeros_like(acc_ref)

    @pl.when((step >= first) & (step < first + middle))
    def _():
        vals = basis_ref[...]
        mixed = jnp.dot(pair_ref[...], vals, preferred_element_type=F32)
        wide = vals.astype(F32)
        rho = jnp.sum(wide * mixed, axis=0, keepdims=True)
        pot = vloc_ref[...] + 0.5 * rho / jnp.sqrt(1.0 + rho * rho)
        weighted = (wide * pot).astype(BF16)
        acc_ref[...] += lax.dot_general(
            weighted, vals, (((1,), (1,)), ((), ())), preferred_element_type=F32
        )

    @pl.when(step == first + middle)
    def _():
        fold(acc_ref, wide_ref)

    @pl.when(step >= first + middle)
    def _():
        row = (step - first - middle) * CHUNK_ROWS
        blocks = matrix_to_blocks(wide_ref, row, CHUNK_TILES, ATOMS)
        out_ref[...] = jnp.dot(
            spread_ref[...], blocks.astype(BF16), preferred_element_type=F32
        ).astype(BF16)


def grid_build(gather_pairs, received, basis_vals, v_loc, spread_pairs):
    order, cells = basis_vals.shape
    tasks, area = received.shape
    tile = 512
    steps = (area // CHUNK, cells // tile, area // CHUNK)
    first, middle, last = steps
    return pl.pallas_call(
        lambda *refs: grid_kernel(steps, *refs),
        grid=(sum(steps),),
        in_specs=[
            pl.BlockSpec(gather_pairs.shape, lambda g: (0, 0)),
            pl.BlockSpec((tasks, CHUNK), lambda g: (0, jnp.minimum(g, first - 1))),
            pl.BlockSpec((order, tile), lambda g: (0, jnp.clip(g - first, 0, middle - 1))),
            pl.BlockSpec((1, tile), lambda g: (0, jnp.clip(g - first, 0, middle - 1))),
            pl.BlockSpec(spread_pairs.shape, lambda g: (0, 0)),
        ],
        out_specs=pl.BlockSpec(
            (tasks, CHUNK), lambda g: (0, jnp.clip(g - first - middle, 0, last - 1))
        ),
        out_shape=jax.ShapeDtypeStruct((tasks, area), BF16),
        scratch_shapes=[
            split_scratch((order, order)),
            pltpu.VMEM((order, order), BF16),
            pltpu.VMEM((order, order), F32),
        ],
        compiler_params=pltpu.CompilerParams(vmem_limit_bytes=48 << 20),
        cost_estimate=pl.CostEstimate(
            flops=4 * order * order * cells,
            bytes_accessed=2 * order * cells + 4 * tasks * area,
            transcendentals=cells,
        ),
    )(gather_pairs, received, basis_vals, v_loc, spread_pairs)


def ham_kernel(scale, select_ref, got_ref, core_ref, mask_ref, ks_ref, x0_ref, wide_ref):
    step = pl.program_id(0)
    heights = core_ref.shape[0] // block_edge
    sums = jnp.dot(select_ref[...], got_ref[...], preferred_element_type=F32)
    blocks_to_matrix(sums, wide_ref, step * CHUNK_ROWS, heights)

    @pl.when(step == pl.num_programs(0) - 1)
    def _():
        for group in range(wide_ref.shape[0]):
            lanes = slice(group * 2 * block_edge, (group + 1) * 2 * block_edge)
            total = core_ref[:, lanes] + wide_ref[group]
            ks_ref[:, lanes] = total
            x0_ref[:, lanes] = (mask_ref[:, lanes] * total * scale).astype(BF16)


def ham_build(scale, select, returned, core_ham, mask):
    tasks, area = returned.shape
    whole = lambda v: pl.BlockSpec(v.shape, lambda g: (0, 0))
    return pl.pallas_call(
        lambda *refs: ham_kernel(scale, *refs),
        grid=(area // CHUNK,),
        in_specs=[
            whole(select),
            pl.BlockSpec((tasks, CHUNK), lambda g: (0, g)),
            whole(core_ham),
            whole(mask),
        ],
        out_specs=[whole(core_ham), whole(core_ham)],
        out_shape=[
            jax.ShapeDtypeStruct(core_ham.shape, F32),
            jax.ShapeDtypeStruct(core_ham.shape, BF16),
        ],
        scratch_shapes=[split_scratch(core_ham.shape)],
        compiler_params=pltpu.CompilerParams(vmem_limit_bytes=32 << 20),
        cost_estimate=pl.CostEstimate(
            flops=2 * tasks * 256 * area, bytes_accessed=2 * tasks * area, transcendentals=0
        ),
    )(select, returned, core_ham, mask)


def panel_sum(where_ref, left_a, left_b, right_refs):
    half = left_a[0].shape[1]
    out = []
    for left, first_y in ((left_a, True), (left_b, False)):
        total = None
        for outer in range(4):
            for inner in range(4):
                dy, dz = (outer, inner) if first_y else (inner, outer)
                piece = left[outer][inner]
                spot = where_ref[dy * 4 + dz]
                depth = piece.shape[1]
                rows = right_refs[pl.ds(pl.multiple_of(spot * depth, depth), depth), :]
                term = jnp.dot(piece, rows, preferred_element_type=F32)
                total = term if total is None else total + term
        out.append(total)
    return out


def square_kernel(where_ref, *refs):
    left_a, left_b = refs[0:4], refs[4:8]
    right_ref, mask_ref, out_ref = refs[8:11]
    top, low = panel_sum(where_ref, left_a, left_b, right_ref)
    half = top.shape[0]
    out_ref[:half] = (mask_ref[:half] * top).astype(BF16)
    out_ref[half:] = (mask_ref[half:] * low).astype(BF16)


def cube_kernel(scale, where_ref, *refs):
    left_a, left_b = refs[0:4], refs[4:8]
    right_ref, mask_ref, x0_ref, out_ref = refs[8:12]
    top, low = panel_sum(where_ref, left_a, left_b, right_ref)
    half = top.shape[0]
    for part, rows in ((top, slice(0, half)), (low, slice(half, 2 * half))):
        x3 = mask_ref[rows] * part
        out_ref[rows] = (1.5 * x0_ref[rows].astype(F32) - 0.5 * x3) / scale


def panel_call(kernel, where, operands, shape, dtype):
    vmem = pl.BlockSpec(memory_space=pltpu.VMEM)
    rows, cols = shape
    return pl.pallas_call(
        kernel,
        in_specs=[pl.BlockSpec(memory_space=pltpu.SMEM)] + [vmem] * len(operands),
        out_specs=vmem,
        out_shape=jax.ShapeDtypeStruct(shape, dtype),
        compiler_params=pltpu.CompilerParams(vmem_limit_bytes=40 << 20),
        cost_estimate=pl.CostEstimate(
            flops=2 * rows * cols * 4096, bytes_accessed=7 << 20, transcendentals=0
        ),
    )(where, *operands)


def gather_left(x0):
    rows = x0.shape[0]
    half = rows // 2
    a, b = x0[:half], x0[half:]
    za = [a] + [None] * 3
    yb = [b] + [None] * 3
    for d in (1, 3, 2):
        za[d] = move_z(a, d)
        yb[d] = move_y(b, d)
    a4, b4 = jnp.stack(za), jnp.stack(yb)
    out_a, out_b = [a4] + [None] * 3, [b4] + [None] * 3
    for d in (1, 3, 2):
        out_a[d] = move_y(a4, d)
        out_b[d] = move_z(b4, d)
    return out_a, out_b


def gather_right(tile):
    got = [move_x(tile, d) for d in (1, 3, 2)]
    other = swap_core(tile)
    same = jnp.concatenate([tile, got[0], got[2], got[1]])
    rest = swap_core(same[tile.shape[0]:])
    return jnp.concatenate([same, other, rest])


def body(density, core_ham, block_mask, send_blocks, task_atoms, basis, v_loc):
    block_rows = density.shape[0] // block_edge
    block_cols = density.shape[1] // block_edge
    local_count = block_rows * block_cols
    area = block_edge * block_edge
    slot_count = send_blocks.shape[2]
    device_count = send_blocks.shape[1]
    row, col = lax.axis_index("row"), lax.axis_index("col")
    x_at, c_at, y_at, z_at = row // NC, row % NC, col // NZ, col % NZ

    slots = send_blocks[0].reshape(-1)
    spot = jnp.arange(local_count, dtype=jnp.int32)
    in_half = local_count // 2
    local_ids = (spot % block_rows) * block_cols
    local_ids += 2 * ((spot % in_half) // block_rows) + spot // in_half
    pick = (slots[:, None] == local_ids[None, :]).astype(BF16)
    outgoing = send_tasks(pick, density)
    received = all_to_all(outgoing.reshape(device_count, slot_count, area)).reshape(-1, area)
    atoms = task_atoms[:, 0]
    pair = (
        (atoms[1] % 2) * (ATOMS * ATOMS // 2) + (atoms[1] // 2) * ATOMS + atoms[0]
    ).reshape(-1)
    pair_ids = jnp.arange(ATOMS * ATOMS, dtype=jnp.int32)
    gather_pairs = (pair_ids[:, None] == pair[None, :]).astype(BF16)
    spread_pairs = (pair[:, None] == pair_ids[None, :]).astype(BF16)
    k_slot = grid_build(gather_pairs, received, basis[0], v_loc, spread_pairs)
    returned = all_to_all(k_slot.reshape(device_count, slot_count, area)).reshape(-1, area)
    select = (local_ids[:, None] == slots[None, :]).astype(BF16)
    mask = jnp.broadcast_to(
        block_mask.astype(F32)[:, None, :, None],
        (block_rows, block_edge, block_cols, block_edge),
    ).reshape(density.shape)
    scale = 1.0 / math.sqrt(16.0 * block_rows * NX * NC)
    ks_matrix, x0 = ham_build(scale, select, returned, core_ham, mask)

    left_a, left_b = gather_left(x0)
    shift = jnp.arange(NY * NZ, dtype=jnp.int32)
    src = ((y_at - shift // NZ) % NY) * NZ + (z_at - shift % NZ) % NZ
    src_x, src_c = src // (2 * NC), (src // 2) % NC
    where = (((src_c ^ c_at) * NX + (x_at - src_x) % NX) * 2 + src % 2).astype(jnp.int32)
    x2 = panel_call(
        square_kernel, where, [*left_a, *left_b, gather_right(x0), mask], x0.shape, BF16
    )
    sign_step = panel_call(
        lambda *refs: cube_kernel(scale, *refs),
        where,
        [*left_a, *left_b, gather_right(x2), mask, x0],
        x0.shape,
        F32,
    )
    return (ks_matrix, sign_step)


def solution(mesh):
    placed = (
        P("row", "col"),
        P("row", "col"),
        P("row", "col"),
        P(("row", "col"), None, None),
        P(None, ("row", "col"), None, None),
        P(("row", "col"), None, None),
        P(("row", "col"), None),
    )
    return jax.shard_map(
        body,
        mesh=mesh,
        in_specs=placed,
        out_specs=(P("row", "col"), P("row", "col")),
        check_vma=False,
    )
```

```python
import math

import jax
import jax.numpy as jnp
from jax import lax
from jax.experimental import pallas as pl
from jax.experimental.pallas import tpu as pltpu
from jax.sharding import PartitionSpec as P

ATOMS = 16
block_edge = 64
NX, NC, NY, NZ = 4, 2, 4, 4
F32 = jnp.float32
BF16 = jnp.bfloat16


def move_x(v, d):
    pairs = [(x * NC + c, ((x + d) % NX) * NC + c) for x in range(NX) for c in range(NC)]
    return lax.ppermute(v, "row", pairs)


def swap_core(v):
    pairs = [(x * NC + c, x * NC + 1 - c) for x in range(NX) for c in range(NC)]
    return lax.ppermute(v, "row", pairs)


def place(x, c, y, z):
    return ((x % NX) * NC + c) * (NY * NZ) + (y % NY) * NZ + z % NZ


def move_two(v, d, axes):
    pairs = []
    for x in range(NX):
        for c in range(NC):
            for y in range(NY):
                for z in range(NZ):
                    step = {"x": 0, "y": 0, "z": 0}
                    step[axes[c]] = d
                    there = place(x + step["x"], c, y + step["y"], z + step["z"])
                    pairs.append((place(x, c, y, z), there))
    return lax.ppermute(v, ("row", "col"), pairs)


def all_to_all(v):
    return lax.all_to_all(v, ("row", "col"), split_axis=0, concat_axis=0, tiled=True)


def low_half(shape):
    return lax.broadcasted_iota(jnp.int32, shape, 1) < block_edge


def trade_halves(first, second):
    low = low_half(first.shape)
    turned_first = pltpu.roll(first, block_edge, 1)
    turned_second = pltpu.roll(second, block_edge, 1)
    return jnp.where(low, first, turned_second), jnp.where(low, turned_first, second)


def blocks_to_matrix(blocks, matrix_ref, first_row, heights):
    groups, _, lanes = matrix_ref.shape
    half = heights * groups
    for tile in range(blocks.shape[1] // lanes):
        cut = slice(tile * lanes, (tile + 1) * lanes)
        rows = trade_halves(blocks[:half, cut], blocks[half:, cut])
        for odd in range(2):
            for group in range(groups):
                matrix_ref[group, pl.ds(first_row + 2 * tile + odd, heights, stride=block_edge), :] = (
                    rows[odd][group * heights : (group + 1) * heights]
                )


def matrix_to_blocks(matrix_ref, first_row, tiles, heights):
    groups = matrix_ref.shape[0]
    out = []
    for tile in range(tiles):
        rows = [
            jnp.concatenate(
                [
                    matrix_ref[group, pl.ds(first_row + 2 * tile + odd, heights, stride=block_edge), :]
                    for group in range(groups)
                ],
                axis=0,
            )
            for odd in range(2)
        ]
        out.append(jnp.concatenate(trade_halves(*rows), axis=0))
    return jnp.concatenate(out, axis=1)


def fold(matrix_ref, split_ref):
    groups, _, lanes = split_ref.shape
    for group in range(groups):
        split_ref[group] = matrix_ref[:, group * lanes : (group + 1) * lanes].astype(F32)


def split_scratch(shape):
    lanes = 2 * block_edge
    return pltpu.VMEM((shape[1] // lanes, shape[0], lanes), F32)


CHUNK = 512
CHUNK_ROWS = CHUNK // block_edge
CHUNK_TILES = CHUNK // (2 * block_edge)


def send_kernel(pick_ref, density_ref, out_ref, wide_ref):
    step = pl.program_id(0)

    @pl.when(step == 0)
    def _():
        fold(density_ref, wide_ref)

    heights = density_ref.shape[0] // block_edge
    blocks = matrix_to_blocks(wide_ref, step * CHUNK_ROWS, CHUNK_TILES, heights)
    out_ref[...] = jnp.dot(
        pick_ref[...], blocks.astype(BF16), preferred_element_type=F32
    ).astype(BF16)


def send_tasks(pick, density):
    tasks = pick.shape[0]
    area = block_edge * block_edge
    return pl.pallas_call(
        send_kernel,
        grid=(area // CHUNK,),
        in_specs=[
            pl.BlockSpec(pick.shape, lambda g: (0, 0)),
            pl.BlockSpec(density.shape, lambda g: (0, 0)),
        ],
        out_specs=pl.BlockSpec((tasks, CHUNK), lambda g: (0, g)),
        out_shape=jax.ShapeDtypeStruct((tasks, area), BF16),
        scratch_shapes=[split_scratch(density.shape)],
        compiler_params=pltpu.CompilerParams(vmem_limit_bytes=32 << 20),
        cost_estimate=pl.CostEstimate(
            flops=2 * tasks * 256 * area, bytes_accessed=2 * tasks * area, transcendentals=0
        ),
    )(pick, density)


def grid_kernel(
    steps, gather_ref, got_ref, basis_ref, vloc_ref, spread_ref, out_ref, wide_ref, pair_ref, acc_ref
):
    first, middle, _ = steps
    step = pl.program_id(0)

    @pl.when(step < first)
    def _():
        sums = jnp.dot(gather_ref[...], got_ref[...], preferred_element_type=F32)
        blocks_to_matrix(sums, wide_ref, step * CHUNK_ROWS, ATOMS)

    @pl.when(step == first)
    def _():
        for group in range(wide_ref.shape[0]):
            lanes = slice(group * 2 * block_edge, (group + 1) * 2 * block_edge)
            pair_ref[:, lanes] = wide_ref[group].astype(BF16)
        acc_ref[...] = jnp.zeros_like(acc_ref)

    @pl.when((step >= first) & (step < first + middle))
    def _():
        vals = basis_ref[...]
        mixed = jnp.dot(pair_ref[...], vals, preferred_element_type=F32)
        wide = vals.astype(F32)
        rho = jnp.sum(wide * mixed, axis=0, keepdims=True)
        pot = vloc_ref[...] + 0.5 * rho / jnp.sqrt(1.0 + rho * rho)
        weighted = (wide * pot).astype(BF16)
        acc_ref[...] += lax.dot_general(
            weighted, vals, (((1,), (1,)), ((), ())), preferred_element_type=F32
        )

    @pl.when(step == first + middle)
    def _():
        fold(acc_ref, wide_ref)

    @pl.when(step >= first + middle)
    def _():
        row = (step - first - middle) * CHUNK_ROWS
        blocks = matrix_to_blocks(wide_ref, row, CHUNK_TILES, ATOMS)
        out_ref[...] = jnp.dot(
            spread_ref[...], blocks.astype(BF16), preferred_element_type=F32
        ).astype(BF16)


def grid_build(gather_pairs, received, basis_vals, v_loc, spread_pairs):
    order, cells = basis_vals.shape
    tasks, area = received.shape
    tile = 512
    steps = (area // CHUNK, cells // tile, area // CHUNK)
    first, middle, last = steps
    return pl.pallas_call(
        lambda *refs: grid_kernel(steps, *refs),
        grid=(sum(steps),),
        in_specs=[
            pl.BlockSpec(gather_pairs.shape, lambda g: (0, 0)),
            pl.BlockSpec((tasks, CHUNK), lambda g: (0, jnp.minimum(g, first - 1))),
            pl.BlockSpec((order, tile), lambda g: (0, jnp.clip(g - first, 0, middle - 1))),
            pl.BlockSpec((1, tile), lambda g: (0, jnp.clip(g - first, 0, middle - 1))),
            pl.BlockSpec(spread_pairs.shape, lambda g: (0, 0)),
        ],
        out_specs=pl.BlockSpec(
            (tasks, CHUNK), lambda g: (0, jnp.clip(g - first - middle, 0, last - 1))
        ),
        out_shape=jax.ShapeDtypeStruct((tasks, area), BF16),
        scratch_shapes=[
            split_scratch((order, order)),
            pltpu.VMEM((order, order), BF16),
            pltpu.VMEM((order, order), F32),
        ],
        compiler_params=pltpu.CompilerParams(vmem_limit_bytes=48 << 20),
        cost_estimate=pl.CostEstimate(
            flops=4 * order * order * cells,
            bytes_accessed=2 * order * cells + 4 * tasks * area,
            transcendentals=cells,
        ),
    )(gather_pairs, received, basis_vals, v_loc, spread_pairs)


def ham_kernel(scale, select_ref, got_ref, core_ref, mask_ref, ks_ref, x0_ref, wide_ref):
    step = pl.program_id(0)
    heights = core_ref.shape[0] // block_edge
    sums = jnp.dot(select_ref[...], got_ref[...], preferred_element_type=F32)
    blocks_to_matrix(sums, wide_ref, step * CHUNK_ROWS, heights)

    @pl.when(step == pl.num_programs(0) - 1)
    def _():
        for group in range(wide_ref.shape[0]):
            lanes = slice(group * 2 * block_edge, (group + 1) * 2 * block_edge)
            total = core_ref[:, lanes] + wide_ref[group]
            ks_ref[:, lanes] = total
            x0_ref[:, lanes] = (mask_ref[:, lanes] * total * scale).astype(BF16)


def ham_build(scale, select, returned, core_ham, mask):
    tasks, area = returned.shape
    whole = lambda v: pl.BlockSpec(v.shape, lambda g: (0, 0))
    return pl.pallas_call(
        lambda *refs: ham_kernel(scale, *refs),
        grid=(area // CHUNK,),
        in_specs=[
            whole(select),
            pl.BlockSpec((tasks, CHUNK), lambda g: (0, g)),
            whole(core_ham),
            whole(mask),
        ],
        out_specs=[whole(core_ham), whole(core_ham)],
        out_shape=[
            jax.ShapeDtypeStruct(core_ham.shape, F32),
            jax.ShapeDtypeStruct(core_ham.shape, BF16),
        ],
        scratch_shapes=[split_scratch(core_ham.shape)],
        compiler_params=pltpu.CompilerParams(vmem_limit_bytes=32 << 20),
        cost_estimate=pl.CostEstimate(
            flops=2 * tasks * 256 * area, bytes_accessed=2 * tasks * area, transcendentals=0
        ),
    )(select, returned, core_ham, mask)


def panel_sum(where_ref, left, right_ref):
    total = None
    for outer in range(4):
        for inner in range(4):
            piece = left[outer][inner]
            depth = piece.shape[1]
            start = pl.multiple_of(where_ref[outer * 4 + inner] * depth, depth)
            term = jnp.dot(piece, right_ref[pl.ds(start, depth), :], preferred_element_type=F32)
            total = term if total is None else total + term
    return total


def square_kernel(where_ref, *refs):
    right_ref, mask_ref, out_ref = refs[4:7]
    out_ref[...] = (mask_ref[...] * panel_sum(where_ref, refs[0:4], right_ref)).astype(BF16)


def cube_kernel(scale, where_ref, *refs):
    right_ref, mask_ref, x0_ref, out_ref = refs[4:8]
    x3 = mask_ref[...] * panel_sum(where_ref, refs[0:4], right_ref)
    out_ref[...] = (1.5 * x0_ref[...].astype(F32) - 0.5 * x3) / scale


def panel_call(kernel, where, operands, shape, dtype):
    vmem = pl.BlockSpec(memory_space=pltpu.VMEM)
    rows, cols = shape
    return pl.pallas_call(
        kernel,
        in_specs=[pl.BlockSpec(memory_space=pltpu.SMEM)] + [vmem] * len(operands),
        out_specs=vmem,
        out_shape=jax.ShapeDtypeStruct(shape, dtype),
        compiler_params=pltpu.CompilerParams(vmem_limit_bytes=40 << 20),
        cost_estimate=pl.CostEstimate(
            flops=2 * rows * cols * 4096, bytes_accessed=7 << 20, transcendentals=0
        ),
    )(where, *operands)


def gather_left(x0):
    near = [x0] + [None] * 3
    for d in (1, 3, 2):
        near[d] = move_two(x0, d, "zy")
    near = jnp.stack(near)
    far = [near] + [None] * 3
    for d in (1, 3, 2):
        far[d] = move_two(near, d, "yz")
    return far


def gather_right(tile):
    got = [move_x(tile, d) for d in (1, 3, 2)]
    other = swap_core(tile)
    same = jnp.concatenate([tile, got[0], got[2], got[1]])
    rest = swap_core(same[tile.shape[0]:])
    return jnp.concatenate([same, other, rest])


def body(density, core_ham, block_mask, send_blocks, task_atoms, basis, v_loc):
    block_rows = density.shape[0] // block_edge
    block_cols = density.shape[1] // block_edge
    local_count = block_rows * block_cols
    area = block_edge * block_edge
    slot_count = send_blocks.shape[2]
    device_count = send_blocks.shape[1]
    row, col = lax.axis_index("row"), lax.axis_index("col")
    x_at, c_at, y_at, z_at = row // NC, row % NC, col // NZ, col % NZ

    slots = send_blocks[0].reshape(-1)
    spot = jnp.arange(local_count, dtype=jnp.int32)
    in_half = local_count // 2
    local_ids = (spot % block_rows) * block_cols
    local_ids += 2 * ((spot % in_half) // block_rows) + spot // in_half
    pick = (slots[:, None] == local_ids[None, :]).astype(BF16)
    outgoing = send_tasks(pick, density)
    received = all_to_all(outgoing.reshape(device_count, slot_count, area)).reshape(-1, area)
    atoms = task_atoms[:, 0]
    pair = (
        (atoms[1] % 2) * (ATOMS * ATOMS // 2) + (atoms[1] // 2) * ATOMS + atoms[0]
    ).reshape(-1)
    pair_ids = jnp.arange(ATOMS * ATOMS, dtype=jnp.int32)
    gather_pairs = (pair_ids[:, None] == pair[None, :]).astype(BF16)
    spread_pairs = (pair[:, None] == pair_ids[None, :]).astype(BF16)
    k_slot = grid_build(gather_pairs, received, basis[0], v_loc, spread_pairs)
    returned = all_to_all(k_slot.reshape(device_count, slot_count, area)).reshape(-1, area)
    select = (local_ids[:, None] == slots[None, :]).astype(BF16)
    mask = jnp.broadcast_to(
        block_mask.astype(F32)[:, None, :, None],
        (block_rows, block_edge, block_cols, block_edge),
    ).reshape(density.shape)
    scale = 1.0 / math.sqrt(16.0 * block_rows * NX * NC)
    ks_matrix, x0 = ham_build(scale, select, returned, core_ham, mask)

    left = gather_left(x0)
    shift = jnp.arange(NY * NZ, dtype=jnp.int32)
    outer, inner = shift // NZ, shift % NZ
    dy = jnp.where(c_at == 0, outer, inner)
    dz = jnp.where(c_at == 0, inner, outer)
    src = ((y_at - dy) % NY) * NZ + (z_at - dz) % NZ
    src_x, src_c = src // (2 * NC), (src // 2) % NC
    where = (((src_c ^ c_at) * NX + (x_at - src_x) % NX) * 2 + src % 2).astype(jnp.int32)
    x2 = panel_call(
        square_kernel, where, [*left, gather_right(x0), mask], x0.shape, BF16
    )
    sign_step = panel_call(
        lambda *refs: cube_kernel(scale, *refs),
        where,
        [*left, gather_right(x2), mask, x0],
        x0.shape,
        F32,
    )
    return (ks_matrix, sign_step)


def solution(mesh):
    placed = (
        P("row", "col"),
        P("row", "col"),
        P("row", "col"),
        P(("row", "col"), None, None),
        P(None, ("row", "col"), None, None),
        P(("row", "col"), None, None),
        P(("row", "col"), None),
    )
    return jax.shard_map(
        body,
        mesh=mesh,
        in_specs=placed,
        out_specs=(P("row", "col"), P("row", "col")),
        check_vma=False,
    )
```

```python
import math

import jax
import jax.numpy as jnp
from jax import lax
from jax.experimental import pallas as pl
from jax.experimental.pallas import tpu as pltpu
from jax.sharding import PartitionSpec as P

ATOMS = 16
block_edge = 64
NX, NC, NY, NZ = 4, 2, 4, 4
F32 = jnp.float32
BF16 = jnp.bfloat16


def move_x(v, d):
    pairs = [(x * NC + c, ((x + d) % NX) * NC + c) for x in range(NX) for c in range(NC)]
    return lax.ppermute(v, "row", pairs)


def swap_core(v):
    pairs = [(x * NC + c, x * NC + 1 - c) for x in range(NX) for c in range(NC)]
    return lax.ppermute(v, "row", pairs)


def place(x, c, y, z):
    return ((x % NX) * NC + c) * (NY * NZ) + (y % NY) * NZ + z % NZ


def move_two(v, d, axes):
    pairs = []
    for x in range(NX):
        for c in range(NC):
            for y in range(NY):
                for z in range(NZ):
                    step = {"x": 0, "y": 0, "z": 0}
                    step[axes[c]] = d
                    there = place(x + step["x"], c, y + step["y"], z + step["z"])
                    pairs.append((place(x, c, y, z), there))
    return lax.ppermute(v, ("row", "col"), pairs)


def low_half(shape):
    return lax.broadcasted_iota(jnp.int32, shape, 1) < block_edge


def trade_halves(first, second):
    low = low_half(first.shape)
    turned_first = pltpu.roll(first, block_edge, 1)
    turned_second = pltpu.roll(second, block_edge, 1)
    return jnp.where(low, first, turned_second), jnp.where(low, turned_first, second)


def blocks_to_matrix(blocks, matrix_ref, first_row, heights):
    groups, _, lanes = matrix_ref.shape
    half = heights * groups
    for tile in range(blocks.shape[1] // lanes):
        cut = slice(tile * lanes, (tile + 1) * lanes)
        rows = trade_halves(blocks[:half, cut], blocks[half:, cut])
        for odd in range(2):
            for group in range(groups):
                matrix_ref[group, pl.ds(first_row + 2 * tile + odd, heights, stride=block_edge), :] = (
                    rows[odd][group * heights : (group + 1) * heights]
                )


def matrix_to_blocks(matrix_ref, first_row, tiles, heights):
    groups = matrix_ref.shape[0]
    out = []
    for tile in range(tiles):
        rows = [
            jnp.concatenate(
                [
                    matrix_ref[group, pl.ds(first_row + 2 * tile + odd, heights, stride=block_edge), :]
                    for group in range(groups)
                ],
                axis=0,
            )
            for odd in range(2)
        ]
        out.append(jnp.concatenate(trade_halves(*rows), axis=0))
    return jnp.concatenate(out, axis=1)


def fold(matrix_ref, split_ref):
    groups, _, lanes = split_ref.shape
    for group in range(groups):
        split_ref[group] = matrix_ref[:, group * lanes : (group + 1) * lanes].astype(F32)


def split_scratch(shape):
    lanes = 2 * block_edge
    return pltpu.VMEM((shape[1] // lanes, shape[0], lanes), F32)


AREA = block_edge * block_edge
HALF = AREA // NC
WIDE = 1408
THIN = HALF - WIDE
HALF_ROWS = HALF // block_edge
CHUNK = 512
CHUNK_ROWS = CHUNK // block_edge
CHUNK_TILES = CHUNK // (2 * block_edge)
CAP = 8
LOCAL = 32
LISTED = 72
VMEM_SPEC = pl.BlockSpec(memory_space=pltpu.VMEM)
SMEM_SPEC = pl.BlockSpec(memory_space=pltpu.SMEM)


def whole_call(kernel, operands, shapes, flops, moved, scalars=0, scratch=()):
    return pl.pallas_call(
        kernel,
        in_specs=[SMEM_SPEC] * scalars + [VMEM_SPEC] * (len(operands) - scalars),
        out_specs=[VMEM_SPEC] * len(shapes),
        out_shape=[jax.ShapeDtypeStruct(shape, dtype) for shape, dtype in shapes],
        scratch_shapes=list(scratch),
        compiler_params=pltpu.CompilerParams(vmem_limit_bytes=40 << 20),
        cost_estimate=pl.CostEstimate(flops=flops, bytes_accessed=moved, transcendentals=0),
    )(*operands)


def split_kernel(core_ref, density_ref, mine_ref, other_ref, wide_ref):
    fold(density_ref, wide_ref)
    heights = density_ref.shape[0] // block_edge
    mine = core_ref[0] * HALF_ROWS
    for ref, first in ((mine_ref, mine), (other_ref, HALF_ROWS - mine)):
        for chunk in range(HALF // CHUNK):
            blocks = matrix_to_blocks(wide_ref, first + chunk * CHUNK_ROWS, CHUNK_TILES, heights)
            ref[:, chunk * CHUNK : (chunk + 1) * CHUNK] = blocks.astype(BF16)


def iota(shape, dim):
    return lax.broadcasted_iota(jnp.int32, shape, dim)


def select_kernel(*refs):
    pieces, find_ref = refs[0:4], refs[4]
    outs, turned_ref = refs[5:9], refs[9]
    tasks, span = 64 * CAP, 4 * NC * LOCAL
    lists = 4 * 8
    rows = iota((tasks, lists), 0)
    want = 8 * ((rows // (NC * CAP)) % 4) + 2 * ((rows // CAP) % NC)
    at = iota((tasks, lists), 1)
    pick = [(at == want + h).astype(BF16) for h in range(2)]
    row, lane = iota((tasks, 64), 0), iota((tasks, 64), 1)
    keep = lane == (row // (8 * CAP)) * CAP + row % CAP
    ones = jnp.ones((64, span), BF16)

    def number(lanes):
        spot = lanes % LOCAL
        return (spot % 8) * 4 + 2 * ((spot // 8) % 2) + spot // 16

    here = (iota((tasks, span), 0) // CAP) % 8 == iota((tasks, span), 1) // LOCAL
    block = number(iota((tasks, span), 1)).astype(F32)
    here_turned = (iota((span, tasks), 1) // CAP) % 8 == iota((span, tasks), 0) // LOCAL
    block_turned = number(iota((span, tasks), 0)).astype(F32)
    for step in range(4):
        piece = pieces[step]
        names = jnp.concatenate([piece[k, 64:LISTED, :CHUNK] for k in range(4)], axis=0)
        full = None
        for h in range(2):
            found = jnp.dot(names, find_ref[h], preferred_element_type=F32).astype(BF16)
            term = jnp.dot(pick[h], found, preferred_element_type=F32)
            full = term if full is None else full + term
        kept = jnp.where(keep, full, 0.0).astype(BF16)
        value = jnp.dot(kept, ones, preferred_element_type=F32)
        chosen = (here & (value == block)).astype(BF16)
        value_turned = lax.dot_general(
            ones, kept, (((0,), (1,)), ((), ())), preferred_element_type=F32
        )
        turned_ref[step] = (here_turned & (value_turned == block_turned)).astype(BF16)
        table = jnp.concatenate([piece[k, 0:64, :] for k in range(4)], axis=0)
        got = jnp.dot(chosen, table, preferred_element_type=F32).astype(BF16)
        for hop in range(4):
            for side in range(NC):
                start = (hop * NC + side) * 64
                outs[hop][side, step * 64 : (step + 1) * 64, :] = got[start : start + 64]


def select_tasks(pieces, find, width):
    shapes = [((NC, 256, width), BF16)] * 4 + [((4, 256, 512), BF16)]
    out = whole_call(
        select_kernel, [*pieces, find], shapes, 2 * 4 * 512 * 256 * width, 2 * 3200 * width
    )
    return out[0:4], out[4]


def reduce_kernel(*refs):
    turned_ref, parts, outs = refs[0], refs[1:5], refs[5:9]
    for step in range(4):
        tasks = jnp.concatenate(
            [
                parts[hop][side, step * 64 : (step + 1) * 64, :]
                for hop in range(4)
                for side in range(NC)
            ],
            axis=0,
        )
        outs[step][...] = jnp.dot(turned_ref[step], tasks, preferred_element_type=F32).astype(BF16)


def reduce_tasks(turned, parts, width):
    return whole_call(
        reduce_kernel,
        [turned, *parts],
        [((256, width), BF16)] * 4,
        2 * 4 * 512 * 256 * width,
        2 * 3072 * width,
    )


def pair_kernel(*refs):
    wide_sel, thin_sel = refs[0], refs[1]
    wide, thin, outs = refs[2:6], refs[6:10], refs[10:12]
    for side in range(NC):
        start = 0
        for select, parts in ((wide_sel, wide), (thin_sel, thin)):
            total = None
            for hop in range(4):
                term = jnp.dot(
                    select[side, :, hop * 256 : (hop + 1) * 256],
                    parts[hop][side],
                    preferred_element_type=F32,
                )
                total = term if total is None else total + term
            width = parts[0].shape[2]
            outs[side][:, start : start + width] = total.astype(BF16)
            start += width


def spread_kernel(select_ref, *refs):
    tables, outs = refs[0:2], refs[2:6]
    for hop in range(4):
        for side in range(NC):
            outs[hop][side] = jnp.dot(
                select_ref[side, hop * 256 : (hop + 1) * 256, :],
                tables[side][...],
                preferred_element_type=F32,
            ).astype(BF16)


def grid_kernel(
    core_ref, mine_ref, other_ref, basis_ref, vloc_ref, out_ref, out_other_ref, wide_ref, pair_ref, acc_ref
):
    step = pl.program_id(0)
    mine = core_ref[0] * HALF_ROWS

    @pl.when(step == 0)
    def _():
        for ref, first in ((mine_ref, mine), (other_ref, HALF_ROWS - mine)):

            @pl.loop(0, HALF // CHUNK)
            def _(chunk):
                lanes = pl.ds(pl.multiple_of(chunk * CHUNK, CHUNK), CHUNK)
                sums = ref[:, lanes].astype(F32)
                blocks_to_matrix(sums, wide_ref, first + chunk * CHUNK_ROWS, ATOMS)

        for group in range(wide_ref.shape[0]):
            lanes = slice(group * 2 * block_edge, (group + 1) * 2 * block_edge)
            pair_ref[:, lanes] = wide_ref[group].astype(BF16)
        acc_ref[...] = jnp.zeros_like(acc_ref)

    vals = basis_ref[...]
    mixed = jnp.dot(pair_ref[...], vals, preferred_element_type=F32)
    wide = vals.astype(F32)
    rho = jnp.sum(wide * mixed, axis=0, keepdims=True)
    pot = vloc_ref[...] + 0.5 * rho / jnp.sqrt(1.0 + rho * rho)
    weighted = (wide * pot).astype(BF16)
    acc_ref[...] += lax.dot_general(
        weighted, vals, (((1,), (1,)), ((), ())), preferred_element_type=F32
    )

    @pl.when(step == pl.num_programs(0) - 1)
    def _():
        fold(acc_ref, wide_ref)
        for ref, first in ((out_ref, mine), (out_other_ref, HALF_ROWS - mine)):

            @pl.loop(0, HALF // CHUNK)
            def _(chunk):
                lanes = pl.ds(pl.multiple_of(chunk * CHUNK, CHUNK), CHUNK)
                blocks = matrix_to_blocks(
                    wide_ref, first + chunk * CHUNK_ROWS, CHUNK_TILES, ATOMS
                )
                ref[:, lanes] = blocks.astype(BF16)


def grid_build(core, mine, other, basis_vals, v_loc):
    order, cells = basis_vals.shape
    tile = 512
    fixed = pl.BlockSpec(mine.shape, lambda g: (0, 0))
    return pl.pallas_call(
        grid_kernel,
        grid=(cells // tile,),
        in_specs=[
            SMEM_SPEC,
            fixed,
            fixed,
            pl.BlockSpec((order, tile), lambda g: (0, g)),
            pl.BlockSpec((1, tile), lambda g: (0, g)),
        ],
        out_specs=[fixed, fixed],
        out_shape=[jax.ShapeDtypeStruct(mine.shape, BF16)] * 2,
        scratch_shapes=[
            split_scratch((order, order)),
            pltpu.VMEM((order, order), BF16),
            pltpu.VMEM((order, order), F32),
        ],
        compiler_params=pltpu.CompilerParams(vmem_limit_bytes=48 << 20),
        cost_estimate=pl.CostEstimate(
            flops=4 * order * order * cells,
            bytes_accessed=2 * order * cells + 8 * order * order,
            transcendentals=cells,
        ),
    )(core, mine, other, basis_vals, v_loc)


def ham_kernel(scale, core_ref, mine_ref, other_ref, ham_ref, mask_ref, ks_ref, x0_ref, wide_ref):
    heights = ham_ref.shape[0] // block_edge
    mine = core_ref[0] * HALF_ROWS
    for ref, first in ((mine_ref, mine), (other_ref, HALF_ROWS - mine)):
        for chunk in range(HALF // CHUNK):
            sums = ref[:, chunk * CHUNK : (chunk + 1) * CHUNK]
            blocks_to_matrix(sums, wide_ref, first + chunk * CHUNK_ROWS, heights)
    for group in range(wide_ref.shape[0]):
        lanes = slice(group * 2 * block_edge, (group + 1) * 2 * block_edge)
        total = ham_ref[:, lanes] + wide_ref[group]
        ks_ref[:, lanes] = total
        x0_ref[:, lanes] = (mask_ref[:, lanes] * total * scale).astype(BF16)


def panel_sum(where_ref, left, right_ref):
    total = None
    for outer in range(4):
        for inner in range(4):
            piece = left[outer][inner]
            depth = piece.shape[1]
            start = pl.multiple_of(where_ref[outer * 4 + inner] * depth, depth)
            term = jnp.dot(piece, right_ref[pl.ds(start, depth), :], preferred_element_type=F32)
            total = term if total is None else total + term
    return total


def square_kernel(where_ref, *refs):
    right_ref, mask_ref, out_ref = refs[4:7]
    out_ref[...] = (mask_ref[...] * panel_sum(where_ref, refs[0:4], right_ref)).astype(BF16)


def cube_kernel(scale, where_ref, *refs):
    right_ref, mask_ref, x0_ref, out_ref = refs[4:8]
    x3 = mask_ref[...] * panel_sum(where_ref, refs[0:4], right_ref)
    out_ref[...] = (1.5 * x0_ref[...].astype(F32) - 0.5 * x3) / scale


def panel_call(kernel, where, operands, shape, dtype):
    vmem = pl.BlockSpec(memory_space=pltpu.VMEM)
    rows, cols = shape
    return pl.pallas_call(
        kernel,
        in_specs=[pl.BlockSpec(memory_space=pltpu.SMEM)] + [vmem] * len(operands),
        out_specs=vmem,
        out_shape=jax.ShapeDtypeStruct(shape, dtype),
        compiler_params=pltpu.CompilerParams(vmem_limit_bytes=40 << 20),
        cost_estimate=pl.CostEstimate(
            flops=2 * rows * cols * 4096, bytes_accessed=7 << 20, transcendentals=0
        ),
    )(where, *operands)


def gather_left(x0):
    near = [x0] + [None] * 3
    for d in (1, 3, 2):
        near[d] = move_two(x0, d, "zy")
    near = jnp.stack(near)
    far = [near] + [None] * 3
    for d in (1, 3, 2):
        far[d] = move_two(near, d, "yz")
    return far


def gather_right(tile):
    got = [move_x(tile, d) for d in (1, 3, 2)]
    other = swap_core(tile)
    same = jnp.concatenate([tile, got[0], got[2], got[1]])
    rest = swap_core(same[tile.shape[0]:])
    return jnp.concatenate([same, other, rest])


def body(density, core_ham, block_mask, send_blocks, task_atoms, basis, v_loc):
    block_rows = density.shape[0] // block_edge
    block_cols = density.shape[1] // block_edge
    device_count = send_blocks.shape[1]
    row, col = lax.axis_index("row"), lax.axis_index("col")
    x_at, c_at, y_at, z_at = row // NC, row % NC, col // NZ, col % NZ

    core = c_at.astype(jnp.int32).reshape(1)

    where_wide = [jnp.where(c_at == 0, p, q) for p, q in ((x_at, y_at), (y_at, z_at), (z_at, x_at))]
    where_thin = [z_at, x_at, y_at]

    def device_of(spots, cores, thin):
        one, two, three = [v % 4 for v in spots]
        if thin:
            return place(two, cores, three, one)
        return jnp.where(c_at == 0, place(one, cores, two, three), place(three, cores, one, two))

    slots = send_blocks[0]
    names = slots.reshape(2, CHUNK).astype(BF16)
    names = jnp.concatenate(
        [
            names,
            jnp.zeros((2, WIDE - CHUNK), BF16),
            names,
            jnp.zeros((2, THIN - CHUNK), BF16),
        ],
        axis=1,
    )
    mine, other = whole_call(
        split_kernel,
        [core, density],
        [((LOCAL, HALF), BF16)] * 2,
        0,
        1 << 20,
        scalars=1,
        scratch=[split_scratch(density.shape)],
    )
    sent = swap_core(jnp.concatenate([other, names, jnp.zeros((6, HALF), BF16)]))
    chip = jnp.concatenate(
        [mine, sent[:LOCAL], names, sent[LOCAL : LOCAL + 2], jnp.zeros((4, HALF), BF16)]
    )

    def gather(v, far_axes, near_axes):
        near = [v] + [None] * 3
        for d in (1, 3, 2):
            near[d] = move_two(v, d, far_axes)
        near = jnp.stack(near)
        out = [near] + [None] * 3
        for d in (1, 3, 2):
            out[d] = move_two(near, d, near_axes)
        return out

    wide_pieces = gather(chip[:, :WIDE], "zx", "yz")
    thin_pieces = gather(chip[:, WIDE:], "yy", "xx")

    atoms = task_atoms[:, 0]
    pair = (atoms[1] % 2) * (ATOMS * ATOMS // 2) + (atoms[1] // 2) * ATOMS + atoms[0]
    pair = pair.astype(BF16)
    pairs = jnp.concatenate([pair, swap_core(pair)], axis=1)
    pair_ids = jnp.arange(ATOMS * ATOMS, dtype=jnp.int32).astype(F32)

    def plans(spots, thin):
        j = jnp.arange(device_count, dtype=jnp.int32)
        away = (j // 32, (j // 8) % 4, (j // 2) % 4)
        owner = device_of([p - d for p, d in zip(spots, away)], c_at ^ (j % 2), thin)
        order = (owner[:, None] == j[None, :]).astype(BF16)
        moved = jnp.dot(order, pairs, preferred_element_type=F32)
        moved = moved.reshape(device_count, NC, CAP).transpose(1, 0, 2).reshape(NC, -1)
        gather_sel = (pair_ids[None, :, None] == moved[:, None, :]).astype(BF16)
        spread_sel = (moved[:, :, None] == pair_ids[None, None, :]).astype(BF16)
        k = jnp.arange(64, dtype=jnp.int32)
        dest = device_of(
            [spots[0] + k // 16, spots[1] + 0 * k, spots[2] + 0 * k], c_at ^ ((k // 8) % 2), thin
        )
        target = dest * CAP + k % CAP
        line = jnp.arange(2 * CHUNK, dtype=jnp.int32).reshape(2, CHUNK, 1)
        find = (line == target[None, None, :]).astype(BF16)
        return gather_sel, spread_sel, find

    gather_wide, spread_wide, find_wide = plans(where_wide, False)
    gather_thin, spread_thin, find_thin = plans(where_thin, True)

    def exchange(parts, axes, sign):
        out = [parts[0]] + [None] * 3
        for d in (1, 3, 2):
            out[d] = move_two(parts[d], sign * d, axes)
        return out

    wide_tasks, wide_turned = select_tasks(wide_pieces, find_wide, WIDE)
    wide_tasks = exchange(wide_tasks, "xy", 1)
    thin_tasks, thin_turned = select_tasks(thin_pieces, find_thin, THIN)
    thin_tasks = exchange(thin_tasks, "zz", 1)
    pair_mine, pair_other = whole_call(
        pair_kernel,
        [gather_wide, gather_thin, *wide_tasks, *thin_tasks],
        [((256, HALF), BF16)] * 2,
        4 * 256 * 1024 * HALF,
        10 << 20,
    )
    k_mine, k_other = grid_build(core, pair_mine, swap_core(pair_other), basis[0], v_loc)
    k_swapped = swap_core(k_other)

    def spread(select, lanes, width):
        return whole_call(
            spread_kernel,
            [select, k_mine[:, lanes], k_swapped[:, lanes]],
            [((NC, 256, width), BF16)] * 4,
            4 * 256 * 1024 * width,
            2 * 2600 * width,
        )

    wide_back = exchange(spread(spread_wide, slice(0, WIDE), WIDE), "xy", -1)
    thin_back = exchange(spread(spread_thin, slice(WIDE, HALF), THIN), "zz", -1)

    def add_up(parts):
        total = parts[0].astype(F32)
        for part in parts[1:]:
            total = total + part.astype(F32)
        return total

    def scatter(parts, near_axes, far_axes):
        near = add_up(exchange(parts, near_axes, -1)).astype(BF16)
        far = [near[64 * d : 64 * (d + 1)] for d in range(4)]
        return add_up(exchange(far, far_axes, -1))

    wide_ham = scatter(reduce_tasks(wide_turned, wide_back, WIDE), "yz", "zx")
    thin_ham = scatter(reduce_tasks(thin_turned, thin_back, THIN), "xx", "yy")
    ham = jnp.concatenate([wide_ham, thin_ham], axis=1)
    ham_other = swap_core(ham[LOCAL:])
    mask = jnp.broadcast_to(
        block_mask.astype(F32)[:, None, :, None],
        (block_rows, block_edge, block_cols, block_edge),
    ).reshape(density.shape)
    scale = 1.0 / math.sqrt(16.0 * block_rows * NX * NC)
    ks_matrix, x0 = whole_call(
        lambda *refs: ham_kernel(scale, *refs),
        [core, ham[:LOCAL], ham_other, core_ham, mask],
        [(density.shape, F32), (density.shape, BF16)],
        0,
        2 << 20,
        scalars=1,
        scratch=[split_scratch(density.shape)],
    )

    left = gather_left(x0)
    shift = jnp.arange(NY * NZ, dtype=jnp.int32)
    outer, inner = shift // NZ, shift % NZ
    dy = jnp.where(c_at == 0, outer, inner)
    dz = jnp.where(c_at == 0, inner, outer)
    src = ((y_at - dy) % NY) * NZ + (z_at - dz) % NZ
    src_x, src_c = src // (2 * NC), (src // 2) % NC
    where = (((src_c ^ c_at) * NX + (x_at - src_x) % NX) * 2 + src % 2).astype(jnp.int32)
    x2 = panel_call(
        square_kernel, where, [*left, gather_right(x0), mask], x0.shape, BF16
    )
    sign_step = panel_call(
        lambda *refs: cube_kernel(scale, *refs),
        where,
        [*left, gather_right(x2), mask, x0],
        x0.shape,
        F32,
    )
    return (ks_matrix, sign_step)


def solution(mesh):
    placed = (
        P("row", "col"),
        P("row", "col"),
        P("row", "col"),
        P(("row", "col"), None, None),
        P(None, ("row", "col"), None, None),
        P(("row", "col"), None, None),
        P(("row", "col"), None),
    )
    return jax.shard_map(
        body,
        mesh=mesh,
        in_specs=placed,
        out_specs=(P("row", "col"), P("row", "col")),
        check_vma=False,
    )
```

```python
import math

import jax
import jax.numpy as jnp
from jax import lax
from jax.experimental import pallas as pl
from jax.experimental.pallas import tpu as pltpu
from jax.sharding import PartitionSpec as P

ATOMS = 16
block_edge = 64
NX, NC, NY, NZ = 4, 2, 4, 4
F32 = jnp.float32
BF16 = jnp.bfloat16


def move_x(v, d):
    pairs = [(x * NC + c, ((x + d) % NX) * NC + c) for x in range(NX) for c in range(NC)]
    return lax.ppermute(v, "row", pairs)


def swap_core(v):
    pairs = [(x * NC + c, x * NC + 1 - c) for x in range(NX) for c in range(NC)]
    return lax.ppermute(v, "row", pairs)


def place(x, c, y, z):
    return ((x % NX) * NC + c) * (NY * NZ) + (y % NY) * NZ + z % NZ


def move_two(v, d, axes):
    pairs = []
    for x in range(NX):
        for c in range(NC):
            for y in range(NY):
                for z in range(NZ):
                    step = {"x": 0, "y": 0, "z": 0}
                    step[axes[c]] = d
                    there = place(x + step["x"], c, y + step["y"], z + step["z"])
                    pairs.append((place(x, c, y, z), there))
    return lax.ppermute(v, ("row", "col"), pairs)


def low_half(shape):
    return lax.broadcasted_iota(jnp.int32, shape, 1) < block_edge


def trade_halves(first, second):
    low = low_half(first.shape)
    turned_first = pltpu.roll(first, block_edge, 1)
    turned_second = pltpu.roll(second, block_edge, 1)
    return jnp.where(low, first, turned_second), jnp.where(low, turned_first, second)


def blocks_to_matrix(blocks, matrix_ref, first_row, heights):
    groups, _, lanes = matrix_ref.shape
    half = heights * groups
    for tile in range(blocks.shape[1] // lanes):
        cut = slice(tile * lanes, (tile + 1) * lanes)
        rows = trade_halves(blocks[:half, cut], blocks[half:, cut])
        for odd in range(2):
            for group in range(groups):
                matrix_ref[group, pl.ds(first_row + 2 * tile + odd, heights, stride=block_edge), :] = (
                    rows[odd][group * heights : (group + 1) * heights]
                )


def matrix_to_blocks(matrix_ref, first_row, tiles, heights):
    groups = matrix_ref.shape[0]
    out = []
    for tile in range(tiles):
        rows = [
            jnp.concatenate(
                [
                    matrix_ref[group, pl.ds(first_row + 2 * tile + odd, heights, stride=block_edge), :]
                    for group in range(groups)
                ],
                axis=0,
            )
            for odd in range(2)
        ]
        out.append(jnp.concatenate(trade_halves(*rows), axis=0))
    return jnp.concatenate(out, axis=1)


def fold(matrix_ref, split_ref):
    groups, _, lanes = split_ref.shape
    for group in range(groups):
        split_ref[group] = matrix_ref[:, group * lanes : (group + 1) * lanes].astype(F32)


def split_scratch(shape):
    lanes = 2 * block_edge
    return pltpu.VMEM((shape[1] // lanes, shape[0], lanes), F32)


AREA = block_edge * block_edge
HALF = AREA // NC
WIDE = 1408
THIN = HALF - WIDE
HALF_ROWS = HALF // block_edge
CHUNK = 512
CHUNK_ROWS = CHUNK // block_edge
CHUNK_TILES = CHUNK // (2 * block_edge)
CAP = 8
LOCAL = 32
LISTED = 72
VMEM_SPEC = pl.BlockSpec(memory_space=pltpu.VMEM)
SMEM_SPEC = pl.BlockSpec(memory_space=pltpu.SMEM)


def whole_call(kernel, operands, shapes, flops, moved, scalars=0, scratch=()):
    return pl.pallas_call(
        kernel,
        in_specs=[SMEM_SPEC] * scalars + [VMEM_SPEC] * (len(operands) - scalars),
        out_specs=[VMEM_SPEC] * len(shapes),
        out_shape=[jax.ShapeDtypeStruct(shape, dtype) for shape, dtype in shapes],
        scratch_shapes=list(scratch),
        compiler_params=pltpu.CompilerParams(vmem_limit_bytes=40 << 20),
        cost_estimate=pl.CostEstimate(flops=flops, bytes_accessed=moved, transcendentals=0),
    )(*operands)


def split_kernel(core_ref, density_ref, mine_ref, other_ref, wide_ref):
    fold(density_ref, wide_ref)
    heights = density_ref.shape[0] // block_edge
    mine = core_ref[0] * HALF_ROWS
    for ref, first in ((mine_ref, mine), (other_ref, HALF_ROWS - mine)):
        for chunk in range(HALF // CHUNK):
            blocks = matrix_to_blocks(wide_ref, first + chunk * CHUNK_ROWS, CHUNK_TILES, heights)
            ref[:, chunk * CHUNK : (chunk + 1) * CHUNK] = blocks.astype(BF16)


def iota(shape, dim):
    return lax.broadcasted_iota(jnp.int32, shape, dim)


def lane_loop(width, body):
    step = 256
    whole = width // step

    @pl.loop(0, whole)
    def _(k):
        body(pl.ds(pl.multiple_of(k * step, step), step))

    if width % step:
        body(pl.ds(whole * step, width % step))


def select_kernel(*refs):
    pieces, find_ref = refs[0:4], refs[4]
    outs, turned_ref, names_ref, chosen_ref = refs[5:9], refs[9], refs[10], refs[11]
    tasks, span = 64 * CAP, 4 * NC * LOCAL
    lists = 4 * 8
    for step in range(4):
        for k in range(4):
            names_ref[step, 8 * k : 8 * k + 8] = pieces[step][k, 64:LISTED, :CHUNK].astype(F32)

    def number(lanes):
        spot = lanes % LOCAL
        return (spot % 8) * 4 + 2 * ((spot // 8) % 2) + spot // 16

    @pl.loop(0, 4)
    def _(step):
        rows = iota((tasks, lists), 0)
        want = 8 * ((rows // (NC * CAP)) % 4) + 2 * ((rows // CAP) % NC)
        at = iota((tasks, lists), 1)
        row, lane = iota((tasks, 64), 0), iota((tasks, 64), 1)
        keep = lane == (row // (8 * CAP)) * CAP + row % CAP
        ones = jnp.ones((64, span), BF16)
        names = names_ref[step].astype(BF16)
        full = None
        for h in range(2):
            found = jnp.dot(names, find_ref[h], preferred_element_type=F32).astype(BF16)
            pick = (at == want + h).astype(BF16)
            term = jnp.dot(pick, found, preferred_element_type=F32)
            full = term if full is None else full + term
        kept = jnp.where(keep, full, 0.0).astype(BF16)
        value = jnp.dot(kept, ones, preferred_element_type=F32)
        here = (iota((tasks, span), 0) // CAP) % 8 == iota((tasks, span), 1) // LOCAL
        block = number(iota((tasks, span), 1)).astype(F32)
        chosen_ref[step] = (here & (value == block)).astype(BF16)
        value = lax.dot_general(ones, kept, (((0,), (1,)), ((), ())), preferred_element_type=F32)
        here = (iota((span, tasks), 1) // CAP) % 8 == iota((span, tasks), 0) // LOCAL
        block = number(iota((span, tasks), 0)).astype(F32)
        turned_ref[step] = (here & (value == block)).astype(BF16)

    def body(lanes):
        for step in range(4):
            table = jnp.concatenate([pieces[step][k, 0:64, lanes] for k in range(4)], axis=0)
            got = jnp.dot(chosen_ref[step], table, preferred_element_type=F32).astype(BF16)
            for hop in range(4):
                for side in range(NC):
                    start = (hop * NC + side) * 64
                    outs[hop][side, step * 64 : (step + 1) * 64, lanes] = got[start : start + 64]

    lane_loop(outs[0].shape[2], body)


def select_tasks(pieces, find, width):
    shapes = [((NC, 256, width), BF16)] * 4 + [((4, 256, 512), BF16)]
    out = whole_call(
        select_kernel,
        [*pieces, find],
        shapes,
        2 * 4 * 512 * 256 * width,
        2 * 3200 * width,
        scratch=[pltpu.VMEM((4, 32, CHUNK), F32), pltpu.VMEM((4, 512, 256), BF16)],
    )
    return out[0:4], out[4]


def reduce_kernel(*refs):
    turned_ref, parts, outs = refs[0], refs[1:5], refs[5:9]

    def body(lanes):
        for step in range(4):
            tasks = jnp.concatenate(
                [
                    parts[hop][side, step * 64 : (step + 1) * 64, lanes]
                    for hop in range(4)
                    for side in range(NC)
                ],
                axis=0,
            )
            total = jnp.dot(turned_ref[step], tasks, preferred_element_type=F32)
            outs[step][:, lanes] = total.astype(BF16)

    lane_loop(outs[0].shape[1], body)


def reduce_tasks(turned, parts, width):
    return whole_call(
        reduce_kernel,
        [turned, *parts],
        [((256, width), BF16)] * 4,
        2 * 4 * 512 * 256 * width,
        2 * 3072 * width,
    )


def pair_kernel(*refs):
    wide_sel, thin_sel = refs[0], refs[1]
    wide, thin, outs = refs[2:6], refs[6:10], refs[10:12]
    for side in range(NC):
        start = 0
        for select, parts in ((wide_sel, wide), (thin_sel, thin)):

            def body(lanes, side=side, start=start, select=select, parts=parts):
                total = None
                for hop in range(4):
                    term = jnp.dot(
                        select[side, :, hop * 256 : (hop + 1) * 256],
                        parts[hop][side, :, lanes],
                        preferred_element_type=F32,
                    )
                    total = term if total is None else total + term
                where = lanes.start + start
                if not isinstance(where, int):
                    where = pl.multiple_of(where, 128)
                outs[side][:, pl.ds(where, lanes.size)] = total.astype(BF16)

            lane_loop(parts[0].shape[2], body)
            start += parts[0].shape[2]


def spread_kernel(select_ref, *refs):
    tables, outs = refs[0:2], refs[2:6]

    def body(lanes):
        for hop in range(4):
            for side in range(NC):
                outs[hop][side, :, lanes] = jnp.dot(
                    select_ref[side, hop * 256 : (hop + 1) * 256, :],
                    tables[side][:, lanes],
                    preferred_element_type=F32,
                ).astype(BF16)

    lane_loop(outs[0].shape[2], body)


def grid_kernel(
    core_ref, mine_ref, other_ref, basis_ref, vloc_ref, out_ref, out_other_ref, wide_ref, pair_ref, pot_ref
):
    mine = core_ref[0] * HALF_ROWS
    order, cells = basis_ref.shape
    tile, lanes_of_tile = 256, 2 * block_edge
    for ref, first in ((mine_ref, mine), (other_ref, HALF_ROWS - mine)):

        @pl.loop(0, HALF // CHUNK)
        def _(chunk):
            lanes = pl.ds(pl.multiple_of(chunk * CHUNK, CHUNK), CHUNK)
            sums = ref[:, lanes].astype(F32)
            blocks_to_matrix(sums, wide_ref, first + chunk * CHUNK_ROWS, ATOMS)

    for group in range(wide_ref.shape[0]):
        pair_ref[:, group * lanes_of_tile : (group + 1) * lanes_of_tile] = wide_ref[group].astype(BF16)

    @pl.loop(0, cells // tile)
    def _(step):
        lanes = pl.ds(pl.multiple_of(step * tile, tile), tile)
        vals = basis_ref[:, lanes]
        mixed = jnp.dot(pair_ref[...], vals, preferred_element_type=F32)
        wide = vals.astype(F32)
        rho = jnp.sum(wide * mixed, axis=0, keepdims=True)
        pot = vloc_ref[:, lanes] + 0.5 * rho / jnp.sqrt(1.0 + rho * rho)
        pot_ref[:, lanes] = (wide * pot).astype(BF16)

    @pl.loop(0, order // 256)
    def _(step):
        rows = pl.ds(pl.multiple_of(step * 256, 256), 256)
        part = lax.dot_general(
            pot_ref[...], basis_ref[rows, :], (((1,), (1,)), ((), ())), preferred_element_type=F32
        )
        for half in range(2):
            wide_ref[2 * step + half] = part[:, half * lanes_of_tile : (half + 1) * lanes_of_tile]

    for ref, first in ((out_ref, mine), (out_other_ref, HALF_ROWS - mine)):

        @pl.loop(0, HALF // CHUNK)
        def _(chunk):
            lanes = pl.ds(pl.multiple_of(chunk * CHUNK, CHUNK), CHUNK)
            blocks = matrix_to_blocks(wide_ref, first + chunk * CHUNK_ROWS, CHUNK_TILES, ATOMS)
            ref[:, lanes] = blocks.astype(BF16)


def grid_build(core, mine, other, basis_vals, v_loc):
    order, cells = basis_vals.shape
    return whole_call(
        grid_kernel,
        [core, mine, other, basis_vals, v_loc],
        [(mine.shape, BF16)] * 2,
        4 * order * order * cells,
        2 * order * cells + 8 * order * order,
        scalars=1,
        scratch=[
            split_scratch((order, order)),
            pltpu.VMEM((order, order), BF16),
            pltpu.VMEM((order, cells), BF16),
        ],
    )


def ham_kernel(scale, core_ref, mine_ref, other_ref, ham_ref, mask_ref, ks_ref, x0_ref, wide_ref):
    heights = ham_ref.shape[0] // block_edge
    mine = core_ref[0] * HALF_ROWS
    for ref, first in ((mine_ref, mine), (other_ref, HALF_ROWS - mine)):
        for chunk in range(HALF // CHUNK):
            sums = ref[:, chunk * CHUNK : (chunk + 1) * CHUNK]
            blocks_to_matrix(sums, wide_ref, first + chunk * CHUNK_ROWS, heights)
    for group in range(wide_ref.shape[0]):
        lanes = slice(group * 2 * block_edge, (group + 1) * 2 * block_edge)
        total = ham_ref[:, lanes] + wide_ref[group]
        ks_ref[:, lanes] = total
        x0_ref[:, lanes] = (mask_ref[:, lanes] * total * scale).astype(BF16)


def panel_sum(where_ref, left, right_ref):
    total = None
    for outer in range(4):
        for inner in range(4):
            piece = left[outer][inner]
            depth = piece.shape[1]
            start = pl.multiple_of(where_ref[outer * 4 + inner] * depth, depth)
            term = jnp.dot(piece, right_ref[pl.ds(start, depth), :], preferred_element_type=F32)
            total = term if total is None else total + term
    return total


def square_kernel(where_ref, *refs):
    right_ref, mask_ref, out_ref = refs[4:7]
    out_ref[...] = (mask_ref[...] * panel_sum(where_ref, refs[0:4], right_ref)).astype(BF16)


def cube_kernel(scale, where_ref, *refs):
    right_ref, mask_ref, x0_ref, out_ref = refs[4:8]
    x3 = mask_ref[...] * panel_sum(where_ref, refs[0:4], right_ref)
    out_ref[...] = (1.5 * x0_ref[...].astype(F32) - 0.5 * x3) / scale


def panel_call(kernel, where, operands, shape, dtype):
    vmem = pl.BlockSpec(memory_space=pltpu.VMEM)
    rows, cols = shape
    return pl.pallas_call(
        kernel,
        in_specs=[pl.BlockSpec(memory_space=pltpu.SMEM)] + [vmem] * len(operands),
        out_specs=vmem,
        out_shape=jax.ShapeDtypeStruct(shape, dtype),
        compiler_params=pltpu.CompilerParams(vmem_limit_bytes=40 << 20),
        cost_estimate=pl.CostEstimate(
            flops=2 * rows * cols * 4096, bytes_accessed=7 << 20, transcendentals=0
        ),
    )(where, *operands)


def gather_left(x0):
    near = [x0] + [None] * 3
    for d in (1, 3, 2):
        near[d] = move_two(x0, d, "zy")
    near = jnp.stack(near)
    far = [near] + [None] * 3
    for d in (1, 3, 2):
        far[d] = move_two(near, d, "yz")
    return far


def gather_right(tile):
    got = [move_x(tile, d) for d in (1, 3, 2)]
    other = swap_core(tile)
    same = jnp.concatenate([tile, got[0], got[2], got[1]])
    rest = swap_core(same[tile.shape[0]:])
    return jnp.concatenate([same, other, rest])


def body(density, core_ham, block_mask, send_blocks, task_atoms, basis, v_loc):
    block_rows = density.shape[0] // block_edge
    block_cols = density.shape[1] // block_edge
    device_count = send_blocks.shape[1]
    row, col = lax.axis_index("row"), lax.axis_index("col")
    x_at, c_at, y_at, z_at = row // NC, row % NC, col // NZ, col % NZ

    core = c_at.astype(jnp.int32).reshape(1)

    where_wide = [jnp.where(c_at == 0, p, q) for p, q in ((x_at, y_at), (y_at, z_at), (z_at, x_at))]
    where_thin = [z_at, x_at, y_at]

    def device_of(spots, cores, thin):
        one, two, three = [v % 4 for v in spots]
        if thin:
            return place(two, cores, three, one)
        return jnp.where(c_at == 0, place(one, cores, two, three), place(three, cores, one, two))

    slots = send_blocks[0]
    names = slots.reshape(2, CHUNK).astype(BF16)
    names = jnp.concatenate(
        [
            names,
            jnp.zeros((2, WIDE - CHUNK), BF16),
            names,
            jnp.zeros((2, THIN - CHUNK), BF16),
        ],
        axis=1,
    )
    mine, other = whole_call(
        split_kernel,
        [core, density],
        [((LOCAL, HALF), BF16)] * 2,
        0,
        1 << 20,
        scalars=1,
        scratch=[split_scratch(density.shape)],
    )
    sent = swap_core(jnp.concatenate([other, names, jnp.zeros((6, HALF), BF16)]))
    chip = jnp.concatenate(
        [mine, sent[:LOCAL], names, sent[LOCAL : LOCAL + 2], jnp.zeros((4, HALF), BF16)]
    )

    atoms = task_atoms[:, 0]
    pair = (atoms[1] % 2) * (ATOMS * ATOMS // 2) + (atoms[1] // 2) * ATOMS + atoms[0]
    pair = pair.astype(BF16)
    pair_other = swap_core(pair)

    def spread_out(v, axes):
        out = [v] + [None] * 3
        for d in (1, 3, 2):
            out[d] = move_two(v, d, axes)
        return out

    wide_near = spread_out(chip[:, :WIDE], "zx")
    thin_near = spread_out(chip[:, WIDE:], "yy")
    wide_near, thin_near, pair_other = lax.optimization_barrier((wide_near, thin_near, pair_other))
    wide_pieces = spread_out(jnp.stack(wide_near), "yz")
    thin_pieces = spread_out(jnp.stack(thin_near), "xx")
    wide_pieces, thin_pieces = lax.optimization_barrier((wide_pieces, thin_pieces))

    pairs = jnp.concatenate([pair, pair_other], axis=1)
    pair_ids = jnp.arange(ATOMS * ATOMS, dtype=jnp.int32).astype(F32)

    def plans(spots, thin):
        j = jnp.arange(device_count, dtype=jnp.int32)
        away = (j // 32, (j // 8) % 4, (j // 2) % 4)
        owner = device_of([p - d for p, d in zip(spots, away)], c_at ^ (j % 2), thin)
        order = (owner[:, None] == j[None, :]).astype(BF16)
        moved = jnp.dot(order, pairs, preferred_element_type=F32)
        moved = moved.reshape(device_count, NC, CAP).transpose(1, 0, 2).reshape(NC, -1)
        gather_sel = (pair_ids[None, :, None] == moved[:, None, :]).astype(BF16)
        spread_sel = (moved[:, :, None] == pair_ids[None, None, :]).astype(BF16)
        k = jnp.arange(64, dtype=jnp.int32)
        dest = device_of(
            [spots[0] + k // 16, spots[1] + 0 * k, spots[2] + 0 * k], c_at ^ ((k // 8) % 2), thin
        )
        target = dest * CAP + k % CAP
        line = jnp.arange(2 * CHUNK, dtype=jnp.int32).reshape(2, CHUNK, 1)
        find = (line == target[None, None, :]).astype(BF16)
        return gather_sel, spread_sel, find

    gather_wide, spread_wide, find_wide = plans(where_wide, False)
    gather_thin, spread_thin, find_thin = plans(where_thin, True)

    def exchange(parts, axes, sign):
        out = [parts[0]] + [None] * 3
        for d in (1, 3, 2):
            out[d] = move_two(parts[d], sign * d, axes)
        return out

    wide_tasks, wide_turned = select_tasks(wide_pieces, find_wide, WIDE)
    wide_tasks = exchange(wide_tasks, "xy", 1)
    thin_tasks, thin_turned = select_tasks(thin_pieces, find_thin, THIN)
    thin_tasks = exchange(thin_tasks, "zz", 1)
    sum_mine, sum_other = whole_call(
        pair_kernel,
        [gather_wide, gather_thin, *wide_tasks, *thin_tasks],
        [((256, HALF), BF16)] * 2,
        4 * 256 * 1024 * HALF,
        10 << 20,
    )
    k_mine, k_other = grid_build(core, sum_mine, swap_core(sum_other), basis[0], v_loc)
    k_swapped = swap_core(k_other)

    def spread(select, lanes, width):
        return whole_call(
            spread_kernel,
            [select, k_mine[:, lanes], k_swapped[:, lanes]],
            [((NC, 256, width), BF16)] * 4,
            4 * 256 * 1024 * width,
            2 * 2600 * width,
        )

    wide_back = exchange(spread(spread_wide, slice(0, WIDE), WIDE), "xy", -1)
    thin_back = exchange(spread(spread_thin, slice(WIDE, HALF), THIN), "zz", -1)

    def add_up(parts):
        total = parts[0].astype(F32)
        for part in parts[1:]:
            total = total + part.astype(F32)
        return total

    def scatter(parts, near_axes, far_axes):
        near = add_up(exchange(parts, near_axes, -1)).astype(BF16)
        far = [near[64 * d : 64 * (d + 1)] for d in range(4)]
        return add_up(exchange(far, far_axes, -1))

    wide_ham = scatter(reduce_tasks(wide_turned, wide_back, WIDE), "yz", "zx")
    thin_ham = scatter(reduce_tasks(thin_turned, thin_back, THIN), "xx", "yy")
    ham = jnp.concatenate([wide_ham, thin_ham], axis=1)
    ham_other = swap_core(ham[LOCAL:])
    mask = jnp.broadcast_to(
        block_mask.astype(F32)[:, None, :, None],
        (block_rows, block_edge, block_cols, block_edge),
    ).reshape(density.shape)
    scale = 1.0 / math.sqrt(16.0 * block_rows * NX * NC)
    ks_matrix, x0 = whole_call(
        lambda *refs: ham_kernel(scale, *refs),
        [core, ham[:LOCAL], ham_other, core_ham, mask],
        [(density.shape, F32), (density.shape, BF16)],
        0,
        2 << 20,
        scalars=1,
        scratch=[split_scratch(density.shape)],
    )

    left = gather_left(x0)
    shift = jnp.arange(NY * NZ, dtype=jnp.int32)
    outer, inner = shift // NZ, shift % NZ
    dy = jnp.where(c_at == 0, outer, inner)
    dz = jnp.where(c_at == 0, inner, outer)
    src = ((y_at - dy) % NY) * NZ + (z_at - dz) % NZ
    src_x, src_c = src // (2 * NC), (src // 2) % NC
    where = (((src_c ^ c_at) * NX + (x_at - src_x) % NX) * 2 + src % 2).astype(jnp.int32)
    x2 = panel_call(
        square_kernel, where, [*left, gather_right(x0), mask], x0.shape, BF16
    )
    sign_step = panel_call(
        lambda *refs: cube_kernel(scale, *refs),
        where,
        [*left, gather_right(x2), mask, x0],
        x0.shape,
        F32,
    )
    return (ks_matrix, sign_step)


def solution(mesh):
    placed = (
        P("row", "col"),
        P("row", "col"),
        P("row", "col"),
        P(("row", "col"), None, None),
        P(None, ("row", "col"), None, None),
        P(("row", "col"), None, None),
        P(("row", "col"), None),
    )
    return jax.shard_map(
        body,
        mesh=mesh,
        in_specs=placed,
        out_specs=(P("row", "col"), P("row", "col")),
        check_vma=False,
    )
```

```python
import math

import jax
import jax.numpy as jnp
from jax import lax
from jax.experimental import pallas as pl
from jax.experimental.pallas import tpu as pltpu
from jax.sharding import PartitionSpec as P

ATOMS = 16
block_edge = 64
NX, NC, NY, NZ = 4, 2, 4, 4
F32 = jnp.float32
BF16 = jnp.bfloat16


def move_x(v, d):
    pairs = [(x * NC + c, ((x + d) % NX) * NC + c) for x in range(NX) for c in range(NC)]
    return lax.ppermute(v, "row", pairs)


def swap_core(v):
    pairs = [(x * NC + c, x * NC + 1 - c) for x in range(NX) for c in range(NC)]
    return lax.ppermute(v, "row", pairs)


def place(x, c, y, z):
    return ((x % NX) * NC + c) * (NY * NZ) + (y % NY) * NZ + z % NZ


def move_two(v, d, axes):
    pairs = []
    for x in range(NX):
        for c in range(NC):
            for y in range(NY):
                for z in range(NZ):
                    step = {"x": 0, "y": 0, "z": 0}
                    step[axes[c]] = d
                    there = place(x + step["x"], c, y + step["y"], z + step["z"])
                    pairs.append((place(x, c, y, z), there))
    return lax.ppermute(v, ("row", "col"), pairs)


def low_half(shape):
    return lax.broadcasted_iota(jnp.int32, shape, 1) < block_edge


def trade_halves(first, second):
    low = low_half(first.shape)
    turned_first = pltpu.roll(first, block_edge, 1)
    turned_second = pltpu.roll(second, block_edge, 1)
    return jnp.where(low, first, turned_second), jnp.where(low, turned_first, second)


def blocks_to_matrix(blocks, matrix_ref, first_row, heights):
    groups, _, lanes = matrix_ref.shape
    half = heights * groups
    for tile in range(blocks.shape[1] // lanes):
        cut = slice(tile * lanes, (tile + 1) * lanes)
        rows = trade_halves(blocks[:half, cut], blocks[half:, cut])
        for odd in range(2):
            for group in range(groups):
                matrix_ref[group, pl.ds(first_row + 2 * tile + odd, heights, stride=block_edge), :] = (
                    rows[odd][group * heights : (group + 1) * heights]
                )


def matrix_to_blocks(matrix_ref, first_row, tiles, heights):
    groups = matrix_ref.shape[0]
    out = []
    for tile in range(tiles):
        rows = [
            jnp.concatenate(
                [
                    matrix_ref[group, pl.ds(first_row + 2 * tile + odd, heights, stride=block_edge), :]
                    for group in range(groups)
                ],
                axis=0,
            )
            for odd in range(2)
        ]
        out.append(jnp.concatenate(trade_halves(*rows), axis=0))
    return jnp.concatenate(out, axis=1)


def fold(matrix_ref, split_ref):
    groups, _, lanes = split_ref.shape
    for group in range(groups):
        split_ref[group] = matrix_ref[:, group * lanes : (group + 1) * lanes].astype(F32)


def split_scratch(shape):
    lanes = 2 * block_edge
    return pltpu.VMEM((shape[1] // lanes, shape[0], lanes), F32)


AREA = block_edge * block_edge
HALF = AREA // NC
WIDE = 1536
THIN = HALF - WIDE
HALF_ROWS = HALF // block_edge
CHUNK = 512
CHUNK_ROWS = CHUNK // block_edge
CHUNK_TILES = CHUNK // (2 * block_edge)
CAP = 8
LOCAL = 32
LISTED = 72
VMEM_SPEC = pl.BlockSpec(memory_space=pltpu.VMEM)
SMEM_SPEC = pl.BlockSpec(memory_space=pltpu.SMEM)


def whole_call(kernel, operands, shapes, flops, moved, scalars=0, scratch=()):
    return pl.pallas_call(
        kernel,
        in_specs=[SMEM_SPEC] * scalars + [VMEM_SPEC] * (len(operands) - scalars),
        out_specs=[VMEM_SPEC] * len(shapes),
        out_shape=[jax.ShapeDtypeStruct(shape, dtype) for shape, dtype in shapes],
        scratch_shapes=list(scratch),
        compiler_params=pltpu.CompilerParams(vmem_limit_bytes=40 << 20),
        cost_estimate=pl.CostEstimate(flops=flops, bytes_accessed=moved, transcendentals=0),
    )(*operands)


def split_kernel(core_ref, density_ref, mine_ref, other_ref, wide_ref):
    fold(density_ref, wide_ref)
    heights = density_ref.shape[0] // block_edge
    mine = core_ref[0] * HALF_ROWS
    for ref, first in ((mine_ref, mine), (other_ref, HALF_ROWS - mine)):
        for chunk in range(HALF // CHUNK):
            blocks = matrix_to_blocks(wide_ref, first + chunk * CHUNK_ROWS, CHUNK_TILES, heights)
            ref[:, chunk * CHUNK : (chunk + 1) * CHUNK] = blocks.astype(BF16)


def iota(shape, dim):
    return lax.broadcasted_iota(jnp.int32, shape, dim)


def lane_loop(width, body):
    step = 256
    whole = width // step

    @pl.loop(0, whole)
    def _(k):
        body(pl.ds(pl.multiple_of(k * step, step), step))

    if width % step:
        body(pl.ds(whole * step, width % step))


def select_kernel(*refs):
    pieces, find_ref = refs[0:4], refs[4]
    outs, turned_ref, names_ref, chosen_ref = refs[5:9], refs[9], refs[10], refs[11]
    tasks, span = 64 * CAP, 4 * NC * LOCAL
    lists = 4 * 8
    for step in range(4):
        for k in range(4):
            names_ref[step, 8 * k : 8 * k + 8] = pieces[step][k, 64:LISTED, :CHUNK].astype(F32)

    def target(shape, dim):
        spot = iota(shape, dim)
        block = ((spot & 7) << 2) + ((spot >> 2) & 2) + ((spot >> 4) & 1)
        return (((spot >> 5) << 6) + block).astype(F32)

    def offset(shape, dim):
        return (((iota(shape, dim) >> 3) & 7) << 6).astype(F32)

    @pl.loop(0, 4)
    def _(step):
        rows, at = iota((tasks, lists), 0), iota((tasks, lists), 1)
        want = (((rows >> 4) & 3) << 3) + (((rows >> 3) & 1) << 1)
        row, lane = iota((tasks, 64), 0), iota((tasks, 64), 1)
        keep = lane == ((row >> 6) << 3) + (row & 7)
        ones = jnp.ones((64, span), BF16)
        names = names_ref[step].astype(BF16)
        full = None
        for h in range(2):
            found = jnp.dot(names, find_ref[h], preferred_element_type=F32).astype(BF16)
            pick = (at == want + h).astype(BF16)
            term = jnp.dot(pick, found, preferred_element_type=F32)
            full = term if full is None else full + term
        kept = jnp.where(keep, full, 0.0).astype(BF16)
        value = jnp.dot(kept, ones, preferred_element_type=F32) + offset((tasks, span), 0)
        chosen_ref[step] = (value == target((1, span), 1)).astype(BF16)
        value = lax.dot_general(ones, kept, (((0,), (1,)), ((), ())), preferred_element_type=F32)
        value = value + offset((1, tasks), 1)
        turned_ref[step] = (value == target((span, tasks), 0)).astype(BF16)

    def body(lanes):
        for step in range(4):
            table = jnp.concatenate([pieces[step][k, 0:64, lanes] for k in range(4)], axis=0)
            got = jnp.dot(chosen_ref[step], table, preferred_element_type=F32).astype(BF16)
            for hop in range(4):
                for side in range(NC):
                    start = (hop * NC + side) * 64
                    outs[hop][side, step * 64 : (step + 1) * 64, lanes] = got[start : start + 64]

    lane_loop(outs[0].shape[2], body)


def select_tasks(pieces, find, width):
    shapes = [((NC, 256, width), BF16)] * 4 + [((4, 256, 512), BF16)]
    out = whole_call(
        select_kernel,
        [*pieces, find],
        shapes,
        2 * 4 * 512 * 256 * width,
        2 * 3200 * width,
        scratch=[pltpu.VMEM((4, 32, CHUNK), F32), pltpu.VMEM((4, 512, 256), BF16)],
    )
    return out[0:4], out[4]


def reduce_kernel(*refs):
    turned_ref, parts, outs = refs[0], refs[1:5], refs[5:9]

    def body(lanes):
        for step in range(4):
            tasks = jnp.concatenate(
                [
                    parts[hop][side, step * 64 : (step + 1) * 64, lanes]
                    for hop in range(4)
                    for side in range(NC)
                ],
                axis=0,
            )
            total = jnp.dot(turned_ref[step], tasks, preferred_element_type=F32)
            outs[step][:, lanes] = total.astype(BF16)

    lane_loop(outs[0].shape[1], body)


def reduce_tasks(turned, parts, width):
    return whole_call(
        reduce_kernel,
        [turned, *parts],
        [((256, width), BF16)] * 4,
        2 * 4 * 512 * 256 * width,
        2 * 3072 * width,
    )


def pair_kernel(hops, old, *refs):
    count = len(hops)
    wide_sel, thin_sel = refs[0], refs[1]
    wide, thin = refs[2 : 2 + count], refs[2 + count : 2 + 2 * count]
    before = refs[2 + 2 * count : 4 + 2 * count] if old else (None, None)
    outs = refs[-2:]
    for side in range(NC):
        start = 0
        for select, parts in ((wide_sel, wide), (thin_sel, thin)):

            def body(lanes, side=side, start=start, select=select, parts=parts):
                where = lanes.start + start
                if not isinstance(where, int):
                    where = pl.multiple_of(where, 128)
                where = pl.ds(where, lanes.size)
                total = before[side][:, where] if old else None
                for hop, part in zip(hops, parts):
                    term = jnp.dot(
                        select[side, :, hop * 256 : (hop + 1) * 256],
                        part[side, :, lanes],
                        preferred_element_type=F32,
                    )
                    total = term if total is None else total + term
                outs[side][:, where] = total.astype(outs[side].dtype)

            lane_loop(parts[0].shape[2], body)
            start += parts[0].shape[2]


def pair_sums(hops, wide_sel, thin_sel, wide, thin, before, dtype):
    operands = [wide_sel, thin_sel, *[wide[d] for d in hops], *[thin[d] for d in hops], *before]
    return whole_call(
        lambda *refs: pair_kernel(hops, len(before) > 0, *refs),
        operands,
        [((256, HALF), dtype)] * 2,
        len(hops) * 256 * 1024 * HALF,
        len(hops) * (3 << 20),
    )


def spread_kernel(select_ref, *refs):
    tables, outs = refs[0:2], refs[2:6]

    def body(lanes):
        for hop in range(4):
            for side in range(NC):
                outs[hop][side, :, lanes] = jnp.dot(
                    select_ref[side, hop * 256 : (hop + 1) * 256, :],
                    tables[side][:, lanes],
                    preferred_element_type=F32,
                ).astype(BF16)

    lane_loop(outs[0].shape[2], body)


def grid_kernel(
    core_ref, mine_ref, other_ref, basis_ref, vloc_ref, out_ref, out_other_ref, wide_ref, pair_ref, pot_ref
):
    mine = core_ref[0] * HALF_ROWS
    order, cells = basis_ref.shape
    tile, lanes_of_tile = 256, 2 * block_edge
    for ref, first in ((mine_ref, mine), (other_ref, HALF_ROWS - mine)):

        @pl.loop(0, HALF // CHUNK)
        def _(chunk):
            lanes = pl.ds(pl.multiple_of(chunk * CHUNK, CHUNK), CHUNK)
            sums = ref[:, lanes].astype(F32)
            blocks_to_matrix(sums, wide_ref, first + chunk * CHUNK_ROWS, ATOMS)

    for group in range(wide_ref.shape[0]):
        pair_ref[:, group * lanes_of_tile : (group + 1) * lanes_of_tile] = wide_ref[group].astype(BF16)

    @pl.loop(0, cells // tile)
    def _(step):
        lanes = pl.ds(pl.multiple_of(step * tile, tile), tile)
        vals = basis_ref[:, lanes]
        mixed = jnp.dot(pair_ref[...], vals, preferred_element_type=F32)
        wide = vals.astype(F32)
        rho = jnp.sum(wide * mixed, axis=0, keepdims=True)
        pot = vloc_ref[:, lanes] + 0.5 * rho / jnp.sqrt(1.0 + rho * rho)
        pot_ref[:, lanes] = (wide * pot).astype(BF16)

    @pl.loop(0, order // 256)
    def _(step):
        rows = pl.ds(pl.multiple_of(step * 256, 256), 256)
        part = lax.dot_general(
            pot_ref[...], basis_ref[rows, :], (((1,), (1,)), ((), ())), preferred_element_type=F32
        )
        for half in range(2):
            wide_ref[2 * step + half] = part[:, half * lanes_of_tile : (half + 1) * lanes_of_tile]

    for ref, first in ((out_ref, mine), (out_other_ref, HALF_ROWS - mine)):

        @pl.loop(0, HALF // CHUNK)
        def _(chunk):
            lanes = pl.ds(pl.multiple_of(chunk * CHUNK, CHUNK), CHUNK)
            blocks = matrix_to_blocks(wide_ref, first + chunk * CHUNK_ROWS, CHUNK_TILES, ATOMS)
            ref[:, lanes] = blocks.astype(BF16)


def grid_build(core, mine, other, basis_vals, v_loc):
    order, cells = basis_vals.shape
    return whole_call(
        grid_kernel,
        [core, mine, other, basis_vals, v_loc],
        [(mine.shape, BF16)] * 2,
        4 * order * order * cells,
        2 * order * cells + 8 * order * order,
        scalars=1,
        scratch=[
            split_scratch((order, order)),
            pltpu.VMEM((order, order), BF16),
            pltpu.VMEM((order, cells), BF16),
        ],
    )


def ham_kernel(scale, core_ref, mine_ref, other_ref, ham_ref, mask_ref, ks_ref, x0_ref, wide_ref):
    heights = ham_ref.shape[0] // block_edge
    mine = core_ref[0] * HALF_ROWS
    for ref, first in ((mine_ref, mine), (other_ref, HALF_ROWS - mine)):
        for chunk in range(HALF // CHUNK):
            sums = ref[:, chunk * CHUNK : (chunk + 1) * CHUNK]
            blocks_to_matrix(sums, wide_ref, first + chunk * CHUNK_ROWS, heights)
    for group in range(wide_ref.shape[0]):
        lanes = slice(group * 2 * block_edge, (group + 1) * 2 * block_edge)
        total = ham_ref[:, lanes] + wide_ref[group]
        ks_ref[:, lanes] = total
        x0_ref[:, lanes] = (mask_ref[:, lanes] * total * scale).astype(BF16)


def panel_sum(where_ref, left, right_ref):
    total = None
    for outer in range(4):
        for inner in range(4):
            piece = left[outer][inner]
            depth = piece.shape[1]
            start = pl.multiple_of(where_ref[outer * 4 + inner] * depth, depth)
            term = jnp.dot(piece, right_ref[pl.ds(start, depth), :], preferred_element_type=F32)
            total = term if total is None else total + term
    return total


def square_kernel(where_ref, *refs):
    right_ref, mask_ref, out_ref = refs[4:7]
    out_ref[...] = (mask_ref[...] * panel_sum(where_ref, refs[0:4], right_ref)).astype(BF16)


def cube_kernel(scale, where_ref, *refs):
    right_ref, mask_ref, x0_ref, out_ref = refs[4:8]
    x3 = mask_ref[...] * panel_sum(where_ref, refs[0:4], right_ref)
    out_ref[...] = (1.5 * x0_ref[...].astype(F32) - 0.5 * x3) / scale


def panel_call(kernel, where, operands, shape, dtype):
    vmem = pl.BlockSpec(memory_space=pltpu.VMEM)
    rows, cols = shape
    return pl.pallas_call(
        kernel,
        in_specs=[pl.BlockSpec(memory_space=pltpu.SMEM)] + [vmem] * len(operands),
        out_specs=vmem,
        out_shape=jax.ShapeDtypeStruct(shape, dtype),
        compiler_params=pltpu.CompilerParams(vmem_limit_bytes=40 << 20),
        cost_estimate=pl.CostEstimate(
            flops=2 * rows * cols * 4096, bytes_accessed=7 << 20, transcendentals=0
        ),
    )(where, *operands)


def gather_left(x0):
    near = [x0] + [None] * 3
    for d in (1, 3, 2):
        near[d] = move_two(x0, d, "zy")
    near = jnp.stack(near)
    far = [near] + [None] * 3
    for d in (1, 3, 2):
        far[d] = move_two(near, d, "yz")
    return far


def gather_right(tile):
    got = [move_x(tile, d) for d in (1, 3, 2)]
    other = swap_core(tile)
    same = jnp.concatenate([tile, got[0], got[2], got[1]])
    rest = swap_core(same[tile.shape[0]:])
    return jnp.concatenate([same, other, rest])


def body(density, core_ham, block_mask, send_blocks, task_atoms, basis, v_loc):
    block_rows = density.shape[0] // block_edge
    block_cols = density.shape[1] // block_edge
    device_count = send_blocks.shape[1]
    row, col = lax.axis_index("row"), lax.axis_index("col")
    x_at, c_at, y_at, z_at = row // NC, row % NC, col // NZ, col % NZ

    core = c_at.astype(jnp.int32).reshape(1)

    where_wide = [jnp.where(c_at == 0, p, q) for p, q in ((x_at, y_at), (y_at, z_at), (z_at, x_at))]
    where_thin = [z_at, x_at, y_at]

    def device_of(spots, cores, thin):
        one, two, three = [v % 4 for v in spots]
        if thin:
            return place(two, cores, three, one)
        return jnp.where(c_at == 0, place(one, cores, two, three), place(three, cores, one, two))

    slots = send_blocks[0]
    names = slots.reshape(2, CHUNK).astype(BF16)
    names = jnp.concatenate(
        [
            names,
            jnp.zeros((2, WIDE - CHUNK), BF16),
            names,
        ],
        axis=1,
    )
    mine, other = whole_call(
        split_kernel,
        [core, density],
        [((LOCAL, HALF), BF16)] * 2,
        0,
        1 << 20,
        scalars=1,
        scratch=[split_scratch(density.shape)],
    )
    sent = swap_core(jnp.concatenate([other, names, jnp.zeros((6, HALF), BF16)]))
    chip = jnp.concatenate(
        [mine, sent[:LOCAL], names, sent[LOCAL : LOCAL + 2], jnp.zeros((4, HALF), BF16)]
    )

    atoms = task_atoms[:, 0]
    pair = (atoms[1] % 2) * (ATOMS * ATOMS // 2) + (atoms[1] // 2) * ATOMS + atoms[0]
    pair = pair.astype(BF16)
    pair_other = swap_core(pair)

    def spread_out(v, axes):
        out = [v] + [None] * 3
        for d in (1, 3, 2):
            out[d] = move_two(v, d, axes)
        return out

    wide_near = spread_out(chip[:, :WIDE], "zx")
    thin_near = spread_out(chip[:, WIDE:], "yy")
    wide_near, thin_near, pair_other = lax.optimization_barrier((wide_near, thin_near, pair_other))
    wide_pieces = spread_out(jnp.stack(wide_near), "yz")
    thin_pieces = spread_out(jnp.stack(thin_near), "xx")
    wide_pieces, thin_pieces = lax.optimization_barrier((wide_pieces, thin_pieces))

    pairs = jnp.concatenate([pair, pair_other], axis=1)
    pair_ids = jnp.arange(ATOMS * ATOMS, dtype=jnp.int32).astype(F32)

    def plans(spots, thin):
        j = jnp.arange(device_count, dtype=jnp.int32)
        away = (j // 32, (j // 8) % 4, (j // 2) % 4)
        owner = device_of([p - d for p, d in zip(spots, away)], c_at ^ (j % 2), thin)
        order = (owner[:, None] == j[None, :]).astype(BF16)
        moved = jnp.dot(order, pairs, preferred_element_type=F32)
        moved = moved.reshape(device_count, NC, CAP).transpose(1, 0, 2).reshape(NC, -1)
        gather_sel = (pair_ids[None, :, None] == moved[:, None, :]).astype(BF16)
        spread_sel = (moved[:, :, None] == pair_ids[None, None, :]).astype(BF16)
        k = jnp.arange(64, dtype=jnp.int32)
        dest = device_of(
            [spots[0] + k // 16, spots[1] + 0 * k, spots[2] + 0 * k], c_at ^ ((k // 8) % 2), thin
        )
        target = dest * CAP + k % CAP
        line = jnp.arange(2 * CHUNK, dtype=jnp.int32).reshape(2, CHUNK, 1)
        find = (line == target[None, None, :]).astype(BF16)
        return gather_sel, spread_sel, find

    gather_wide, spread_wide, find_wide = plans(where_wide, False)
    gather_thin, spread_thin, find_thin = plans(where_thin, True)

    def exchange(parts, axes, sign):
        out = [parts[0]] + [None] * 3
        for d in (1, 3, 2):
            out[d] = move_two(parts[d], sign * d, axes)
        return out

    wide_tasks, wide_turned = select_tasks(wide_pieces, find_wide, WIDE)
    wide_tasks = exchange(wide_tasks, "xy", 1)
    thin_tasks, thin_turned = select_tasks(thin_pieces, find_thin, THIN)
    thin_tasks = exchange(thin_tasks, "zz", 1)
    sums = pair_sums((0, 1, 3), gather_wide, gather_thin, wide_tasks, thin_tasks, [], F32)
    sum_mine, sum_other = pair_sums(
        (2,), gather_wide, gather_thin, wide_tasks, thin_tasks, sums, BF16
    )
    k_mine, k_other = grid_build(core, sum_mine, swap_core(sum_other), basis[0], v_loc)
    k_swapped = swap_core(k_other)

    def spread(select, lanes, width):
        return whole_call(
            spread_kernel,
            [select, k_mine[:, lanes], k_swapped[:, lanes]],
            [((NC, 256, width), BF16)] * 4,
            4 * 256 * 1024 * width,
            2 * 2600 * width,
        )

    wide_back = exchange(spread(spread_wide, slice(0, WIDE), WIDE), "xy", -1)
    thin_back = exchange(spread(spread_thin, slice(WIDE, HALF), THIN), "zz", -1)

    def add_up(parts):
        total = parts[0].astype(F32)
        for part in parts[1:]:
            total = total + part.astype(F32)
        return total

    def scatter(parts, near_axes, far_axes):
        near = add_up(exchange(parts, near_axes, -1)).astype(BF16)
        far = [near[64 * d : 64 * (d + 1)] for d in range(4)]
        return add_up(exchange(far, far_axes, -1))

    wide_parts = reduce_tasks(wide_turned, wide_back, WIDE)
    wide_parts, thin_turned = lax.optimization_barrier((wide_parts, thin_turned))
    wide_ham = scatter(wide_parts, "yz", "zx")
    thin_ham = scatter(reduce_tasks(thin_turned, thin_back, THIN), "xx", "yy")
    ham = jnp.concatenate([wide_ham, thin_ham], axis=1)
    ham_other = swap_core(ham[LOCAL:])
    mask = jnp.broadcast_to(
        block_mask.astype(F32)[:, None, :, None],
        (block_rows, block_edge, block_cols, block_edge),
    ).reshape(density.shape)
    scale = 1.0 / math.sqrt(16.0 * block_rows * NX * NC)
    ks_matrix, x0 = whole_call(
        lambda *refs: ham_kernel(scale, *refs),
        [core, ham[:LOCAL], ham_other, core_ham, mask],
        [(density.shape, F32), (density.shape, BF16)],
        0,
        2 << 20,
        scalars=1,
        scratch=[split_scratch(density.shape)],
    )

    left = gather_left(x0)
    shift = jnp.arange(NY * NZ, dtype=jnp.int32)
    outer, inner = shift // NZ, shift % NZ
    dy = jnp.where(c_at == 0, outer, inner)
    dz = jnp.where(c_at == 0, inner, outer)
    src = ((y_at - dy) % NY) * NZ + (z_at - dz) % NZ
    src_x, src_c = src // (2 * NC), (src // 2) % NC
    where = (((src_c ^ c_at) * NX + (x_at - src_x) % NX) * 2 + src % 2).astype(jnp.int32)
    x2 = panel_call(
        square_kernel, where, [*left, gather_right(x0), mask], x0.shape, BF16
    )
    sign_step = panel_call(
        lambda *refs: cube_kernel(scale, *refs),
        where,
        [*left, gather_right(x2), mask, x0],
        x0.shape,
        F32,
    )
    return (ks_matrix, sign_step)


def solution(mesh):
    placed = (
        P("row", "col"),
        P("row", "col"),
        P("row", "col"),
        P(("row", "col"), None, None),
        P(None, ("row", "col"), None, None),
        P(("row", "col"), None, None),
        P(("row", "col"), None),
    )
    return jax.shard_map(
        body,
        mesh=mesh,
        in_specs=placed,
        out_specs=(P("row", "col"), P("row", "col")),
        check_vma=False,
    )
```

```python
import math

import jax
import jax.numpy as jnp
from jax import lax
from jax.experimental import pallas as pl
from jax.experimental.pallas import tpu as pltpu
from jax.sharding import PartitionSpec as P

ATOMS = 16
block_edge = 64
NX, NC, NY, NZ = 4, 2, 4, 4
F32 = jnp.float32
BF16 = jnp.bfloat16


def move_x(v, d):
    pairs = [(x * NC + c, ((x + d) % NX) * NC + c) for x in range(NX) for c in range(NC)]
    return lax.ppermute(v, "row", pairs)


def swap_core(v):
    pairs = [(x * NC + c, x * NC + 1 - c) for x in range(NX) for c in range(NC)]
    return lax.ppermute(v, "row", pairs)


def place(x, c, y, z):
    return ((x % NX) * NC + c) * (NY * NZ) + (y % NY) * NZ + z % NZ


def move_two(v, d, axes):
    pairs = []
    for x in range(NX):
        for c in range(NC):
            for y in range(NY):
                for z in range(NZ):
                    step = {"x": 0, "y": 0, "z": 0}
                    step[axes[c]] = d
                    there = place(x + step["x"], c, y + step["y"], z + step["z"])
                    pairs.append((place(x, c, y, z), there))
    return lax.ppermute(v, ("row", "col"), pairs)


def low_half(shape):
    return lax.broadcasted_iota(jnp.int32, shape, 1) < block_edge


def trade_halves(first, second):
    low = low_half(first.shape)
    turned_first = pltpu.roll(first, block_edge, 1)
    turned_second = pltpu.roll(second, block_edge, 1)
    return jnp.where(low, first, turned_second), jnp.where(low, turned_first, second)


def blocks_to_matrix(blocks, matrix_ref, first_row, heights):
    groups, _, lanes = matrix_ref.shape
    half = heights * groups
    for tile in range(blocks.shape[1] // lanes):
        cut = slice(tile * lanes, (tile + 1) * lanes)
        rows = trade_halves(blocks[:half, cut], blocks[half:, cut])
        for odd in range(2):
            for group in range(groups):
                matrix_ref[group, pl.ds(first_row + 2 * tile + odd, heights, stride=block_edge), :] = (
                    rows[odd][group * heights : (group + 1) * heights]
                )


def matrix_to_blocks(matrix_ref, first_row, tiles, heights):
    groups = matrix_ref.shape[0]
    out = []
    for tile in range(tiles):
        rows = [
            jnp.concatenate(
                [
                    matrix_ref[group, pl.ds(first_row + 2 * tile + odd, heights, stride=block_edge), :]
                    for group in range(groups)
                ],
                axis=0,
            )
            for odd in range(2)
        ]
        out.append(jnp.concatenate(trade_halves(*rows), axis=0))
    return jnp.concatenate(out, axis=1)


def fold(matrix_ref, split_ref):
    groups, _, lanes = split_ref.shape
    for group in range(groups):
        split_ref[group] = matrix_ref[:, group * lanes : (group + 1) * lanes].astype(F32)


def split_scratch(shape):
    lanes = 2 * block_edge
    return pltpu.VMEM((shape[1] // lanes, shape[0], lanes), F32)


AREA = block_edge * block_edge
HALF = AREA // NC
WIDE = 1536
THIN = HALF - WIDE
WIDE_BACK = 1408
HALF_ROWS = HALF // block_edge
CHUNK = 512
CHUNK_ROWS = CHUNK // block_edge
CHUNK_TILES = CHUNK // (2 * block_edge)
CAP = 8
LOCAL = 32
LISTED = 72
VMEM_SPEC = pl.BlockSpec(memory_space=pltpu.VMEM)
SMEM_SPEC = pl.BlockSpec(memory_space=pltpu.SMEM)


def whole_call(kernel, operands, shapes, flops, moved, scalars=0, scratch=()):
    return pl.pallas_call(
        kernel,
        in_specs=[SMEM_SPEC] * scalars + [VMEM_SPEC] * (len(operands) - scalars),
        out_specs=[VMEM_SPEC] * len(shapes),
        out_shape=[jax.ShapeDtypeStruct(shape, dtype) for shape, dtype in shapes],
        scratch_shapes=list(scratch),
        compiler_params=pltpu.CompilerParams(vmem_limit_bytes=40 << 20),
        cost_estimate=pl.CostEstimate(flops=flops, bytes_accessed=moved, transcendentals=0),
    )(*operands)


def split_kernel(core_ref, density_ref, mine_ref, other_ref, wide_ref):
    fold(density_ref, wide_ref)
    heights = density_ref.shape[0] // block_edge
    mine = core_ref[0] * HALF_ROWS
    for ref, first in ((mine_ref, mine), (other_ref, HALF_ROWS - mine)):
        for chunk in range(HALF // CHUNK):
            blocks = matrix_to_blocks(wide_ref, first + chunk * CHUNK_ROWS, CHUNK_TILES, heights)
            ref[:, chunk * CHUNK : (chunk + 1) * CHUNK] = blocks.astype(BF16)


def iota(shape, dim):
    return lax.broadcasted_iota(jnp.int32, shape, dim)


def lane_loop(width, body):
    step = 256
    whole = width // step

    @pl.loop(0, whole)
    def _(k):
        body(pl.ds(pl.multiple_of(k * step, step), step))

    if width % step:
        body(pl.ds(whole * step, width % step))


def select_kernel(*refs):
    pieces, lists_of, find_ref = refs[0:4], refs[4:8], refs[8]
    outs, turned_ref, names_ref, chosen_ref = refs[9:13], refs[13], refs[14], refs[15]
    tasks, span = 64 * CAP, 4 * NC * LOCAL
    lists = 4 * 8

    def target(shape, dim):
        spot = iota(shape, dim)
        block = ((spot & 7) << 2) + ((spot >> 2) & 2) + ((spot >> 4) & 1)
        return (((spot >> 5) << 6) + block).astype(F32)

    def offset(shape, dim):
        return (((iota(shape, dim) >> 3) & 7) << 6).astype(F32)

    @pl.when(pl.program_id(0) == 0)
    def _():
        for step in range(4):
            for k in range(4):
                names_ref[step, 8 * k : 8 * k + 8] = lists_of[step][k].astype(F32)

        @pl.loop(0, 4)
        def _(step):
            rows, at = iota((tasks, lists), 0), iota((tasks, lists), 1)
            want = (((rows >> 4) & 3) << 3) + (((rows >> 3) & 1) << 1)
            row, lane = iota((tasks, 64), 0), iota((tasks, 64), 1)
            keep = lane == ((row >> 6) << 3) + (row & 7)
            ones = jnp.ones((64, span), BF16)
            names = names_ref[step].astype(BF16)
            full = None
            for h in range(2):
                found = jnp.dot(names, find_ref[h], preferred_element_type=F32).astype(BF16)
                pick = (at == want + h).astype(BF16)
                term = jnp.dot(pick, found, preferred_element_type=F32)
                full = term if full is None else full + term
            kept = jnp.where(keep, full, 0.0).astype(BF16)
            value = jnp.dot(kept, ones, preferred_element_type=F32) + offset((tasks, span), 0)
            chosen_ref[step] = (value == target((1, span), 1)).astype(BF16)
            value = lax.dot_general(ones, kept, (((0,), (1,)), ((), ())), preferred_element_type=F32)
            value = value + offset((1, tasks), 1)
            turned_ref[step] = (value == target((span, tasks), 0)).astype(BF16)

    for step in range(4):
        table = jnp.concatenate([pieces[step][k] for k in range(4)], axis=0)
        got = jnp.dot(chosen_ref[step], table, preferred_element_type=F32).astype(BF16)
        for hop in range(4):
            for side in range(NC):
                start = (hop * NC + side) * 64
                outs[hop][side, step * 64 : (step + 1) * 64, :] = got[start : start + 64]


def select_tasks(pieces, find, width, chunk):
    part = pl.BlockSpec((4, 64, chunk), lambda g: (0, 0, g))
    names = pl.BlockSpec((4, LISTED - 64, CHUNK), lambda g: (0, 64 // (LISTED - 64), 0))
    out = pl.pallas_call(
        select_kernel,
        grid=(width // chunk,),
        in_specs=[part] * 4 + [names] * 4 + [pl.BlockSpec(find.shape, lambda g: (0, 0, 0))],
        out_specs=[pl.BlockSpec((NC, 256, chunk), lambda g: (0, 0, g))] * 4
        + [pl.BlockSpec((4, 256, 512), lambda g: (0, 0, 0))],
        out_shape=[jax.ShapeDtypeStruct((NC, 256, width), BF16)] * 4
        + [jax.ShapeDtypeStruct((4, 256, 512), BF16)],
        scratch_shapes=[pltpu.VMEM((4, 32, CHUNK), F32), pltpu.VMEM((4, 512, 256), BF16)],
        compiler_params=pltpu.CompilerParams(vmem_limit_bytes=40 << 20),
        cost_estimate=pl.CostEstimate(
            flops=2 * 4 * 512 * 256 * width, bytes_accessed=2 * 3200 * width, transcendentals=0
        ),
    )(*pieces, *pieces, find)
    return out[0:4], out[4]


def reduce_kernel(*refs):
    turned_ref, parts, outs = refs[0], refs[1:5], refs[5:9]

    def body(lanes):
        for step in range(4):
            tasks = jnp.concatenate(
                [
                    parts[hop][side, step * 64 : (step + 1) * 64, lanes]
                    for hop in range(4)
                    for side in range(NC)
                ],
                axis=0,
            )
            total = jnp.dot(turned_ref[step], tasks, preferred_element_type=F32)
            outs[step][:, lanes] = total.astype(BF16)

    lane_loop(outs[0].shape[1], body)


def reduce_tasks(turned, parts, width):
    return whole_call(
        reduce_kernel,
        [turned, *parts],
        [((256, width), BF16)] * 4,
        2 * 4 * 512 * 256 * width,
        2 * 3072 * width,
    )


def pair_kernel(first, *refs):
    wide_sel, thin_sel = refs[0], refs[1]
    wide, thin, outs = refs[2:6], refs[6:10], refs[10:12]

    def add(select, parts):
        for side in range(NC):
            tasks = jnp.concatenate([part[side] for part in parts], axis=0)
            total = jnp.dot(select[side], tasks, preferred_element_type=F32)
            outs[side][...] = total.astype(BF16)

    @pl.when(pl.program_id(0) < first)
    def _():
        add(wide_sel, wide)

    @pl.when(pl.program_id(0) >= first)
    def _():
        add(thin_sel, thin)


def pair_sums(wide_sel, thin_sel, wide, thin):
    chunk = 256
    first = WIDE // chunk
    sel = pl.BlockSpec(wide_sel.shape, lambda g: (0, 0, 0))
    wide_spec = pl.BlockSpec((NC, 256, chunk), lambda g: (0, 0, jnp.minimum(g, first - 1)))
    thin_spec = pl.BlockSpec((NC, 256, chunk), lambda g: (0, 0, jnp.maximum(g - first, 0)))
    return pl.pallas_call(
        lambda *refs: pair_kernel(first, *refs),
        grid=(HALF // chunk,),
        in_specs=[sel, sel] + [wide_spec] * 4 + [thin_spec] * 4,
        out_specs=[pl.BlockSpec((256, chunk), lambda g: (0, g))] * 2,
        out_shape=[jax.ShapeDtypeStruct((256, HALF), BF16)] * 2,
        compiler_params=pltpu.CompilerParams(vmem_limit_bytes=40 << 20),
        cost_estimate=pl.CostEstimate(
            flops=4 * 256 * 1024 * HALF, bytes_accessed=12 << 20, transcendentals=0
        ),
    )(wide_sel, thin_sel, *wide, *thin)


def spread_kernel(select_ref, *refs):
    tables, outs = refs[0:2], refs[2:6]

    def body(lanes):
        for hop in range(4):
            for side in range(NC):
                outs[hop][side, :, lanes] = jnp.dot(
                    select_ref[side, hop * 256 : (hop + 1) * 256, :],
                    tables[side][:, lanes],
                    preferred_element_type=F32,
                ).astype(BF16)

    lane_loop(outs[0].shape[2], body)


def grid_kernel(
    core_ref, mine_ref, other_ref, basis_ref, vloc_ref, out_ref, out_other_ref, wide_ref, pair_ref, pot_ref
):
    mine = core_ref[0] * HALF_ROWS
    order, cells = basis_ref.shape
    tile, lanes_of_tile = 256, 2 * block_edge
    for ref, first in ((mine_ref, mine), (other_ref, HALF_ROWS - mine)):

        @pl.loop(0, HALF // CHUNK)
        def _(chunk):
            lanes = pl.ds(pl.multiple_of(chunk * CHUNK, CHUNK), CHUNK)
            sums = ref[:, lanes].astype(F32)
            blocks_to_matrix(sums, wide_ref, first + chunk * CHUNK_ROWS, ATOMS)

    for group in range(wide_ref.shape[0]):
        pair_ref[:, group * lanes_of_tile : (group + 1) * lanes_of_tile] = wide_ref[group].astype(BF16)

    @pl.loop(0, cells // tile)
    def _(step):
        lanes = pl.ds(pl.multiple_of(step * tile, tile), tile)
        vals = basis_ref[:, lanes]
        mixed = jnp.dot(pair_ref[...], vals, preferred_element_type=F32)
        wide = vals.astype(F32)
        rho = jnp.sum(wide * mixed, axis=0, keepdims=True)
        pot = vloc_ref[:, lanes] + 0.5 * rho / jnp.sqrt(1.0 + rho * rho)
        pot_ref[:, lanes] = (wide * pot).astype(BF16)

    @pl.loop(0, order // 256)
    def _(step):
        rows = pl.ds(pl.multiple_of(step * 256, 256), 256)
        part = lax.dot_general(
            pot_ref[...], basis_ref[rows, :], (((1,), (1,)), ((), ())), preferred_element_type=F32
        )
        for half in range(2):
            wide_ref[2 * step + half] = part[:, half * lanes_of_tile : (half + 1) * lanes_of_tile]

    for ref, first in ((out_ref, mine), (out_other_ref, HALF_ROWS - mine)):

        @pl.loop(0, HALF // CHUNK)
        def _(chunk):
            lanes = pl.ds(pl.multiple_of(chunk * CHUNK, CHUNK), CHUNK)
            blocks = matrix_to_blocks(wide_ref, first + chunk * CHUNK_ROWS, CHUNK_TILES, ATOMS)
            ref[:, lanes] = blocks.astype(BF16)


def grid_build(core, mine, other, basis_vals, v_loc):
    order, cells = basis_vals.shape
    return whole_call(
        grid_kernel,
        [core, mine, other, basis_vals, v_loc],
        [(mine.shape, BF16)] * 2,
        4 * order * order * cells,
        2 * order * cells + 8 * order * order,
        scalars=1,
        scratch=[
            split_scratch((order, order)),
            pltpu.VMEM((order, order), BF16),
            pltpu.VMEM((order, cells), BF16),
        ],
    )


def ham_kernel(
    scale, core_ref, mine_ref, other_ref, ham_ref, block_ref, ks_ref, x0_ref, mask_ref, wide_ref
):
    heights = ham_ref.shape[0] // block_edge
    mine = core_ref[0] * HALF_ROWS
    for ref, first in ((mine_ref, mine), (other_ref, HALF_ROWS - mine)):
        for chunk in range(HALF // CHUNK):
            sums = ref[:, chunk * CHUNK : (chunk + 1) * CHUNK]
            blocks_to_matrix(sums, wide_ref, first + chunk * CHUNK_ROWS, heights)
    rows, cols = ham_ref.shape
    down = (iota((rows, rows // block_edge), 0) >> 6 == iota((rows, rows // block_edge), 1)).astype(BF16)
    over = (iota((cols // block_edge, cols), 1) >> 6 == iota((cols // block_edge, cols), 0)).astype(BF16)
    kept = block_ref[...].astype(F32).astype(BF16)
    kept = jnp.dot(down, kept, preferred_element_type=F32).astype(BF16)
    mask_ref[...] = jnp.dot(kept, over, preferred_element_type=F32)
    for group in range(wide_ref.shape[0]):
        lanes = slice(group * 2 * block_edge, (group + 1) * 2 * block_edge)
        total = ham_ref[:, lanes] + wide_ref[group]
        ks_ref[:, lanes] = total
        x0_ref[:, lanes] = (mask_ref[:, lanes] * total * scale).astype(BF16)


def panel_sum(where_ref, left, right_ref, total_ref):
    total_ref[...] = jnp.zeros_like(total_ref)
    for outer in range(4):

        @pl.loop(0, 4)
        def _(inner):
            piece = left[outer][inner]
            depth = piece.shape[1]
            start = pl.multiple_of(where_ref[outer * 4 + inner] * depth, depth)
            total_ref[...] += jnp.dot(
                piece, right_ref[pl.ds(start, depth), :], preferred_element_type=F32
            )

    return total_ref[...]


def square_kernel(where_ref, *refs):
    right_ref, mask_ref, out_ref, total_ref = refs[4:8]
    total = panel_sum(where_ref, refs[0:4], right_ref, total_ref)
    out_ref[...] = (mask_ref[...] * total).astype(BF16)


def cube_kernel(scale, where_ref, *refs):
    right_ref, mask_ref, x0_ref, out_ref, total_ref = refs[4:9]
    x3 = mask_ref[...] * panel_sum(where_ref, refs[0:4], right_ref, total_ref)
    out_ref[...] = (1.5 * x0_ref[...].astype(F32) - 0.5 * x3) / scale


def panel_call(kernel, where, operands, shape, dtype):
    vmem = pl.BlockSpec(memory_space=pltpu.VMEM)
    rows, cols = shape
    return pl.pallas_call(
        kernel,
        in_specs=[pl.BlockSpec(memory_space=pltpu.SMEM)] + [vmem] * len(operands),
        out_specs=vmem,
        out_shape=jax.ShapeDtypeStruct(shape, dtype),
        scratch_shapes=[pltpu.VMEM(shape, F32)],
        compiler_params=pltpu.CompilerParams(vmem_limit_bytes=40 << 20),
        cost_estimate=pl.CostEstimate(
            flops=2 * rows * cols * 4096, bytes_accessed=7 << 20, transcendentals=0
        ),
    )(where, *operands)


def gather_left(x0):
    near = [x0] + [None] * 3
    for d in (1, 3, 2):
        near[d] = move_two(x0, d, "zy")
    near = jnp.stack(near)
    far = [near] + [None] * 3
    for d in (1, 3, 2):
        far[d] = move_two(near, d, "yz")
    return far


def gather_right(tile):
    got = [move_x(tile, d) for d in (1, 3, 2)]
    other = swap_core(tile)
    same = jnp.concatenate([tile, got[0], got[2], got[1]])
    rest = swap_core(same[tile.shape[0]:])
    return jnp.concatenate([same, other, rest])


def body(density, core_ham, block_mask, send_blocks, task_atoms, basis, v_loc):
    block_rows = density.shape[0] // block_edge
    block_cols = density.shape[1] // block_edge
    device_count = send_blocks.shape[1]
    row, col = lax.axis_index("row"), lax.axis_index("col")
    x_at, c_at, y_at, z_at = row // NC, row % NC, col // NZ, col % NZ

    core = c_at.astype(jnp.int32).reshape(1)

    where_wide = [jnp.where(c_at == 0, p, q) for p, q in ((x_at, y_at), (y_at, z_at), (z_at, x_at))]
    where_thin = [z_at, x_at, y_at]

    def device_of(spots, cores, thin):
        one, two, three = [v % 4 for v in spots]
        if thin:
            return place(two, cores, three, one)
        return jnp.where(c_at == 0, place(one, cores, two, three), place(three, cores, one, two))

    slots = send_blocks[0]
    names = slots.reshape(2, CHUNK).astype(BF16)
    names = jnp.concatenate(
        [
            names,
            jnp.zeros((2, WIDE - CHUNK), BF16),
            names,
        ],
        axis=1,
    )
    mine, other = whole_call(
        split_kernel,
        [core, density],
        [((LOCAL, HALF), BF16)] * 2,
        0,
        1 << 20,
        scalars=1,
        scratch=[split_scratch(density.shape)],
    )
    sent = swap_core(jnp.concatenate([other, names, jnp.zeros((6, HALF), BF16)]))
    chip = jnp.concatenate(
        [mine, sent[:LOCAL], names, sent[LOCAL : LOCAL + 2], jnp.zeros((4, HALF), BF16)]
    )

    atoms = task_atoms[:, 0]
    pair = (atoms[1] % 2) * (ATOMS * ATOMS // 2) + (atoms[1] // 2) * ATOMS + atoms[0]
    pair = pair.astype(BF16)
    pair_other = swap_core(pair)

    def spread_out(v, axes):
        out = [v] + [None] * 3
        for d in (1, 3, 2):
            out[d] = move_two(v, d, axes)
        return out

    wide_near = spread_out(chip[:, :WIDE], "zx")
    thin_near = spread_out(chip[:, WIDE:], "yy")
    wide_near, thin_near, pair_other = lax.optimization_barrier((wide_near, thin_near, pair_other))
    wide_pieces = spread_out(jnp.stack(wide_near), "yz")
    thin_pieces = spread_out(jnp.stack(thin_near), "xx")
    wide_pieces, thin_pieces = lax.optimization_barrier((wide_pieces, thin_pieces))

    pairs = jnp.concatenate([pair, pair_other], axis=1)
    pair_ids = jnp.arange(ATOMS * ATOMS, dtype=jnp.int32).astype(F32)

    def plans(spots, thin):
        j = jnp.arange(device_count, dtype=jnp.int32)
        away = (j // 32, (j // 8) % 4, (j // 2) % 4)
        owner = device_of([p - d for p, d in zip(spots, away)], c_at ^ (j % 2), thin)
        order = (owner[:, None] == j[None, :]).astype(BF16)
        moved = jnp.dot(order, pairs, preferred_element_type=F32)
        moved = moved.reshape(device_count, NC, CAP).transpose(1, 0, 2).reshape(NC, -1)
        gather_sel = (pair_ids[None, :, None] == moved[:, None, :]).astype(BF16)
        spread_sel = (moved[:, :, None] == pair_ids[None, None, :]).astype(BF16)
        k = jnp.arange(64, dtype=jnp.int32)
        dest = device_of(
            [spots[0] + k // 16, spots[1] + 0 * k, spots[2] + 0 * k], c_at ^ ((k // 8) % 2), thin
        )
        target = dest * CAP + k % CAP
        line = jnp.arange(2 * CHUNK, dtype=jnp.int32).reshape(2, CHUNK, 1)
        find = (line == target[None, None, :]).astype(BF16)
        return gather_sel, spread_sel, find

    gather_wide, spread_wide, find_wide = plans(where_wide, False)
    gather_thin, spread_thin, find_thin = plans(where_thin, True)

    def exchange(parts, axes, sign):
        out = [parts[0]] + [None] * 3
        for d in (1, 3, 2):
            out[d] = move_two(parts[d], sign * d, axes)
        return out

    wide_tasks, wide_turned = select_tasks(wide_pieces, find_wide, WIDE, 512)
    wide_tasks = exchange(wide_tasks, "xy", 1)
    thin_tasks, thin_turned = select_tasks(thin_pieces, find_thin, THIN, 256)
    thin_tasks = exchange(thin_tasks, "zz", 1)
    sum_mine, sum_other = pair_sums(gather_wide, gather_thin, wide_tasks, thin_tasks)
    k_mine, k_other = grid_build(core, sum_mine, swap_core(sum_other), basis[0], v_loc)
    k_swapped = swap_core(k_other)

    def spread(select, lanes, width):
        return whole_call(
            spread_kernel,
            [select, k_mine[:, lanes], k_swapped[:, lanes]],
            [((NC, 256, width), BF16)] * 4,
            4 * 256 * 1024 * width,
            2 * 2600 * width,
        )

    wide_back = exchange(spread(spread_wide, slice(0, WIDE_BACK), WIDE_BACK), "xy", -1)
    thin_back = exchange(spread(spread_thin, slice(WIDE_BACK, HALF), HALF - WIDE_BACK), "zz", -1)

    def add_up(parts):
        total = parts[0].astype(F32)
        for part in parts[1:]:
            total = total + part.astype(F32)
        return total

    def scatter(parts, near_axes, far_axes):
        near = add_up(exchange(parts, near_axes, -1)).astype(BF16)
        far = [near[64 * d : 64 * (d + 1)] for d in range(4)]
        return add_up(exchange(far, far_axes, -1))

    wide_parts = reduce_tasks(wide_turned, wide_back, WIDE_BACK)
    wide_parts, thin_turned = lax.optimization_barrier((wide_parts, thin_turned))
    wide_ham = scatter(wide_parts, "yz", "zx")
    thin_ham = scatter(reduce_tasks(thin_turned, thin_back, HALF - WIDE_BACK), "xx", "yy")
    ham = jnp.concatenate([wide_ham, thin_ham], axis=1)
    ham_other = swap_core(ham[LOCAL:])
    scale = 1.0 / math.sqrt(16.0 * block_rows * NX * NC)
    ks_matrix, x0, mask = whole_call(
        lambda *refs: ham_kernel(scale, *refs),
        [core, ham[:LOCAL], ham_other, core_ham, block_mask],
        [(density.shape, F32), (density.shape, BF16), (density.shape, F32)],
        0,
        2 << 20,
        scalars=1,
        scratch=[split_scratch(density.shape)],
    )

    left = gather_left(x0)
    shift = jnp.arange(NY * NZ, dtype=jnp.int32)
    outer, inner = shift // NZ, shift % NZ
    dy = jnp.where(c_at == 0, outer, inner)
    dz = jnp.where(c_at == 0, inner, outer)
    src = ((y_at - dy) % NY) * NZ + (z_at - dz) % NZ
    src_x, src_c = src // (2 * NC), (src // 2) % NC
    where = (((src_c ^ c_at) * NX + (x_at - src_x) % NX) * 2 + src % 2).astype(jnp.int32)
    x2 = panel_call(
        square_kernel, where, [*left, gather_right(x0), mask], x0.shape, BF16
    )
    sign_step = panel_call(
        lambda *refs: cube_kernel(scale, *refs),
        where,
        [*left, gather_right(x2), mask, x0],
        x0.shape,
        F32,
    )
    return (ks_matrix, sign_step)


def solution(mesh):
    placed = (
        P("row", "col"),
        P("row", "col"),
        P("row", "col"),
        P(("row", "col"), None, None),
        P(None, ("row", "col"), None, None),
        P(("row", "col"), None, None),
        P(("row", "col"), None),
    )
    return jax.shard_map(
        body,
        mesh=mesh,
        in_specs=placed,
        out_specs=(P("row", "col"), P("row", "col")),
        check_vma=False,
    )
```

```python
import math

import jax
import jax.numpy as jnp
from jax import lax
from jax.experimental import pallas as pl
from jax.experimental.pallas import tpu as pltpu
from jax.sharding import PartitionSpec as P

ATOMS = 16
block_edge = 64
NX, NC, NY, NZ = 4, 2, 4, 4
F32 = jnp.float32
BF16 = jnp.bfloat16


def move_x(v, d):
    pairs = [(x * NC + c, ((x + d) % NX) * NC + c) for x in range(NX) for c in range(NC)]
    return lax.ppermute(v, "row", pairs)


def swap_core(v):
    pairs = [(x * NC + c, x * NC + 1 - c) for x in range(NX) for c in range(NC)]
    return lax.ppermute(v, "row", pairs)


def place(x, c, y, z):
    return ((x % NX) * NC + c) * (NY * NZ) + (y % NY) * NZ + z % NZ


def move_two(v, d, axes):
    pairs = []
    for x in range(NX):
        for c in range(NC):
            for y in range(NY):
                for z in range(NZ):
                    step = {"x": 0, "y": 0, "z": 0}
                    step[axes[c]] = d
                    there = place(x + step["x"], c, y + step["y"], z + step["z"])
                    pairs.append((place(x, c, y, z), there))
    return lax.ppermute(v, ("row", "col"), pairs)


def low_half(shape):
    return lax.broadcasted_iota(jnp.int32, shape, 1) < block_edge


def trade_halves(first, second):
    low = low_half(first.shape)
    turned_first = pltpu.roll(first, block_edge, 1)
    turned_second = pltpu.roll(second, block_edge, 1)
    return jnp.where(low, first, turned_second), jnp.where(low, turned_first, second)


def blocks_to_matrix(blocks, matrix_ref, first_row, heights):
    groups, _, lanes = matrix_ref.shape
    half = heights * groups
    for tile in range(blocks.shape[1] // lanes):
        cut = slice(tile * lanes, (tile + 1) * lanes)
        rows = trade_halves(blocks[:half, cut], blocks[half:, cut])
        for odd in range(2):
            for group in range(groups):
                matrix_ref[group, pl.ds(first_row + 2 * tile + odd, heights, stride=PITCH), :] = (
                    rows[odd][group * heights : (group + 1) * heights]
                )


def matrix_to_blocks(matrix_ref, first_row, tiles, heights):
    groups = matrix_ref.shape[0]
    out = []
    for tile in range(tiles):
        rows = [
            jnp.concatenate(
                [
                    matrix_ref[group, pl.ds(first_row + 2 * tile + odd, heights, stride=PITCH), :]
                    for group in range(groups)
                ],
                axis=0,
            )
            for odd in range(2)
        ]
        out.append(jnp.concatenate(trade_halves(*rows), axis=0))
    return jnp.concatenate(out, axis=1)


PITCH = 72


def block_cuts(rows):
    for block in range(rows // block_edge):
        plain = slice(block * block_edge, (block + 1) * block_edge)
        yield plain, slice(block * PITCH, block * PITCH + block_edge)


def fold(matrix_ref, split_ref):
    groups, _, lanes = split_ref.shape
    for plain, spaced in block_cuts(matrix_ref.shape[0]):
        for group in range(groups):
            part = matrix_ref[plain, group * lanes : (group + 1) * lanes]
            split_ref[group, spaced] = part.astype(F32)


def split_scratch(shape):
    lanes = 2 * block_edge
    return pltpu.VMEM((shape[1] // lanes, shape[0] // block_edge * PITCH, lanes), F32)


AREA = block_edge * block_edge
HALF = AREA // NC
WIDE = 1536
THIN = HALF - WIDE
WIDE_BACK = 1408
HALF_ROWS = HALF // block_edge
CHUNK = 512
CHUNK_ROWS = CHUNK // block_edge
CHUNK_TILES = CHUNK // (2 * block_edge)
CAP = 8
LOCAL = 32
LISTED = 72
VMEM_SPEC = pl.BlockSpec(memory_space=pltpu.VMEM)
SMEM_SPEC = pl.BlockSpec(memory_space=pltpu.SMEM)


def whole_call(kernel, operands, shapes, flops, moved, scalars=0, scratch=()):
    return pl.pallas_call(
        kernel,
        in_specs=[SMEM_SPEC] * scalars + [VMEM_SPEC] * (len(operands) - scalars),
        out_specs=[VMEM_SPEC] * len(shapes),
        out_shape=[jax.ShapeDtypeStruct(shape, dtype) for shape, dtype in shapes],
        scratch_shapes=list(scratch),
        compiler_params=pltpu.CompilerParams(vmem_limit_bytes=40 << 20),
        cost_estimate=pl.CostEstimate(flops=flops, bytes_accessed=moved, transcendentals=0),
    )(*operands)


def split_kernel(core_ref, density_ref, mine_ref, other_ref, wide_ref):
    fold(density_ref, wide_ref)
    heights = density_ref.shape[0] // block_edge
    mine = core_ref[0] * HALF_ROWS
    for ref, first in ((mine_ref, mine), (other_ref, HALF_ROWS - mine)):
        for chunk in range(HALF // CHUNK):
            blocks = matrix_to_blocks(wide_ref, first + chunk * CHUNK_ROWS, CHUNK_TILES, heights)
            ref[:, chunk * CHUNK : (chunk + 1) * CHUNK] = blocks.astype(BF16)


def iota(shape, dim):
    return lax.broadcasted_iota(jnp.int32, shape, dim)


def lane_loop(width, body):
    step = 256
    whole = width // step

    @pl.loop(0, whole)
    def _(k):
        body(pl.ds(pl.multiple_of(k * step, step), step))

    if width % step:
        body(pl.ds(whole * step, width % step))


def select_kernel(*refs):
    pieces, lists_of, find_ref = refs[0:4], refs[4:8], refs[8]
    outs, kept_ref, names_ref, chosen_ref, turned_ref, sem = refs[9:13], *refs[13:18]
    save = pltpu.make_async_copy(turned_ref, kept_ref, sem)
    tasks, span = 64 * CAP, 4 * NC * LOCAL
    lists = 4 * 8

    def target(shape, dim):
        spot = iota(shape, dim)
        block = ((spot & 7) << 2) + ((spot >> 2) & 2) + ((spot >> 4) & 1)
        return (((spot >> 5) << 6) + block).astype(F32)

    def offset(shape, dim):
        return (((iota(shape, dim) >> 3) & 7) << 6).astype(F32)

    @pl.when(pl.program_id(0) == 0)
    def _():
        for step in range(4):
            for k in range(4):
                names_ref[step, 8 * k : 8 * k + 8] = lists_of[step][k].astype(F32)

        @pl.loop(0, 4)
        def _(step):
            rows, at = iota((tasks, lists), 0), iota((tasks, lists), 1)
            want = (((rows >> 4) & 3) << 3) + (((rows >> 3) & 1) << 1)
            row, lane = iota((tasks, 64), 0), iota((tasks, 64), 1)
            keep = lane == ((row >> 6) << 3) + (row & 7)
            ones = jnp.ones((64, span), BF16)
            names = names_ref[step].astype(BF16)
            full = None
            for h in range(2):
                found = jnp.dot(names, find_ref[h], preferred_element_type=F32).astype(BF16)
                pick = (at == want + h).astype(BF16)
                term = jnp.dot(pick, found, preferred_element_type=F32)
                full = term if full is None else full + term
            kept = jnp.where(keep, full, 0.0).astype(BF16)
            value = jnp.dot(kept, ones, preferred_element_type=F32) + offset((tasks, span), 0)
            chosen_ref[step] = (value == target((1, span), 1)).astype(BF16)
            value = lax.dot_general(ones, kept, (((0,), (1,)), ((), ())), preferred_element_type=F32)
            value = value + offset((1, tasks), 1)
            turned_ref[step] = (value == target((span, tasks), 0)).astype(BF16)

    for step in range(4):
        table = jnp.concatenate([pieces[step][k] for k in range(4)], axis=0)
        got = jnp.dot(chosen_ref[step], table, preferred_element_type=F32).astype(BF16)
        for hop in range(4):
            for side in range(NC):
                start = (hop * NC + side) * 64
                outs[hop][side, step * 64 : (step + 1) * 64, :] = got[start : start + 64]

    @pl.when(pl.program_id(0) == 0)
    def _():
        save.start()

    @pl.when(pl.program_id(0) == pl.num_programs(0) - 1)
    def _():
        save.wait()


def select_tasks(pieces, find, width, chunk):
    part = pl.BlockSpec((4, 64, chunk), lambda g: (0, 0, g))
    names = pl.BlockSpec((4, LISTED - 64, CHUNK), lambda g: (0, 64 // (LISTED - 64), 0))
    out = pl.pallas_call(
        select_kernel,
        grid=(width // chunk,),
        in_specs=[part] * 4 + [names] * 4 + [pl.BlockSpec(find.shape, lambda g: (0, 0, 0))],
        out_specs=[pl.BlockSpec((NC, 256, chunk), lambda g: (0, 0, g))] * 4
        + [pl.BlockSpec(memory_space=pltpu.HBM)],
        out_shape=[jax.ShapeDtypeStruct((NC, 256, width), BF16)] * 4
        + [jax.ShapeDtypeStruct((4, 256, 512), BF16)],
        scratch_shapes=[
            pltpu.VMEM((4, 32, CHUNK), F32),
            pltpu.VMEM((4, 512, 256), BF16),
            pltpu.VMEM((4, 256, 512), BF16),
            pltpu.SemaphoreType.DMA,
        ],
        compiler_params=pltpu.CompilerParams(vmem_limit_bytes=40 << 20),
        cost_estimate=pl.CostEstimate(
            flops=2 * 4 * 512 * 256 * width, bytes_accessed=2 * 3200 * width, transcendentals=0
        ),
    )(*pieces, *pieces, find)
    return out[0:4], out[4]


def reduce_kernel(*refs):
    turned_ref, parts, outs = refs[0], refs[1:5], refs[5:9]

    def body(lanes):
        for step in range(4):
            tasks = jnp.concatenate(
                [
                    parts[hop][side, step * 64 : (step + 1) * 64, lanes]
                    for hop in range(4)
                    for side in range(NC)
                ],
                axis=0,
            )
            total = jnp.dot(turned_ref[step], tasks, preferred_element_type=F32)
            outs[step][:, lanes] = total.astype(BF16)

    lane_loop(outs[0].shape[1], body)


def reduce_tasks(turned, parts, width):
    return whole_call(
        reduce_kernel,
        [turned, *parts],
        [((256, width), BF16)] * 4,
        2 * 4 * 512 * 256 * width,
        2 * 3072 * width,
    )


def pair_kernel(first, *refs):
    wide_sel, thin_sel = refs[0], refs[1]
    wide, thin, outs = refs[2:6], refs[6:10], refs[10:12]

    def add(select, parts):
        for side in range(NC):
            tasks = jnp.concatenate([part[side] for part in parts], axis=0)
            total = jnp.dot(select[side], tasks, preferred_element_type=F32)
            outs[side][...] = total.astype(BF16)

    @pl.when(pl.program_id(0) < first)
    def _():
        add(wide_sel, wide)

    @pl.when(pl.program_id(0) >= first)
    def _():
        add(thin_sel, thin)


def pair_sums(wide_sel, thin_sel, wide, thin):
    chunk = 512
    first = WIDE // chunk
    sel = pl.BlockSpec(wide_sel.shape, lambda g: (0, 0, 0))
    wide_spec = pl.BlockSpec((NC, 256, chunk), lambda g: (0, 0, jnp.minimum(g, first - 1)))
    thin_spec = pl.BlockSpec((NC, 256, chunk), lambda g: (0, 0, jnp.maximum(g - first, 0)))
    return pl.pallas_call(
        lambda *refs: pair_kernel(first, *refs),
        grid=(HALF // chunk,),
        in_specs=[sel, sel] + [wide_spec] * 4 + [thin_spec] * 4,
        out_specs=[pl.BlockSpec((256, chunk), lambda g: (0, g))] * 2,
        out_shape=[jax.ShapeDtypeStruct((256, HALF), BF16)] * 2,
        compiler_params=pltpu.CompilerParams(vmem_limit_bytes=40 << 20),
        cost_estimate=pl.CostEstimate(
            flops=4 * 256 * 1024 * HALF, bytes_accessed=12 << 20, transcendentals=0
        ),
    )(wide_sel, thin_sel, *wide, *thin)


def spread_kernel(select_ref, *refs):
    tables, outs = refs[0:2], refs[2:6]

    def body(lanes):
        for hop in range(4):
            for side in range(NC):
                outs[hop][side, :, lanes] = jnp.dot(
                    select_ref[side, hop * 256 : (hop + 1) * 256, :],
                    tables[side][:, lanes],
                    preferred_element_type=F32,
                ).astype(BF16)

    lane_loop(outs[0].shape[2], body)


def grid_kernel(
    core_ref, mine_ref, other_ref, basis_ref, vloc_ref, out_ref, out_other_ref, wide_ref, pair_ref, pot_ref
):
    mine = core_ref[0] * HALF_ROWS
    order, cells = basis_ref.shape
    tile, lanes_of_tile = 256, 2 * block_edge
    for ref, first in ((mine_ref, mine), (other_ref, HALF_ROWS - mine)):

        @pl.loop(0, HALF // CHUNK)
        def _(chunk):
            lanes = pl.ds(pl.multiple_of(chunk * CHUNK, CHUNK), CHUNK)
            sums = ref[:, lanes].astype(F32)
            blocks_to_matrix(sums, wide_ref, first + chunk * CHUNK_ROWS, ATOMS)

    for plain, spaced in block_cuts(order):
        for group in range(wide_ref.shape[0]):
            lanes = slice(group * lanes_of_tile, (group + 1) * lanes_of_tile)
            pair_ref[plain, lanes] = wide_ref[group, spaced].astype(BF16)

    @pl.loop(0, cells // tile)
    def _(step):
        lanes = pl.ds(pl.multiple_of(step * tile, tile), tile)
        vals = basis_ref[:, lanes]
        mixed = jnp.dot(pair_ref[...], vals, preferred_element_type=F32)
        wide = vals.astype(F32)
        rho = jnp.sum(wide * mixed, axis=0, keepdims=True)
        pot = vloc_ref[:, lanes] + 0.5 * rho / jnp.sqrt(1.0 + rho * rho)
        pot_ref[:, lanes] = (wide * pot).astype(BF16)

    @pl.loop(0, order // 256)
    def _(step):
        rows = pl.ds(pl.multiple_of(step * 256, 256), 256)
        part = lax.dot_general(
            pot_ref[...], basis_ref[rows, :], (((1,), (1,)), ((), ())), preferred_element_type=F32
        )
        for plain, spaced in block_cuts(order):
            for half in range(2):
                lanes = slice(half * lanes_of_tile, (half + 1) * lanes_of_tile)
                wide_ref[2 * step + half, spaced] = part[plain, lanes]

    for ref, first in ((out_ref, mine), (out_other_ref, HALF_ROWS - mine)):

        @pl.loop(0, HALF // CHUNK)
        def _(chunk):
            lanes = pl.ds(pl.multiple_of(chunk * CHUNK, CHUNK), CHUNK)
            blocks = matrix_to_blocks(wide_ref, first + chunk * CHUNK_ROWS, CHUNK_TILES, ATOMS)
            ref[:, lanes] = blocks.astype(BF16)


def grid_build(core, mine, other, basis_vals, v_loc):
    order, cells = basis_vals.shape
    return whole_call(
        grid_kernel,
        [core, mine, other, basis_vals, v_loc],
        [(mine.shape, BF16)] * 2,
        4 * order * order * cells,
        2 * order * cells + 8 * order * order,
        scalars=1,
        scratch=[
            split_scratch((order, order)),
            pltpu.VMEM((order, order), BF16),
            pltpu.VMEM((order, cells), BF16),
        ],
    )


def ham_kernel(
    scale, core_ref, mine_ref, other_ref, ham_ref, block_ref, ks_ref, x0_ref, mask_ref, wide_ref
):
    heights = ham_ref.shape[0] // block_edge
    mine = core_ref[0] * HALF_ROWS
    for ref, first in ((mine_ref, mine), (other_ref, HALF_ROWS - mine)):
        for chunk in range(HALF // CHUNK):
            sums = ref[:, chunk * CHUNK : (chunk + 1) * CHUNK]
            blocks_to_matrix(sums, wide_ref, first + chunk * CHUNK_ROWS, heights)
    rows, cols = ham_ref.shape
    down = (iota((rows, rows // block_edge), 0) >> 6 == iota((rows, rows // block_edge), 1)).astype(BF16)
    over = (iota((cols // block_edge, cols), 1) >> 6 == iota((cols // block_edge, cols), 0)).astype(BF16)
    kept = block_ref[...].astype(F32).astype(BF16)
    kept = jnp.dot(down, kept, preferred_element_type=F32).astype(BF16)
    mask_ref[...] = jnp.dot(kept, over, preferred_element_type=F32)
    for plain, spaced in block_cuts(rows):
        for group in range(wide_ref.shape[0]):
            lanes = slice(group * 2 * block_edge, (group + 1) * 2 * block_edge)
            total = ham_ref[plain, lanes] + wide_ref[group, spaced]
            ks_ref[plain, lanes] = total
            x0_ref[plain, lanes] = (mask_ref[plain, lanes] * total * scale).astype(BF16)


def panel_sum(where_ref, left, right_ref):
    total = None
    for outer in range(4):
        for inner in range(4):
            piece = left[outer][inner]
            depth = piece.shape[1]
            start = pl.multiple_of(where_ref[outer * 4 + inner] * depth, depth)
            term = jnp.dot(piece, right_ref[pl.ds(start, depth), :], preferred_element_type=F32)
            total = term if total is None else total + term
    return total


def square_kernel(where_ref, *refs):
    right_ref, mask_ref, out_ref = refs[4:7]
    out_ref[...] = (mask_ref[...] * panel_sum(where_ref, refs[0:4], right_ref)).astype(BF16)


def cube_kernel(scale, where_ref, *refs):
    right_ref, mask_ref, x0_ref, out_ref = refs[4:8]
    x3 = mask_ref[...] * panel_sum(where_ref, refs[0:4], right_ref)
    out_ref[...] = (1.5 * x0_ref[...].astype(F32) - 0.5 * x3) / scale


def panel_call(kernel, where, operands, shape, dtype):
    vmem = pl.BlockSpec(memory_space=pltpu.VMEM)
    rows, cols = shape
    return pl.pallas_call(
        kernel,
        in_specs=[pl.BlockSpec(memory_space=pltpu.SMEM)] + [vmem] * len(operands),
        out_specs=vmem,
        out_shape=jax.ShapeDtypeStruct(shape, dtype),
        compiler_params=pltpu.CompilerParams(vmem_limit_bytes=40 << 20),
        cost_estimate=pl.CostEstimate(
            flops=2 * rows * cols * 4096, bytes_accessed=7 << 20, transcendentals=0
        ),
    )(where, *operands)


def gather_left(x0):
    near = [x0] + [None] * 3
    for d in (1, 3, 2):
        near[d] = move_two(x0, d, "zy")
    near = jnp.stack(near)
    far = [near] + [None] * 3
    for d in (1, 3, 2):
        far[d] = move_two(near, d, "yz")
    return far


def gather_right(tile):
    got = [move_x(tile, d) for d in (1, 3, 2)]
    other = swap_core(tile)
    same = jnp.concatenate([tile, got[0], got[2], got[1]])
    rest = swap_core(same[tile.shape[0]:])
    return jnp.concatenate([same, other, rest])


def body(density, core_ham, block_mask, send_blocks, task_atoms, basis, v_loc):
    block_rows = density.shape[0] // block_edge
    block_cols = density.shape[1] // block_edge
    device_count = send_blocks.shape[1]
    row, col = lax.axis_index("row"), lax.axis_index("col")
    x_at, c_at, y_at, z_at = row // NC, row % NC, col // NZ, col % NZ

    core = c_at.astype(jnp.int32).reshape(1)

    where_wide = [jnp.where(c_at == 0, p, q) for p, q in ((x_at, y_at), (y_at, z_at), (z_at, x_at))]
    where_thin = [z_at, x_at, y_at]

    def device_of(spots, cores, thin):
        one, two, three = [v % 4 for v in spots]
        if thin:
            return place(two, cores, three, one)
        return jnp.where(c_at == 0, place(one, cores, two, three), place(three, cores, one, two))

    slots = send_blocks[0]
    names = slots.reshape(2, CHUNK).astype(BF16)
    names = jnp.concatenate(
        [
            names,
            jnp.zeros((2, WIDE - CHUNK), BF16),
            names,
        ],
        axis=1,
    )
    mine, other = whole_call(
        split_kernel,
        [core, density],
        [((LOCAL, HALF), BF16)] * 2,
        0,
        1 << 20,
        scalars=1,
        scratch=[split_scratch(density.shape)],
    )
    sent = swap_core(jnp.concatenate([other, names, jnp.zeros((6, HALF), BF16)]))
    chip = jnp.concatenate(
        [mine, sent[:LOCAL], names, sent[LOCAL : LOCAL + 2], jnp.zeros((4, HALF), BF16)]
    )

    atoms = task_atoms[:, 0]
    pair = (atoms[1] % 2) * (ATOMS * ATOMS // 2) + (atoms[1] // 2) * ATOMS + atoms[0]
    pair = pair.astype(BF16)
    pair_other = swap_core(pair)

    def spread_out(v, axes):
        out = [v] + [None] * 3
        for d in (1, 3, 2):
            out[d] = move_two(v, d, axes)
        return out

    wide_near = spread_out(chip[:, :WIDE], "zx")
    thin_near = spread_out(chip[:, WIDE:], "yy")
    wide_near, thin_near, pair_other = lax.optimization_barrier((wide_near, thin_near, pair_other))
    wide_pieces = spread_out(jnp.stack(wide_near), "yz")
    thin_pieces = spread_out(jnp.stack(thin_near), "xx")
    wide_pieces, thin_pieces = lax.optimization_barrier((wide_pieces, thin_pieces))

    pairs = jnp.concatenate([pair, pair_other], axis=1)
    pair_ids = jnp.arange(ATOMS * ATOMS, dtype=jnp.int32).astype(F32)

    def plans(spots, thin):
        j = jnp.arange(device_count, dtype=jnp.int32)
        away = (j // 32, (j // 8) % 4, (j // 2) % 4)
        owner = device_of([p - d for p, d in zip(spots, away)], c_at ^ (j % 2), thin)
        order = (owner[:, None] == j[None, :]).astype(BF16)
        moved = jnp.dot(order, pairs, preferred_element_type=F32)
        moved = moved.reshape(device_count, NC, CAP).transpose(1, 0, 2).reshape(NC, -1)
        gather_sel = (pair_ids[None, :, None] == moved[:, None, :]).astype(BF16)
        spread_sel = (moved[:, :, None] == pair_ids[None, None, :]).astype(BF16)
        k = jnp.arange(64, dtype=jnp.int32)
        dest = device_of(
            [spots[0] + k // 16, spots[1] + 0 * k, spots[2] + 0 * k], c_at ^ ((k // 8) % 2), thin
        )
        target = dest * CAP + k % CAP
        line = jnp.arange(2 * CHUNK, dtype=jnp.int32).reshape(2, CHUNK, 1)
        find = (line == target[None, None, :]).astype(BF16)
        return gather_sel, spread_sel, find

    gather_wide, spread_wide, find_wide = plans(where_wide, False)
    gather_thin, spread_thin, find_thin = plans(where_thin, True)

    def exchange(parts, axes, sign):
        out = [parts[0]] + [None] * 3
        for d in (1, 3, 2):
            out[d] = move_two(parts[d], sign * d, axes)
        return out

    wide_tasks, wide_turned = select_tasks(wide_pieces, find_wide, WIDE, 512)
    wide_tasks = exchange(wide_tasks, "xy", 1)
    thin_tasks, thin_turned = select_tasks(thin_pieces, find_thin, THIN, 256)
    thin_tasks = exchange(thin_tasks, "zz", 1)
    sum_mine, sum_other = pair_sums(gather_wide, gather_thin, wide_tasks, thin_tasks)
    k_mine, k_other = grid_build(core, sum_mine, swap_core(sum_other), basis[0], v_loc)
    k_swapped = swap_core(k_other)

    def spread(select, lanes, width):
        return whole_call(
            spread_kernel,
            [select, k_mine[:, lanes], k_swapped[:, lanes]],
            [((NC, 256, width), BF16)] * 4,
            4 * 256 * 1024 * width,
            2 * 2600 * width,
        )

    wide_back = exchange(spread(spread_wide, slice(0, WIDE_BACK), WIDE_BACK), "xy", -1)
    thin_back = exchange(spread(spread_thin, slice(WIDE_BACK, HALF), HALF - WIDE_BACK), "zz", -1)

    def add_up(parts):
        total = parts[0].astype(F32)
        for part in parts[1:]:
            total = total + part.astype(F32)
        return total

    def scatter(parts, near_axes, far_axes):
        near = add_up(exchange(parts, near_axes, -1)).astype(BF16)
        far = [near[64 * d : 64 * (d + 1)] for d in range(4)]
        return add_up(exchange(far, far_axes, -1))

    wide_parts = reduce_tasks(wide_turned, wide_back, WIDE_BACK)
    wide_parts, thin_turned = lax.optimization_barrier((wide_parts, thin_turned))
    wide_ham = scatter(wide_parts, "yz", "zx")
    thin_ham = scatter(reduce_tasks(thin_turned, thin_back, HALF - WIDE_BACK), "xx", "yy")
    ham = jnp.concatenate([wide_ham, thin_ham], axis=1)
    ham_other = swap_core(ham[LOCAL:])
    scale = 1.0 / math.sqrt(16.0 * block_rows * NX * NC)
    ks_matrix, x0, mask = whole_call(
        lambda *refs: ham_kernel(scale, *refs),
        [core, ham[:LOCAL], ham_other, core_ham, block_mask],
        [(density.shape, F32), (density.shape, BF16), (density.shape, F32)],
        0,
        2 << 20,
        scalars=1,
        scratch=[split_scratch(density.shape)],
    )

    left = gather_left(x0)
    shift = jnp.arange(NY * NZ, dtype=jnp.int32)
    outer, inner = shift // NZ, shift % NZ
    dy = jnp.where(c_at == 0, outer, inner)
    dz = jnp.where(c_at == 0, inner, outer)
    src = ((y_at - dy) % NY) * NZ + (z_at - dz) % NZ
    src_x, src_c = src // (2 * NC), (src // 2) % NC
    where = (((src_c ^ c_at) * NX + (x_at - src_x) % NX) * 2 + src % 2).astype(jnp.int32)
    x2 = panel_call(
        square_kernel, where, [*left, gather_right(x0), mask], x0.shape, BF16
    )
    sign_step = panel_call(
        lambda *refs: cube_kernel(scale, *refs),
        where,
        [*left, gather_right(x2), mask, x0],
        x0.shape,
        F32,
    )
    return (ks_matrix, sign_step)


def solution(mesh):
    placed = (
        P("row", "col"),
        P("row", "col"),
        P("row", "col"),
        P(("row", "col"), None, None),
        P(None, ("row", "col"), None, None),
        P(("row", "col"), None, None),
        P(("row", "col"), None),
    )
    return jax.shard_map(
        body,
        mesh=mesh,
        in_specs=placed,
        out_specs=(P("row", "col"), P("row", "col")),
        check_vma=False,
    )
```

```python
import math

import jax
import jax.numpy as jnp
from jax import lax
from jax.experimental import pallas as pl
from jax.experimental.pallas import tpu as pltpu
from jax.sharding import PartitionSpec as P

ATOMS = 16
block_edge = 64
NX, NC, NY, NZ = 4, 2, 4, 4
F32 = jnp.float32
BF16 = jnp.bfloat16


def move_x(v, d):
    pairs = [(x * NC + c, ((x + d) % NX) * NC + c) for x in range(NX) for c in range(NC)]
    return lax.ppermute(v, "row", pairs)


def swap_core(v):
    pairs = [(x * NC + c, x * NC + 1 - c) for x in range(NX) for c in range(NC)]
    return lax.ppermute(v, "row", pairs)


def place(x, c, y, z):
    return ((x % NX) * NC + c) * (NY * NZ) + (y % NY) * NZ + z % NZ


def move_two(v, d, axes):
    pairs = []
    for x in range(NX):
        for c in range(NC):
            for y in range(NY):
                for z in range(NZ):
                    step = {"x": 0, "y": 0, "z": 0}
                    step[axes[c]] = d
                    there = place(x + step["x"], c, y + step["y"], z + step["z"])
                    pairs.append((place(x, c, y, z), there))
    return lax.ppermute(v, ("row", "col"), pairs)


def low_half(shape):
    return lax.broadcasted_iota(jnp.int32, shape, 1) < block_edge


def trade_halves(first, second):
    low = low_half(first.shape)
    turned_first = pltpu.roll(first, block_edge, 1)
    turned_second = pltpu.roll(second, block_edge, 1)
    return jnp.where(low, first, turned_second), jnp.where(low, turned_first, second)


def blocks_to_matrix(blocks, matrix_ref, first_row, heights):
    groups, _, lanes = matrix_ref.shape
    half = heights * groups
    for tile in range(blocks.shape[1] // lanes):
        cut = slice(tile * lanes, (tile + 1) * lanes)
        rows = trade_halves(blocks[:half, cut], blocks[half:, cut])
        for odd in range(2):
            for group in range(groups):
                matrix_ref[group, pl.ds(first_row + 2 * tile + odd, heights, stride=PITCH), :] = (
                    rows[odd][group * heights : (group + 1) * heights]
                )


def matrix_to_blocks(matrix_ref, first_row, tiles, heights):
    groups = matrix_ref.shape[0]
    out = []
    for tile in range(tiles):
        rows = [
            jnp.concatenate(
                [
                    matrix_ref[group, pl.ds(first_row + 2 * tile + odd, heights, stride=PITCH), :]
                    for group in range(groups)
                ],
                axis=0,
            )
            for odd in range(2)
        ]
        out.append(jnp.concatenate(trade_halves(*rows), axis=0))
    return jnp.concatenate(out, axis=1)


PITCH = 72


def block_cuts(rows):
    for block in range(rows // block_edge):
        plain = slice(block * block_edge, (block + 1) * block_edge)
        yield plain, slice(block * PITCH, block * PITCH + block_edge)


def fold(matrix_ref, split_ref):
    groups, _, lanes = split_ref.shape
    for plain, spaced in block_cuts(matrix_ref.shape[0]):
        for group in range(groups):
            part = matrix_ref[plain, group * lanes : (group + 1) * lanes]
            split_ref[group, spaced] = part.astype(F32)


def split_scratch(shape):
    lanes = 2 * block_edge
    return pltpu.VMEM((shape[1] // lanes, shape[0] // block_edge * PITCH, lanes), F32)


AREA = block_edge * block_edge
HALF = AREA // NC
WIDE = 1536
THIN = HALF - WIDE
WIDE_BACK = 1408
HALF_ROWS = HALF // block_edge
CHUNK = 512
CHUNK_ROWS = CHUNK // block_edge
CHUNK_TILES = CHUNK // (2 * block_edge)
CAP = 8
LOCAL = 32
LISTED = 72
VMEM_SPEC = pl.BlockSpec(memory_space=pltpu.VMEM)
SMEM_SPEC = pl.BlockSpec(memory_space=pltpu.SMEM)


def whole_call(kernel, operands, shapes, flops, moved, scalars=0, scratch=()):
    return pl.pallas_call(
        kernel,
        in_specs=[SMEM_SPEC] * scalars + [VMEM_SPEC] * (len(operands) - scalars),
        out_specs=[VMEM_SPEC] * len(shapes),
        out_shape=[jax.ShapeDtypeStruct(shape, dtype) for shape, dtype in shapes],
        scratch_shapes=list(scratch),
        compiler_params=pltpu.CompilerParams(vmem_limit_bytes=24 << 20),
        cost_estimate=pl.CostEstimate(flops=flops, bytes_accessed=moved, transcendentals=0),
    )(*operands)


def split_kernel(core_ref, density_ref, mine_ref, other_ref, wide_ref):
    fold(density_ref, wide_ref)
    heights = density_ref.shape[0] // block_edge
    mine = core_ref[0] * HALF_ROWS
    for ref, first in ((mine_ref, mine), (other_ref, HALF_ROWS - mine)):
        for chunk in range(HALF // CHUNK):
            blocks = matrix_to_blocks(wide_ref, first + chunk * CHUNK_ROWS, CHUNK_TILES, heights)
            ref[:, chunk * CHUNK : (chunk + 1) * CHUNK] = blocks.astype(BF16)


def iota(shape, dim):
    return lax.broadcasted_iota(jnp.int32, shape, dim)


def lane_loop(width, body):
    step = 256
    whole = width // step

    @pl.loop(0, whole)
    def _(k):
        body(pl.ds(pl.multiple_of(k * step, step), step))

    if width % step:
        body(pl.ds(whole * step, width % step))


def select_kernel(*refs):
    pieces, lists_of, find_ref = refs[0:4], refs[4:8], refs[8]
    outs, kept_ref, names_ref, chosen_ref, turned_ref, sem = refs[9:13], *refs[13:18]
    save = pltpu.make_async_copy(turned_ref, kept_ref, sem)
    tasks, span = 64 * CAP, 4 * NC * LOCAL
    lists = 4 * 8

    def target(shape, dim):
        spot = iota(shape, dim)
        block = ((spot & 7) << 2) + ((spot >> 2) & 2) + ((spot >> 4) & 1)
        return (((spot >> 5) << 6) + block).astype(F32)

    def offset(shape, dim):
        return (((iota(shape, dim) >> 3) & 7) << 6).astype(F32)

    @pl.when(pl.program_id(0) == 0)
    def _():
        for step in range(4):
            for k in range(4):
                names_ref[step, 8 * k : 8 * k + 8] = lists_of[step][k].astype(F32)

        @pl.loop(0, 4)
        def _(step):
            rows, at = iota((tasks, lists), 0), iota((tasks, lists), 1)
            want = (((rows >> 4) & 3) << 3) + (((rows >> 3) & 1) << 1)
            row, lane = iota((tasks, 64), 0), iota((tasks, 64), 1)
            keep = lane == ((row >> 6) << 3) + (row & 7)
            ones = jnp.ones((64, span), BF16)
            names = names_ref[step].astype(BF16)
            full = None
            for h in range(2):
                found = jnp.dot(names, find_ref[h], preferred_element_type=F32).astype(BF16)
                pick = (at == want + h).astype(BF16)
                term = jnp.dot(pick, found, preferred_element_type=F32)
                full = term if full is None else full + term
            kept = jnp.where(keep, full, 0.0).astype(BF16)
            value = jnp.dot(kept, ones, preferred_element_type=F32) + offset((tasks, span), 0)
            chosen_ref[step] = (value == target((1, span), 1)).astype(BF16)
            value = lax.dot_general(ones, kept, (((0,), (1,)), ((), ())), preferred_element_type=F32)
            value = value + offset((1, tasks), 1)
            turned_ref[step] = (value == target((span, tasks), 0)).astype(BF16)

    for step in range(4):
        table = jnp.concatenate([pieces[step][k] for k in range(4)], axis=0)
        got = jnp.dot(chosen_ref[step], table, preferred_element_type=F32).astype(BF16)
        for hop in range(4):
            for side in range(NC):
                start = (hop * NC + side) * 64
                outs[hop][side, step * 64 : (step + 1) * 64, :] = got[start : start + 64]

    @pl.when(pl.program_id(0) == 0)
    def _():
        save.start()

    @pl.when(pl.program_id(0) == pl.num_programs(0) - 1)
    def _():
        save.wait()


def select_tasks(pieces, find, width, chunk):
    part = pl.BlockSpec((4, 64, chunk), lambda g: (0, 0, g))
    names = pl.BlockSpec((4, LISTED - 64, CHUNK), lambda g: (0, 64 // (LISTED - 64), 0))
    out = pl.pallas_call(
        select_kernel,
        grid=(width // chunk,),
        in_specs=[part] * 4 + [names] * 4 + [pl.BlockSpec(find.shape, lambda g: (0, 0, 0))],
        out_specs=[pl.BlockSpec((NC, 256, chunk), lambda g: (0, 0, g))] * 4
        + [pl.BlockSpec(memory_space=pltpu.HBM)],
        out_shape=[jax.ShapeDtypeStruct((NC, 256, width), BF16)] * 4
        + [jax.ShapeDtypeStruct((4, 256, 512), BF16)],
        scratch_shapes=[
            pltpu.VMEM((4, 32, CHUNK), F32),
            pltpu.VMEM((4, 512, 256), BF16),
            pltpu.VMEM((4, 256, 512), BF16),
            pltpu.SemaphoreType.DMA,
        ],
        compiler_params=pltpu.CompilerParams(vmem_limit_bytes=16 << 20),
        cost_estimate=pl.CostEstimate(
            flops=2 * 4 * 512 * 256 * width, bytes_accessed=2 * 3200 * width, transcendentals=0
        ),
    )(*pieces, *pieces, find)
    return out[0:4], out[4]


def reduce_kernel(*refs):
    turned_ref, parts, outs = refs[0], refs[1:5], refs[5:9]

    def body(lanes):
        for step in range(4):
            tasks = jnp.concatenate(
                [
                    parts[hop][side, step * 64 : (step + 1) * 64, lanes]
                    for hop in range(4)
                    for side in range(NC)
                ],
                axis=0,
            )
            total = jnp.dot(turned_ref[step], tasks, preferred_element_type=F32)
            outs[step][:, lanes] = total.astype(BF16)

    lane_loop(outs[0].shape[1], body)


def reduce_tasks(turned, parts, width):
    return whole_call(
        reduce_kernel,
        [turned, *parts],
        [((256, width), BF16)] * 4,
        2 * 4 * 512 * 256 * width,
        2 * 3072 * width,
    )


def pair_kernel(first, *refs):
    wide_sel, thin_sel = refs[0], refs[1]
    wide, thin, outs = refs[2:6], refs[6:10], refs[10:12]

    def add(select, parts):
        for side in range(NC):
            tasks = jnp.concatenate([part[side] for part in parts], axis=0)
            total = jnp.dot(select[side], tasks, preferred_element_type=F32)
            outs[side][...] = total.astype(BF16)

    @pl.when(pl.program_id(0) < first)
    def _():
        add(wide_sel, wide)

    @pl.when(pl.program_id(0) >= first)
    def _():
        add(thin_sel, thin)


def pair_sums(wide_sel, thin_sel, wide, thin):
    chunk = 512
    first = WIDE // chunk
    sel = pl.BlockSpec(wide_sel.shape, lambda g: (0, 0, 0))
    wide_spec = pl.BlockSpec((NC, 256, chunk), lambda g: (0, 0, jnp.minimum(g, first - 1)))
    thin_spec = pl.BlockSpec((NC, 256, chunk), lambda g: (0, 0, jnp.maximum(g - first, 0)))
    return pl.pallas_call(
        lambda *refs: pair_kernel(first, *refs),
        grid=(HALF // chunk,),
        in_specs=[sel, sel] + [wide_spec] * 4 + [thin_spec] * 4,
        out_specs=[pl.BlockSpec((256, chunk), lambda g: (0, g))] * 2,
        out_shape=[jax.ShapeDtypeStruct((256, HALF), BF16)] * 2,
        compiler_params=pltpu.CompilerParams(vmem_limit_bytes=20 << 20),
        cost_estimate=pl.CostEstimate(
            flops=4 * 256 * 1024 * HALF, bytes_accessed=12 << 20, transcendentals=0
        ),
    )(wide_sel, thin_sel, *wide, *thin)


def spread_kernel(select_ref, *refs):
    tables, outs = refs[0:2], refs[2:6]

    def body(lanes):
        for hop in range(4):
            for side in range(NC):
                outs[hop][side, :, lanes] = jnp.dot(
                    select_ref[side, hop * 256 : (hop + 1) * 256, :],
                    tables[side][:, lanes],
                    preferred_element_type=F32,
                ).astype(BF16)

    lane_loop(outs[0].shape[2], body)


def grid_kernel(
    core_ref, mine_ref, other_ref, basis_ref, vloc_ref, out_ref, out_other_ref, wide_ref, pair_ref, pot_ref
):
    mine = core_ref[0] * HALF_ROWS
    order, cells = basis_ref.shape
    tile, lanes_of_tile = 256, 2 * block_edge
    for ref, first in ((mine_ref, mine), (other_ref, HALF_ROWS - mine)):

        @pl.loop(0, HALF // CHUNK)
        def _(chunk):
            lanes = pl.ds(pl.multiple_of(chunk * CHUNK, CHUNK), CHUNK)
            sums = ref[:, lanes].astype(F32)
            blocks_to_matrix(sums, wide_ref, first + chunk * CHUNK_ROWS, ATOMS)

    for plain, spaced in block_cuts(order):
        for group in range(wide_ref.shape[0]):
            lanes = slice(group * lanes_of_tile, (group + 1) * lanes_of_tile)
            pair_ref[plain, lanes] = wide_ref[group, spaced].astype(BF16)

    @pl.loop(0, cells // tile)
    def _(step):
        lanes = pl.ds(pl.multiple_of(step * tile, tile), tile)
        vals = basis_ref[:, lanes]
        mixed = jnp.dot(pair_ref[...], vals, preferred_element_type=F32)
        wide = vals.astype(F32)
        rho = jnp.sum(wide * mixed, axis=0, keepdims=True)
        pot = vloc_ref[:, lanes] + 0.5 * rho / jnp.sqrt(1.0 + rho * rho)
        pot_ref[:, lanes] = (wide * pot).astype(BF16)

    @pl.loop(0, order // 256)
    def _(step):
        rows = pl.ds(pl.multiple_of(step * 256, 256), 256)
        part = lax.dot_general(
            pot_ref[...], basis_ref[rows, :], (((1,), (1,)), ((), ())), preferred_element_type=F32
        )
        for plain, spaced in block_cuts(order):
            for half in range(2):
                lanes = slice(half * lanes_of_tile, (half + 1) * lanes_of_tile)
                wide_ref[2 * step + half, spaced] = part[plain, lanes]

    for ref, first in ((out_ref, mine), (out_other_ref, HALF_ROWS - mine)):

        @pl.loop(0, HALF // CHUNK)
        def _(chunk):
            lanes = pl.ds(pl.multiple_of(chunk * CHUNK, CHUNK), CHUNK)
            blocks = matrix_to_blocks(wide_ref, first + chunk * CHUNK_ROWS, CHUNK_TILES, ATOMS)
            ref[:, lanes] = blocks.astype(BF16)


def grid_build(core, mine, other, basis_vals, v_loc):
    order, cells = basis_vals.shape
    return whole_call(
        grid_kernel,
        [core, mine, other, basis_vals, v_loc],
        [(mine.shape, BF16)] * 2,
        4 * order * order * cells,
        2 * order * cells + 8 * order * order,
        scalars=1,
        scratch=[
            split_scratch((order, order)),
            pltpu.VMEM((order, order), BF16),
            pltpu.VMEM((order, cells), BF16),
        ],
    )


def ham_kernel(
    scale, core_ref, mine_ref, other_ref, ham_ref, block_ref, ks_ref, x0_ref, mask_ref, wide_ref
):
    heights = ham_ref.shape[0] // block_edge
    mine = core_ref[0] * HALF_ROWS
    for ref, first in ((mine_ref, mine), (other_ref, HALF_ROWS - mine)):
        for chunk in range(HALF // CHUNK):
            sums = ref[:, chunk * CHUNK : (chunk + 1) * CHUNK]
            blocks_to_matrix(sums, wide_ref, first + chunk * CHUNK_ROWS, heights)
    rows, cols = ham_ref.shape
    down = (iota((rows, rows // block_edge), 0) >> 6 == iota((rows, rows // block_edge), 1)).astype(BF16)
    over = (iota((cols // block_edge, cols), 1) >> 6 == iota((cols // block_edge, cols), 0)).astype(BF16)
    kept = block_ref[...].astype(F32).astype(BF16)
    kept = jnp.dot(down, kept, preferred_element_type=F32).astype(BF16)
    mask_ref[...] = jnp.dot(kept, over, preferred_element_type=F32)
    for plain, spaced in block_cuts(rows):
        for group in range(wide_ref.shape[0]):
            lanes = slice(group * 2 * block_edge, (group + 1) * 2 * block_edge)
            total = ham_ref[plain, lanes] + wide_ref[group, spaced]
            ks_ref[plain, lanes] = total
            x0_ref[plain, lanes] = (mask_ref[plain, lanes] * total * scale).astype(BF16)


def panel_sum(where_ref, left, right_ref):
    own, rest = left[0:4], left[4:8]
    total = None
    for outer in range(4):
        for inner in range(4):
            piece = rest[outer][inner - 1] if inner else own[outer][...]
            depth = piece.shape[1]
            start = pl.multiple_of(where_ref[outer * 4 + inner] * depth, depth)
            term = jnp.dot(piece, right_ref[pl.ds(start, depth), :], preferred_element_type=F32)
            total = term if total is None else total + term
    return total


def square_kernel(where_ref, *refs):
    right_ref, mask_ref, out_ref = refs[8:11]
    out_ref[...] = (mask_ref[...] * panel_sum(where_ref, refs[0:8], right_ref)).astype(BF16)


def cube_kernel(scale, where_ref, *refs):
    right_ref, mask_ref, x0_ref, out_ref = refs[8:12]
    x3 = mask_ref[...] * panel_sum(where_ref, refs[0:8], right_ref)
    out_ref[...] = (1.5 * x0_ref[...].astype(F32) - 0.5 * x3) / scale


def panel_call(kernel, where, operands, shape, dtype):
    vmem = pl.BlockSpec(memory_space=pltpu.VMEM)
    rows, cols = shape
    return pl.pallas_call(
        kernel,
        in_specs=[pl.BlockSpec(memory_space=pltpu.SMEM)] + [vmem] * len(operands),
        out_specs=vmem,
        out_shape=jax.ShapeDtypeStruct(shape, dtype),
        compiler_params=pltpu.CompilerParams(vmem_limit_bytes=16 << 20),
        cost_estimate=pl.CostEstimate(
            flops=2 * rows * cols * 4096, bytes_accessed=7 << 20, transcendentals=0
        ),
    )(where, *operands)


def gather_left(x0):
    near, own = [None] * 4, [x0] + [None] * 3
    for d in (1, 3, 2):
        near[d] = move_two(x0, d, "zy")
    for d in (1, 3, 2):
        own[d] = move_two(x0, d, "yz")
    held = jnp.stack(near[1:])
    rest = [held] + [None] * 3
    for d in (1, 3, 2):
        rest[d] = move_two(held, d, "yz")
    return [*own, *rest]


def gather_right(tile):
    got = [move_x(tile, d) for d in (1, 3, 2)]
    other = swap_core(tile)
    same = jnp.concatenate([tile, got[0], got[2], got[1]])
    rest = swap_core(same[tile.shape[0]:])
    return jnp.concatenate([same, other, rest])


def body(density, core_ham, block_mask, send_blocks, task_atoms, basis, v_loc):
    block_rows = density.shape[0] // block_edge
    device_count = send_blocks.shape[1]
    row, col = lax.axis_index("row"), lax.axis_index("col")
    x_at, c_at, y_at, z_at = row // NC, row % NC, col // NZ, col % NZ

    core = c_at.astype(jnp.int32).reshape(1)

    where_wide = [jnp.where(c_at == 0, p, q) for p, q in ((x_at, y_at), (y_at, z_at), (z_at, x_at))]
    where_thin = [z_at, x_at, y_at]

    def device_of(spots, cores, thin):
        one, two, three = [v % 4 for v in spots]
        if thin:
            return place(two, cores, three, one)
        return jnp.where(c_at == 0, place(one, cores, two, three), place(three, cores, one, two))

    slots = send_blocks[0]
    names = slots.reshape(2, CHUNK).astype(BF16)
    names = jnp.concatenate(
        [
            names,
            jnp.zeros((2, WIDE - CHUNK), BF16),
            names,
        ],
        axis=1,
    )
    mine, other = whole_call(
        split_kernel,
        [core, density],
        [((LOCAL, HALF), BF16)] * 2,
        0,
        1 << 20,
        scalars=1,
        scratch=[split_scratch(density.shape)],
    )
    sent = swap_core(jnp.concatenate([other, names, jnp.zeros((6, HALF), BF16)]))
    chip = jnp.concatenate(
        [mine, sent[:LOCAL], names, sent[LOCAL : LOCAL + 2], jnp.zeros((4, HALF), BF16)]
    )

    atoms = task_atoms[:, 0]
    pair = (atoms[1] % 2) * (ATOMS * ATOMS // 2) + (atoms[1] // 2) * ATOMS + atoms[0]
    pair = pair.astype(BF16)
    pair_other = swap_core(pair)

    def spread_out(v, axes):
        out = [v] + [None] * 3
        for d in (1, 3, 2):
            out[d] = move_two(v, d, axes)
        return out

    wide_near = spread_out(chip[:, :WIDE], "zx")
    thin_near = spread_out(chip[:, WIDE:], "yy")
    wide_near, thin_near, pair_other = lax.optimization_barrier((wide_near, thin_near, pair_other))
    wide_pieces = spread_out(jnp.stack(wide_near), "yz")
    thin_pieces = spread_out(jnp.stack(thin_near), "xx")
    wide_pieces, thin_pieces = lax.optimization_barrier((wide_pieces, thin_pieces))

    pairs = jnp.concatenate([pair, pair_other], axis=1)
    pair_ids = jnp.arange(ATOMS * ATOMS, dtype=jnp.int32).astype(F32)

    def plans(spots, thin):
        j = jnp.arange(device_count, dtype=jnp.int32)
        away = (j // 32, (j // 8) % 4, (j // 2) % 4)
        owner = device_of([p - d for p, d in zip(spots, away)], c_at ^ (j % 2), thin)
        order = (owner[:, None] == j[None, :]).astype(BF16)
        moved = jnp.dot(order, pairs, preferred_element_type=F32)
        moved = moved.reshape(device_count, NC, CAP).transpose(1, 0, 2).reshape(NC, -1)
        gather_sel = (pair_ids[None, :, None] == moved[:, None, :]).astype(BF16)
        spread_sel = (moved[:, :, None] == pair_ids[None, None, :]).astype(BF16)
        k = jnp.arange(64, dtype=jnp.int32)
        dest = device_of(
            [spots[0] + k // 16, spots[1] + 0 * k, spots[2] + 0 * k], c_at ^ ((k // 8) % 2), thin
        )
        target = dest * CAP + k % CAP
        line = jnp.arange(2 * CHUNK, dtype=jnp.int32).reshape(2, CHUNK, 1)
        find = (line == target[None, None, :]).astype(BF16)
        return gather_sel, spread_sel, find

    gather_wide, spread_wide, find_wide = plans(where_wide, False)
    gather_thin, spread_thin, find_thin = plans(where_thin, True)

    def exchange(parts, axes, sign):
        out = [parts[0]] + [None] * 3
        for d in (1, 3, 2):
            out[d] = move_two(parts[d], sign * d, axes)
        return out

    wide_tasks, wide_turned = select_tasks(wide_pieces, find_wide, WIDE, 512)
    wide_tasks = exchange(wide_tasks, "xy", 1)
    thin_tasks, thin_turned = select_tasks(thin_pieces, find_thin, THIN, 256)
    thin_tasks = exchange(thin_tasks, "zz", 1)
    sum_mine, sum_other = pair_sums(gather_wide, gather_thin, wide_tasks, thin_tasks)
    k_mine, k_other = grid_build(core, sum_mine, swap_core(sum_other), basis[0], v_loc)
    k_swapped = swap_core(k_other)

    def spread(select, lanes, width):
        return whole_call(
            spread_kernel,
            [select, k_mine[:, lanes], k_swapped[:, lanes]],
            [((NC, 256, width), BF16)] * 4,
            4 * 256 * 1024 * width,
            2 * 2600 * width,
        )

    wide_back = exchange(spread(spread_wide, slice(0, WIDE_BACK), WIDE_BACK), "xy", -1)
    thin_back = exchange(spread(spread_thin, slice(WIDE_BACK, HALF), HALF - WIDE_BACK), "zz", -1)

    def add_up(parts):
        total = parts[0].astype(F32)
        for part in parts[1:]:
            total = total + part.astype(F32)
        return total

    def scatter(parts, near_axes, far_axes):
        parts = exchange(parts, near_axes, -1)
        near = add_up(parts).astype(BF16)
        far = [near[64 * d : 64 * (d + 1)] for d in range(4)]
        return add_up(exchange(far, far_axes, -1))

    wide_parts = reduce_tasks(wide_turned, wide_back, WIDE_BACK)
    wide_parts, thin_turned = lax.optimization_barrier((wide_parts, thin_turned))
    wide_ham = scatter(wide_parts, "yz", "zx")
    thin_ham = scatter(reduce_tasks(thin_turned, thin_back, HALF - WIDE_BACK), "xx", "yy")
    ham = jnp.concatenate([wide_ham, thin_ham], axis=1)
    ham_other = swap_core(ham[LOCAL:])
    scale = 1.0 / math.sqrt(16.0 * block_rows * NX * NC)
    ks_matrix, x0, mask = whole_call(
        lambda *refs: ham_kernel(scale, *refs),
        [core, ham[:LOCAL], ham_other, core_ham, block_mask],
        [(density.shape, F32), (density.shape, BF16), (density.shape, F32)],
        0,
        2 << 20,
        scalars=1,
        scratch=[split_scratch(density.shape)],
    )

    left = gather_left(x0)
    right = gather_right(x0)
    shift = jnp.arange(NY * NZ, dtype=jnp.int32)
    outer, inner = shift // NZ, shift % NZ
    dy = jnp.where(c_at == 0, outer, inner)
    dz = jnp.where(c_at == 0, inner, outer)
    src = ((y_at - dy) % NY) * NZ + (z_at - dz) % NZ
    src_x, src_c = src // (2 * NC), (src // 2) % NC
    where = (((src_c ^ c_at) * NX + (x_at - src_x) % NX) * 2 + src % 2).astype(jnp.int32)
    x2 = panel_call(
        square_kernel, where, [*left, right, mask], x0.shape, BF16
    )
    sign_step = panel_call(
        lambda *refs: cube_kernel(scale, *refs),
        where,
        [*left, gather_right(x2), mask, x0],
        x0.shape,
        F32,
    )
    return (ks_matrix, sign_step)


def solution(mesh):
    placed = (
        P("row", "col"),
        P("row", "col"),
        P("row", "col"),
        P(("row", "col"), None, None),
        P(None, ("row", "col"), None, None),
        P(("row", "col"), None, None),
        P(("row", "col"), None),
    )
    return jax.shard_map(
        body,
        mesh=mesh,
        in_specs=placed,
        out_specs=(P("row", "col"), P("row", "col")),
        check_vma=False,
    )
```
